1024 devices in a mesh: row: 64 (over y, z_hi, core), col: 16 (over x, z_lo).
Axes of the slice: x: 4, y: 8, z: 16 (z_hi: 4, z_lo: 4; z = z_hi * 4 + z_lo), core: 2. Of those that a mesh axis runs over, the one named last changes fastest.
Arguments:
- flow: float32 [2, 8, 512, 4096], P(None, None, 'row', 'col'), may hold values from -4 to 4
- temp: float32 [8, 512, 4096], P(None, 'row', 'col'), may hold values from -4 to 4
- tracers: float32 [64, 16, 8, 16, 2048], P('row', None, None, None, 'col'), may hold values from -4 to 4
- bottom: int32 [512, 4096], P('row', 'col'), may hold values from 0 to 8
- sunlight: float32 [512, 4096], P('row', 'col'), may hold values from 0.5 to 2
- rates: float32 [16, 16], replicated, may hold values from -2 to 2
Outputs:
- flow_out: float32 [2, 8, 512, 4096], P(None, None, 'row', 'col')
- temp_out: float32 [8, 512, 4096], P(None, 'row', 'col')
- tracers_out: float32 [64, 16, 8, 16, 2048], P('row', None, None, None, 'col')
The draws below stay inside these ranges and needn't reach their ends.
Inputs may be any that keep to these rules, and one draw needn't show every extreme that they name: Columns are water at levels 0 to bottom - 1; 0 marks land.
All inputs are finite; a program needn't handle non-finite values.
Results may differ from the reference program's by a relative error of at most 0.0001.
Values sent between devices are 32-bit elements; how exact they have to be, the bound alone decides.
A program may use at most 32 MiB of HBM per device.

```python
import math
import jax
import jax.numpy as jnp
from jax import lax

NTR = 16
NZ = 8
KL = 4
STEPS = 2
LAT_DEV = 8
LON_DEV = 256
NLAT = 512
NLON = 4096
N_ROW = 64
N_COL = 16


def touch_ends(result, rng, least, high):
    longest = result.shape.index(max(result.shape))
    spots = []
    for shift in (0, 1):
        where = [jax.random.randint(jax.random.fold_in(rng, axis), (), 0, length) for axis, length in enumerate(result.shape)]
        where[longest] = (where[longest] + shift) % result.shape[longest]
        spots.append(tuple(where))
    return result.at[spots[0]].set(least).at[spots[1]].set(high)


def level_of(rng, extent, split, smallest, high):
    def one(axis_at, blocks):
        heights = jax.random.uniform(jax.random.fold_in(jax.random.fold_in(rng, 6), axis_at), (blocks,), jnp.float32, smallest / len(split), high / len(split))
        return jnp.repeat(jnp.exp(heights), extent[axis_at] // blocks).reshape((-1,) + (1,) * (len(extent) - axis_at - 1))

    gain = one(*split[0])
    for cut in split[1:]:
        gain = gain * one(*cut)
    return gain


def noise(own_key, dims, deviation, limit, pieces=(), kind=jnp.bfloat16):
    loudness = level_of(own_key, dims, pieces, -0.22, 0.18) if pieces else 1.0
    array = jax.random.normal(own_key, dims, jnp.float32) * deviation * loudness
    return jnp.minimum(jnp.maximum(array, -limit), limit).astype(kind)


def setup_inputs(seed: int = 0) -> dict:
    splits = jax.random.split(jax.random.key(seed), 7)
    flow = noise(splits[0], (2, NZ, NLAT, NLON), 1.0, 4.0, ((2, 64), (3, 16)), jnp.float32)
    temp = noise(splits[1], (NZ, NLAT, NLON), 1.0, 4.0, ((1, 64), (2, 16)), jnp.float32)
    tracers = noise(splits[2], (N_ROW, NTR, NZ, 2 * LAT_DEV, NLON // 2), 1.0, 4.0, ((0, 64), (4, 16)), jnp.float32)
    bottom = touch_ends(jax.random.randint(splits[3], (NLAT, NLON), 0, NZ + 1), jax.random.fold_in(splits[3], 1), 0, NZ).astype(jnp.int32)
    sunlight = jnp.clip(jnp.exp(math.log(2.0) - 1.3862944 * jax.random.uniform(splits[4], (NLAT, NLON), jnp.float32) ** level_of(splits[4], (NLAT, NLON), ((0, 64), (1, 16)), -0.2, 0.2)), 0.5, 2.0)
    rates = noise(splits[5], (NTR, NTR), 0.5, 2.0, (), jnp.float32)
    return dict(flow=flow, temp=temp, tracers=tracers, bottom=bottom, sunlight=sunlight, rates=rates)


time_step = 0.2
viscosity = 0.2
expansion = 0.05
coriolis_base = 0.5
kappa_base = 0.05
kappa_shear = 0.2
react_step = 0.25
water_absorb = 0.1
pigment_absorb = 0.6
heat_gain = 1.0

def pad_edges(field):
    widths = [(0, 0)] * (field.ndim - 2) + [(1, 1), (1, 1)]
    return jnp.pad(field, widths)

def neighbour_sides(padded):
    middle = padded[..., 1:-1, 1:-1]
    return (middle, padded[..., 1:-1, 2:], padded[..., 1:-1, :-2], padded[..., 2:, 1:-1], padded[..., :-2, 1:-1])

def shear_kappa(flow_u, flow_v):
    below_u = jnp.concatenate([flow_u[1:], flow_u[-1:]], axis=0)
    below_v = jnp.concatenate([flow_v[1:], flow_v[-1:]], axis=0)
    shear_sq = (flow_u - below_u) ** 2 + (flow_v - below_v) ** 2
    return kappa_base + kappa_shear * shear_sq / (1.0 + shear_sq)

def make_faces(padded):
    kappa_pad = shear_kappa(padded[0], padded[1])
    u_mid, u_east, u_west, u_north, u_south = neighbour_sides(padded[0])
    v_mid, v_east, v_west, v_north, v_south = neighbour_sides(padded[1])
    m_mid, m_east, m_west, m_north, m_south = neighbour_sides(padded[3])
    k_mid, k_east, k_west, k_north, k_south = neighbour_sides(kappa_pad)
    open_e = m_mid * m_east
    open_w = m_mid * m_west
    open_n = m_mid * m_north
    open_s = m_mid * m_south
    return jnp.stack([0.5 * (u_mid + u_east) * open_e, 0.5 * (u_mid + u_west) * open_w, 0.5 * (v_mid + v_north) * open_n, 0.5 * (v_mid + v_south) * open_s, 0.5 * (k_mid + k_east) * open_e, 0.5 * (k_mid + k_west) * open_w, 0.5 * (k_mid + k_north) * open_n, 0.5 * (k_mid + k_south) * open_s, m_mid])

def transport(face_terms, padded):
    east_flux, west_flux, north_flux, south_flux = (face_terms[0], face_terms[1], face_terms[2], face_terms[3])
    east_cond, west_cond, north_cond, south_cond = (face_terms[4], face_terms[5], face_terms[6], face_terms[7])
    wet_mask = face_terms[8]
    middle, eastward, westward, northward, southward = neighbour_sides(padded)
    divergence = east_flux - west_flux + north_flux - south_flux
    upward = -lax.cumsum(divergence, axis=0, reverse=True)
    zero_top = jnp.zeros_like(upward[:1])
    w_bottom = jnp.concatenate([upward[1:], zero_top], axis=0)
    w_top = jnp.concatenate([zero_top, upward[1:]], axis=0)
    above_val = jnp.concatenate([middle[..., :1, :, :], middle[..., :-1, :, :]], axis=-3)
    below_val = jnp.concatenate([middle[..., 1:, :, :], middle[..., -1:, :, :]], axis=-3)
    advection = east_flux * 0.5 * (middle + eastward) - west_flux * 0.5 * (middle + westward) + north_flux * 0.5 * (middle + northward) - south_flux * 0.5 * (middle + southward) + w_top * 0.5 * (middle + above_val) - w_bottom * 0.5 * (middle + below_val)
    diffusion = east_cond * (eastward - middle) + west_cond * (westward - middle) + north_cond * (northward - middle) + south_cond * (southward - middle)
    return wet_mask * (middle + time_step * (diffusion - advection))

def momentum(padded, coriolis):
    pressure = -expansion * jnp.cumsum(padded[2], axis=0)
    p_mid, p_east, p_west, p_north, p_south = neighbour_sides(pressure)
    u_mid, u_east, u_west, u_north, u_south = neighbour_sides(padded[0])
    v_mid, v_east, v_west, v_north, v_south = neighbour_sides(padded[1])
    m_mid, m_east, m_west, m_north, m_south = neighbour_sides(padded[3])
    lap_u = m_mid * (m_east * (u_east - u_mid) + m_west * (u_west - u_mid) + m_north * (u_north - u_mid) + m_south * (u_south - u_mid))
    lap_v = m_mid * (m_east * (v_east - v_mid) + m_west * (v_west - v_mid) + m_north * (v_north - v_mid) + m_south * (v_south - v_mid))
    new_u = m_mid * (u_mid + time_step * (coriolis * v_mid - 0.5 * (p_east - p_west) + viscosity * lap_u))
    new_v = m_mid * (v_mid + time_step * (-coriolis * u_mid - 0.5 * (p_north - p_south) + viscosity * lap_v))
    return (new_u, new_v)

def absorption(pigment_top):
    squared = pigment_top * pigment_top
    transmit = jnp.exp(-(water_absorb + pigment_absorb * squared / (1.0 + squared)))
    above_light = jnp.cumprod(jnp.concatenate([jnp.ones_like(transmit[:1]), transmit[:-1]], axis=0), axis=0)
    return above_light * (1.0 - transmit)

def reaction(moved_field, rates, wet_mask):
    saturated = moved_field / jnp.sqrt(1.0 + moved_field * moved_field)

    def one_tracer(row_rates):
        return jnp.tensordot(row_rates, saturated, axes=1, precision=lax.Precision.HIGHEST)
    coupling = lax.map(one_tracer, rates)
    return moved_field + react_step * wet_mask * coupling

def blocks_to_grid(blocks):
    shaped = blocks.reshape(N_ROW // 2, 2, NTR, NZ, 2 * LAT_DEV, N_COL, LON_DEV // 2)
    shaped = jnp.transpose(shaped, (2, 3, 0, 4, 5, 1, 6))
    return shaped.reshape(NTR, NZ, NLAT, NLON)

def grid_to_blocks(field):
    shaped = field.reshape(NTR, NZ, N_ROW // 2, 2 * LAT_DEV, N_COL, 2, LON_DEV // 2)
    shaped = jnp.transpose(shaped, (2, 5, 0, 1, 3, 4, 6))
    return shaped.reshape(N_ROW, NTR, NZ, 2 * LAT_DEV, NLON // 2)

def reference(flow, temp, tracers, bottom, sunlight, rates):
    levels = jnp.arange(NZ, dtype=jnp.int32)[:, None, None]
    wet_mask = (levels < bottom[None]).astype(jnp.float32)
    latitude = jnp.arange(NLAT, dtype=jnp.int32).astype(jnp.float32)
    coriolis = (coriolis_base * (2.0 * (latitude + 0.5) / NLAT - 1.0))[:, None]
    flow_u = flow[0] * wet_mask
    flow_v = flow[1] * wet_mask
    heat_field = temp * wet_mask
    tracer_field = blocks_to_grid(tracers) * wet_mask
    for step_index in range(STEPS):
        padded = pad_edges(jnp.stack([flow_u, flow_v, heat_field, wet_mask]))
        face_terms = make_faces(padded)
        flow_u, flow_v = momentum(padded, coriolis)
        heat_field = transport(face_terms, padded[2])
        moved_field = lax.map(lambda single: transport(face_terms, pad_edges(single)), tracer_field)
        tracer_field = reaction(moved_field, rates, wet_mask)
        profile = absorption(tracer_field[0, :KL])
        heat_field = heat_field.at[:KL].add(heat_gain * sunlight * wet_mask[:KL] * profile)
    return (jnp.stack([flow_u, flow_v]), heat_field, grid_to_blocks(tracer_field))
```

```python
import functools

import jax
import jax.numpy as jnp
from jax import lax
from jax.experimental import pallas as pl
from jax.experimental.pallas import tpu as pltpu
from jax.sharding import PartitionSpec as P

MESH = pl.DeviceIdType.MESH
NT = 16
NZ = 8
KL = 4

time_step = 0.2
viscosity = 0.2
expansion = 0.05
coriolis_base = 0.5
kappa_base = 0.05
kappa_shear = 0.2
react_step = 0.25
water_absorb = 0.1
pigment_absorb = 0.6
heat_gain = 1.0


def kernel(
    n_row, n_col,
    flow, temp, tr, bot, sun, rates,
    flow_out, temp_out, tr_out,
    c0, c1, c2, p0, p1, psat, fm0, fp0, fm1, fp1, kpm, kpp, am, ap, ap_flow, wmat,
    xo, xw, xe, xc, pf, pt, pb, ps, fo, fr,
    send, recv,
):
    row = lax.axis_index("row")
    col = lax.axis_index("col")
    half = lax.rem(row, 2)
    chip = row // 2
    other = 2 * chip + 1 - half
    west_col = col - 1 + half
    east_col = col + half
    has_w = west_col >= 0
    has_e = east_col < n_col
    has_n = row + 2 < n_row
    has_s = row >= 2
    partner = (other, col)
    west = (other, west_col)
    east = (other, east_col)
    north = (row + 2, col)
    south = (row - 2, col)
    targets = (
        (has_n, north), (has_s, south), (has_e, east), (has_w, west),
        (has_n & has_e, (other + 2, east_col)), (has_n & has_w, (other + 2, west_col)),
        (has_s & has_e, (other - 2, east_col)), (has_s & has_w, (other - 2, west_col)),
    )

    barrier = pltpu.get_barrier_semaphore()
    count = jnp.int32(0)
    for here, target in targets:
        count = count + here.astype(jnp.int32)

        @pl.when(here)
        def _(target=target):
            pl.semaphore_signal(barrier, inc=1, device_id=target, device_id_type=MESH)

    lane = lax.broadcasted_iota(jnp.int32, (NZ, 128), 1)
    level = lax.broadcasted_iota(jnp.int32, (NZ, 128), 0)
    level_f = level.astype(jnp.float32)
    group = lax.rem(lane, 8)
    zero = jnp.zeros((NZ, 128), jnp.float32)

    def roll(x, by, axis=1):
        by = by % x.shape[axis]
        return pltpu.roll(x, by, axis) if by else x

    def turn_in(n, carry):
        for t in range(2):
            c0[pl.ds(2 + 8 * t, 8), n] = jnp.swapaxes(tr[0, n, :, 8 * t : 8 * t + 8, :], 0, 1)
        return carry

    lax.fori_loop(0, NT, turn_in, 0)

    pl.semaphore_wait(barrier, count)

    def copy(src, dst, k, target):
        return pltpu.make_async_remote_copy(
            src_ref=src, dst_ref=dst, send_sem=send.at[k], recv_sem=recv.at[k],
            device_id=target, device_id_type=MESH,
        )

    own_half = pl.ds(pl.multiple_of(half * 128, 128), 128)
    other_half = pl.ds(pl.multiple_of((1 - half) * 128, 128), 128)
    to_partner = (
        copy(flow.at[:, :, :, other_half], pf, 0, partner),
        copy(temp.at[:, :, other_half], pt, 1, partner),
        copy(bot.at[:, other_half], pb, 2, partner),
        copy(sun.at[:, other_half], ps, 3, partner),
    )
    near = (
        (copy(c0.at[17], c0.at[1], 4, north), has_n, has_s),
        (copy(c0.at[2], c0.at[18], 5, south), has_s, has_n),
    )
    far = (
        (copy(c0.at[16], c0.at[0], 6, north), has_n, has_s),
        (copy(c0.at[3], c0.at[19], 7, south), has_s, has_n),
    )
    rows = (
        (copy(fm0.at[pl.ds(16, 2)], fm0.at[pl.ds(0, 2)], 8, north), has_n, has_s),
        (copy(fm0.at[pl.ds(2, 2)], fm0.at[pl.ds(18, 2)], 9, south), has_s, has_n),
    )
    packs = (
        (copy(xo, xw, 10, east), has_e, has_w),
        (copy(xo, xe, 11, west), has_w, has_e),
        (copy(xo.at[15], xc.at[0], 12, targets[4][1]), has_n & has_e, has_s & has_w),
        (copy(xo.at[15], xc.at[1], 13, targets[5][1]), has_n & has_w, has_s & has_e),
        (copy(xo.at[0], xc.at[2], 14, targets[6][1]), has_s & has_e, has_n & has_w),
        (copy(xo.at[0], xc.at[3], 15, targets[7][1]), has_s & has_w, has_n & has_e),
    )

    def start(group_of):
        for one, sends, _ in group_of:
            @pl.when(sends)
            def _(one=one):
                one.start()

    def arrive(group_of):
        for one, _, receives in group_of:
            @pl.when(receives)
            def _(one=one):
                one.wait_recv()

    def sent(group_of):
        for one, sends, _ in group_of:
            @pl.when(sends)
            def _(one=one):
                one.wait_send()

    for one in to_partner:
        one.start()
    start(near)

    for here, ref, at, length in (
        (has_s, c0, 0, 2), (has_n, c0, 18, 2), (has_s, fm0, 0, 2), (has_n, fm0, 18, 2),
        (has_w, xw, 0, 16), (has_e, xe, 0, 16),
        (has_s & has_w, xc, 0, 1), (has_s & has_e, xc, 1, 1),
        (has_n & has_w, xc, 2, 1), (has_n & has_e, xc, 3, 1),
    ):
        @pl.when(jnp.logical_not(here))
        def _(ref=ref, at=at, length=length):
            def clear(r, carry):
                ref[at + r] = jnp.zeros(ref.shape[1:], jnp.float32)
                return carry

            lax.fori_loop(0, length, clear, 0)

    spread = (
        lax.broadcasted_iota(jnp.int32, (128, NT), 0) // 8
        == lax.broadcasted_iota(jnp.int32, (128, NT), 1)
    ).astype(jnp.float32)
    tall = jnp.dot(
        spread, rates[...], precision=lax.Precision.HIGHEST, preferred_element_type=jnp.float32
    )
    square = lax.dot_general(
        tall, spread, (((1,), (1,)), ((), ())), precision=lax.Precision.HIGHEST,
        preferred_element_type=jnp.float32,
    )
    same = lax.rem(lax.broadcasted_iota(jnp.int32, (128, 128), 0), 8) == lax.rem(
        lax.broadcasted_iota(jnp.int32, (128, 128), 1), 8
    )
    wmat[...] = jnp.where(same, square, 0.0)

    def fill(first, field_u, field_v, field_h, field_b, field_s):
        for r in range(8):
            base = field_b[r : r + 1, :].astype(jnp.float32)
            wet = (level_f < jnp.broadcast_to(base, (NZ, 128))).astype(jnp.float32)
            i = first + r
            fm0[i, 0] = field_u[r] * wet
            fm0[i, 1] = field_v[r] * wet
            fm0[i, 2] = field_h[r] * wet
            light = jnp.broadcast_to(field_s[r : r + 1, :], (NZ, 128))
            fm0[i, 3] = jnp.where(level == 0, jnp.broadcast_to(base, (NZ, 128)), light)

    def turn(x):
        return jnp.swapaxes(x, 0, 1)

    fill(
        2 + 8 * half,
        turn(flow[0, :, :, own_half]), turn(flow[1, :, :, own_half]), turn(temp[:, :, own_half]),
        bot[:, own_half], sun[:, own_half],
    )
    for one in to_partner:
        one.wait_recv()
    fill(10 - 8 * half, turn(pf[0]), turn(pf[1]), turn(pt[...]), pb[...], ps[...])
    start(rows)

    def pack(j, carry):
        i = j + 2
        acc = zero
        for n in range(NT):
            x = c0[i, n]
            acc = jnp.where((lane // 2) == (8 * n + 2) // 2, roll(x, 8 * n + 2), acc)
            acc = jnp.where((lane // 2) == (8 * n + 4) // 2, roll(x, 8 * n + 6), acc)
        for f in range(4):
            x = fm0[i, f]
            acc = jnp.where((lane // 2) == (8 * f + 6) // 2, roll(x, 8 * f + 6), acc)
            acc = jnp.where((lane // 2) == (8 * f + 8) // 2, roll(x, 8 * f + 10), acc)
        xo[j] = acc
        return carry

    lax.fori_loop(0, 16, pack, 0)
    start(packs)
    start(far)

    arrive(rows)
    arrive(packs)

    def spread_field(x, f):
        y = jnp.where(lane < 8, roll(x, -8 * f), 0.0)
        for by in (8, 16, 32, 64):
            y = y + roll(y, by)
        return y

    def unpack(i, own, w, e):
        p0[i] = jnp.where(group < 2, roll(w, -4), jnp.where(group >= 6, roll(e, 4), own))
        fields = jnp.where(group < 2, roll(w, -8), jnp.where(group >= 6, e, roll(own, -4)))
        for f in range(4):
            fp0[i, f] = spread_field(fields, f)

    def unpack_row(j, carry):
        unpack(j + 2, xo[j], xw[j], xe[j])
        return carry

    lax.fori_loop(0, 16, unpack_row, 0)
    unpack(1, zero, xc[0], xc[1])
    unpack(18, zero, xc[2], xc[3])
    for i in (0, 19):
        p0[i] = zero
        for f in range(4):
            fp0[i, f] = zero

    def wet_of(aux):
        return (level_f < jnp.broadcast_to(aux[0:1, :], (NZ, 128))).astype(jnp.float32)

    def light_of(aux):
        return jnp.broadcast_to(aux[1:2, :], (NZ, 128))

    def shear_pressure(u, v, h):
        du = u - roll(u, 7, 0)
        dv = v - roll(v, 7, 0)
        q = jnp.where(level < NZ - 1, du * du + dv * dv, 0.0)
        kappa = kappa_base + kappa_shear * q / (1.0 + q)
        total = h
        for by in (1, 2, 4):
            total = total + jnp.where(level >= by, roll(total, by, 0), 0.0)
        return kappa, -expansion * total

    def prepare(fm, fp, first, last):
        def one(i, carry):
            for f, k in ((fm, kpm), (fp, kpp)):
                kappa, pressure = shear_pressure(f[i, 0], f[i, 1], f[i, 2])
                k[i, 0] = kappa
                k[i, 1] = pressure
            return carry

        lax.fori_loop(first, last, one, 0)

    def east_of(m, p, n=0):
        return jnp.where(lane == 127, roll(p, 121 - 8 * n), roll(m, 127))

    def west_of(m, p, n=0):
        return jnp.where(lane == 0, roll(p, 127 - 8 * n), roll(m, 1))

    def apply(a, x, xe_, xw_, xn, xs):
        return (
            a[0] * x + a[1] * xe_ + a[2] * xw_ + a[3] * xn + a[4] * xs
            + a[5] * roll(x, 1, 0) + a[6] * roll(x, 7, 0)
        )

    def flow_row(i, f, k, aux, e_of, w_of, coriolis):
        u, v, h = f[i, 0], f[i, 1], f[i, 2]
        kappa, pressure = k[i, 0], k[i, 1]
        un, us = f[i + 1, 0], f[i - 1, 0]
        vn, vs = f[i + 1, 1], f[i - 1, 1]
        wet = wet_of(aux[i, 3])
        wet_e = w_e = e_of(3)
        wet_w = w_of(3)
        oe = wet * wet_e
        ow = wet * wet_w
        on = wet * wet_of(aux[i + 1, 3])
        os = wet * wet_of(aux[i - 1, 3])
        ue, uw, ve, vw = e_of(0), w_of(0), e_of(1), w_of(1)
        fe = 0.5 * (u + ue) * oe
        fw = 0.5 * (u + uw) * ow
        fn = 0.5 * (v + vn) * on
        fs = 0.5 * (v + vs) * os
        ce = 0.5 * (kappa + e_of(4)) * oe
        cw = 0.5 * (kappa + w_of(4)) * ow
        cn = 0.5 * (kappa + k[i + 1, 0]) * on
        cs = 0.5 * (kappa + k[i - 1, 0]) * os
        lap_u = oe * (ue - u) + ow * (uw - u) + on * (un - u) + os * (us - u)
        lap_v = oe * (ve - v) + ow * (vw - v) + on * (vn - v) + os * (vs - v)
        new_u = wet * (
            u + time_step * (coriolis * v - 0.5 * (e_of(5) - w_of(5)) + viscosity * lap_u)
        )
        new_v = wet * (
            v
            + time_step
            * (-coriolis * u - 0.5 * (k[i + 1, 1] - k[i - 1, 1]) + viscosity * lap_v)
        )
        div = fe - fw + fn - fs
        total = div
        for by in (1, 2, 4):
            total = total + jnp.where(level < NZ - by, roll(total, NZ - by, 0), 0.0)
        w_top = jnp.where(level >= 1, -total, 0.0)
        w_bot = jnp.where(level < NZ - 1, -roll(total, NZ - 1, 0), 0.0)
        a = (
            wet
            * (
                1.0
                - time_step * (ce + cw + cn + cs)
                - 0.5 * time_step * (div + w_top - w_bot)
            ),
            time_step * (ce - 0.5 * fe),
            time_step * (cw + 0.5 * fw),
            time_step * (cn - 0.5 * fn),
            time_step * (cs + 0.5 * fs),
            (-0.5 * time_step) * w_top * wet,
            (0.5 * time_step) * w_bot * wet,
        )
        moved = apply(a, h, e_of(2), w_of(2), f[i + 1, 2], f[i - 1, 2])
        return a, new_u, new_v, moved

    first_lat = 8 * n_row

    def coriolis_of(i):
        latitude = (16 * chip + i - 2).astype(jnp.float32)
        return coriolis_base * (2.0 * (latitude + 0.5) / first_lat - 1.0)

    def main_shift(i, fm, fp, of):
        def one(f):
            if f == 3:
                return of(wet_of(fm0[i, 3]), wet_of(fp0[i, 3]))
            if f >= 4:
                return of(kpm[i, f - 4], kpp[i, f - 4])
            return of(fm[i, f], fp[i, f])

        return one

    def packed_shift(i, fp, by):
        def one(f):
            if f == 3:
                return roll(wet_of(fp0[i, 3]), by)
            if f >= 4:
                return roll(kpp[i, f - 4], by)
            return roll(fp[i, f], by)

        return one

    def flow_main(i, fm, fp, fm_new):
        a, u, v, h = flow_row(
            i, fm, kpm, fm0, main_shift(i, fm, fp, east_of), main_shift(i, fm, fp, west_of),
            coriolis_of(i),
        )
        for s in range(7):
            am[i, s] = a[s]
        fm_new[i, 0] = u
        fm_new[i, 1] = v
        fm_new[i, 2] = h

    def flow_packed(i, fp, fp_new):
        a, u, v, h = flow_row(
            i, fp, kpp, fp0, packed_shift(i, fp, 127), packed_shift(i, fp, 1), coriolis_of(i)
        )
        for s in range(7):
            ap[i, s] = a[s]
        fp_new[i, 0] = u
        fp_new[i, 1] = v
        fp_new[i, 2] = h

    def profile_of(pigment):
        squared = pigment * pigment
        depth = water_absorb + pigment_absorb * squared / (1.0 + squared)
        above = zero
        for by in (1, 2, 3):
            above = above + jnp.where(level >= by, roll(depth, by, 0), 0.0)
        return jnp.where(
            level < KL, jnp.exp(-above) * (1.0 - jnp.exp(-depth)), 0.0
        )

    def tracer_row(i, c, p, c_new, i_new, fm_new):
        a = [am[i, s] for s in range(7)]
        wet = wet_of(fm0[i, 3])
        ghost = p[i]
        moved = []
        for n in range(NT):
            x = c[i, n]
            moved.append(
                apply(a, x, east_of(x, ghost, n), west_of(x, ghost, n), c[i + 1, n], c[i - 1, n])
            )
        bent = jnp.concatenate([m * lax.rsqrt(1.0 + m * m) for m in moved], axis=0)
        coupling = jnp.dot(
            wmat[...], bent, precision=lax.Precision.HIGHEST, preferred_element_type=jnp.float32
        )
        scale = react_step * wet
        for n in range(NT):
            value = moved[n] + scale * coupling[8 * n : 8 * n + 8]
            c_new[i_new, n] = value
            if n == 0:
                fm_new[i, 2] = fm_new[i, 2] + heat_gain * light_of(fm0[i, 3]) * wet * profile_of(
                    value
                )

    prepare(fm0, fp0, 0, 20)

    def step1_flow(i, carry):
        flow_main(i, fm0, fp0, fm1)
        flow_packed(i, fp0, fp1)
        return carry

    lax.fori_loop(1, 19, step1_flow, 0)

    def step1_packed(i, carry):
        x = p0[i]
        a = [ap[i, s] for s in range(7)]
        m = apply(a, x, roll(x, 127), roll(x, 1), p0[i + 1], p0[i - 1])
        p1[i] = m
        psat[pl.ds(pl.multiple_of(8 * (i - 2), 8), 8), :] = m * lax.rsqrt(1.0 + m * m)
        return carry

    lax.fori_loop(2, 18, step1_packed, 0)
    psat[...] = lax.dot_general(
        psat[...], wmat[...], (((1,), (1,)), ((), ())), precision=lax.Precision.HIGHEST,
        preferred_element_type=jnp.float32,
    )

    def step1_react(i, carry):
        wet = wet_of(fp0[i, 3])
        value = p1[i] + react_step * wet * psat[pl.ds(pl.multiple_of(8 * (i - 2), 8), 8), :]
        p1[i] = value
        fp1[i, 2] = fp1[i, 2] + heat_gain * light_of(fp0[i, 3]) * wet * profile_of(
            spread_field(value, 0)
        )
        return carry

    lax.fori_loop(2, 18, step1_react, 0)

    arrive(near)

    def step1_main(i, carry):
        tracer_row(i, c0, p0, c1, i, fm1)
        return carry

    lax.fori_loop(2, 18, step1_main, 0)

    prepare(fm1, fp1, 2, 18)

    def step2_main(i, carry):
        flow_main(i, fm1, fp1, fm0_next)
        tracer_row(i, c1, p1, c2, i - 2, fm0_next)
        return carry

    fm0_next = ap_flow
    lax.fori_loop(3, 17, step2_main, 0)

    arrive(far)
    step1_main(1, 0)
    step1_main(18, 0)

    def prepare_main(i):
        kappa, pressure = shear_pressure(fm1[i, 0], fm1[i, 1], fm1[i, 2])
        kpm[i, 0] = kappa
        kpm[i, 1] = pressure

    prepare_main(1)
    prepare_main(18)
    step2_main(2, 0)
    step2_main(17, 0)

    mine = 2 + 8 * half
    theirs = 10 - 8 * half
    for f in range(3):
        fo[f] = turn(fm0_next[pl.ds(theirs, 8), f])
    back = copy(fo, fr, 16, partner)
    back.start()

    def turn_out(n, carry):
        for t in range(2):
            tr_out[0, n, :, 8 * t : 8 * t + 8, :] = jnp.swapaxes(c2[8 * t : 8 * t + 8, n], 0, 1)
        return carry

    lax.fori_loop(0, NT, turn_out, 0)
    for f in range(2):
        flow_out[f, :, :, own_half] = turn(fm0_next[pl.ds(mine, 8), f])
    temp_out[:, :, own_half] = turn(fm0_next[pl.ds(mine, 8), 2])
    back.wait_recv()
    for f in range(2):
        flow_out[f, :, :, other_half] = fr[f]
    temp_out[:, :, other_half] = fr[2]
    for one in to_partner:
        one.wait_send()
    sent(near)
    sent(rows)
    sent(packs)
    sent(far)
    back.wait_send()


def on_device(n_row, n_col, *args):
    f32 = jnp.float32
    vmem = pl.BlockSpec(memory_space=pltpu.VMEM)
    tile = (NZ, 128)
    return tuple(
        pl.pallas_call(
            functools.partial(kernel, n_row, n_col),
            out_shape=(
                jax.ShapeDtypeStruct((2, NZ, 8, 256), f32),
                jax.ShapeDtypeStruct((NZ, 8, 256), f32),
                jax.ShapeDtypeStruct((1, NT, NZ, 16, 128), f32),
            ),
            in_specs=[vmem] * 6,
            out_specs=(vmem, vmem, vmem),
            scratch_shapes=[
                pltpu.VMEM((20, NT) + tile, f32),
                pltpu.VMEM((20, NT) + tile, f32),
                pltpu.VMEM((16, NT) + tile, f32),
                pltpu.VMEM((20,) + tile, f32),
                pltpu.VMEM((20,) + tile, f32),
                pltpu.VMEM((128, 128), f32),
                pltpu.VMEM((20, 4) + tile, f32),
                pltpu.VMEM((20, 4) + tile, f32),
                pltpu.VMEM((20, 3) + tile, f32),
                pltpu.VMEM((20, 3) + tile, f32),
                pltpu.VMEM((20, 2) + tile, f32),
                pltpu.VMEM((20, 2) + tile, f32),
                pltpu.VMEM((20, 7) + tile, f32),
                pltpu.VMEM((20, 7) + tile, f32),
                pltpu.VMEM((20, 3) + tile, f32),
                pltpu.VMEM((128, 128), f32),
                pltpu.VMEM((16,) + tile, f32),
                pltpu.VMEM((16,) + tile, f32),
                pltpu.VMEM((16,) + tile, f32),
                pltpu.VMEM((4,) + tile, f32),
                pltpu.VMEM((2, NZ, 8, 128), f32),
                pltpu.VMEM((NZ, 8, 128), f32),
                pltpu.VMEM((8, 128), jnp.int32),
                pltpu.VMEM((8, 128), f32),
                pltpu.VMEM((3, NZ, 8, 128), f32),
                pltpu.VMEM((3, NZ, 8, 128), f32),
                pltpu.SemaphoreType.DMA((17,)),
                pltpu.SemaphoreType.DMA((17,)),
            ],
            compiler_params=pltpu.CompilerParams(collective_id=0, has_side_effects=True),
        )(*args)
    )


def solution(mesh):
    in_specs = (
        P(None, None, "row", "col"),
        P(None, "row", "col"),
        P("row", None, None, None, "col"),
        P("row", "col"),
        P("row", "col"),
        P(),
    )
    out_specs = (
        P(None, None, "row", "col"),
        P(None, "row", "col"),
        P("row", None, None, None, "col"),
    )
    return jax.shard_map(
        functools.partial(on_device, mesh.shape["row"], mesh.shape["col"]),
        mesh=mesh, in_specs=in_specs, out_specs=out_specs, check_vma=False,
    )
```

```python
import functools

import jax
import jax.numpy as jnp
from jax import lax
from jax.experimental import pallas as pl
from jax.experimental.pallas import tpu as pltpu
from jax.sharding import PartitionSpec as P

MESH = pl.DeviceIdType.MESH
NT = 16
NZ = 8
KL = 4
PERIOD = 4

time_step = 0.2
viscosity = 0.2
expansion = 0.05
coriolis_base = 0.5
kappa_base = 0.05
kappa_shear = 0.2
react_step = 0.25
water_absorb = 0.1
pigment_absorb = 0.6
heat_gain = 1.0


def kernel(
    n_row, n_col,
    flow, temp, tr, bot, sun, rates,
    c2, mine_out, theirs_out,
    c0, c1, p0, p1, psat, fm0, fp0, fm1, fp1, fm2, kpm, kpp, kpm1, kpp1, am, ap, wmat,
    xo, xw, xe, px_out, px_in, pf, pt, pb, ps, fr,
    send, recv, ready,
):
    row = lax.axis_index("row")
    col = lax.axis_index("col")
    half = lax.rem(row, 2)
    chip = row // 2
    other = 2 * chip + 1 - half
    west_col = col - 1 + half
    east_col = col + half
    has_w = west_col >= 0
    has_e = east_col < n_col
    has_n = row + 2 < n_row
    has_s = row >= 2
    partner = (other, col)
    west = (other, west_col)
    east = (other, east_col)
    north = (row + 2, col)
    south = (row - 2, col)
    place = lax.rem(chip, PERIOD)
    late_n = has_n & (place != PERIOD - 1)
    late_s = has_s & (place == 0)
    soon_n = has_n & (place == PERIOD - 1)
    soon_s = has_s & (place != 0)

    barrier = pltpu.get_barrier_semaphore()
    for tells, target in ((has_e, east), (has_w, west), (late_n, north), (late_s, south)):
        @pl.when(tells)
        def _(target=target):
            pl.semaphore_signal(barrier, inc=1, device_id=target, device_id_type=MESH)

    count = jnp.int32(0)
    for waits in (has_e, has_w, soon_n, soon_s):
        count = count + waits.astype(jnp.int32)

    lane = lax.broadcasted_iota(jnp.int32, (NZ, 128), 1)
    level = lax.broadcasted_iota(jnp.int32, (NZ, 128), 0)
    level_f = level.astype(jnp.float32)
    group = lax.rem(lane, 8)
    zero = jnp.zeros((NZ, 128), jnp.float32)

    def roll(x, by, axis=1):
        by = by % x.shape[axis]
        return pltpu.roll(x, by, axis) if by else x

    def turn_in(n, carry):
        for t in range(2):
            c0[pl.ds(2 + 8 * t, 8), n] = jnp.swapaxes(tr[0, n, :, 8 * t : 8 * t + 8, :], 0, 1)
        return carry

    lax.fori_loop(0, NT, turn_in, 0)

    def copy(src, dst, k, target):
        return pltpu.make_async_remote_copy(
            src_ref=src, dst_ref=dst, send_sem=send.at[k], recv_sem=recv.at[k],
            device_id=target, device_id_type=MESH,
        )

    own_half = pl.ds(pl.multiple_of(half * 128, 128), 128)
    other_half = pl.ds(pl.multiple_of((1 - half) * 128, 128), 128)
    to_partner = (
        copy(flow.at[:, :, :, other_half], pf, 0, partner),
        copy(temp.at[:, :, other_half], pt, 1, partner),
        copy(bot.at[:, other_half], pb, 2, partner),
        copy(sun.at[:, other_half], ps, 3, partner),
    )
    to_east = copy(xo, xw, 4, east)
    to_west = copy(xo, xe, 5, west)
    near_n = copy(c0.at[17], c0.at[1], 6, north)
    near_s = copy(c0.at[2], c0.at[18], 7, south)
    far_n = copy(c0.at[16], c0.at[0], 8, north)
    far_s = copy(c0.at[3], c0.at[19], 9, south)
    rows_n = copy(fm0.at[pl.ds(16, 2)], fm0.at[pl.ds(0, 2)], 10, north)
    rows_s = copy(fm0.at[pl.ds(2, 2)], fm0.at[pl.ds(18, 2)], 11, south)
    edge_n = copy(px_out.at[1], px_in.at[0], 12, north)
    edge_s = copy(px_out.at[0], px_in.at[1], 13, south)

    def start(here, *copies):
        @pl.when(here)
        def _():
            for one in copies:
                one.start()

    for here, ref, at, length in (
        (has_s, c0, 0, 2), (has_n, c0, 18, 2), (has_s, fm0, 0, 2), (has_n, fm0, 18, 2),
        (has_w, xw, 0, 16), (has_e, xe, 0, 16), (has_s, px_in, 0, 1), (has_n, px_in, 1, 1),
    ):
        @pl.when(jnp.logical_not(here))
        def _(ref=ref, at=at, length=length):
            def clear(r, carry):
                ref[at + r] = jnp.zeros(ref.shape[1:], jnp.float32)
                return carry

            lax.fori_loop(0, length, clear, 0)

    pl.semaphore_wait(barrier, count)
    for one in to_partner:
        one.start()
    for here, target, k in ((soon_s, south, 0), (soon_n, north, 1)):
        @pl.when(here)
        def _(target=target, k=k):
            pl.semaphore_signal(ready.at[k], inc=1, device_id=target, device_id_type=MESH)

    start(soon_n, near_n, far_n)
    start(soon_s, near_s, far_s)

    spread = (
        lax.broadcasted_iota(jnp.int32, (128, NT), 0) // 8
        == lax.broadcasted_iota(jnp.int32, (128, NT), 1)
    ).astype(jnp.float32)
    tall = jnp.dot(
        spread, rates[...], precision=lax.Precision.HIGHEST, preferred_element_type=jnp.float32
    )
    square = lax.dot_general(
        tall, spread, (((1,), (1,)), ((), ())), precision=lax.Precision.HIGHEST,
        preferred_element_type=jnp.float32,
    )
    same = lax.rem(lax.broadcasted_iota(jnp.int32, (128, 128), 0), 8) == lax.rem(
        lax.broadcasted_iota(jnp.int32, (128, 128), 1), 8
    )
    wmat[...] = jnp.where(same, square, 0.0)

    def fill(first, field_u, field_v, field_h, field_b, field_s):
        for r in range(8):
            base = field_b[r : r + 1, :].astype(jnp.float32)
            wet = (level_f < jnp.broadcast_to(base, (NZ, 128))).astype(jnp.float32)
            i = first + r
            fm0[i, 0] = field_u[r] * wet
            fm0[i, 1] = field_v[r] * wet
            fm0[i, 2] = field_h[r] * wet
            light = jnp.broadcast_to(field_s[r : r + 1, :], (NZ, 128))
            fm0[i, 3] = jnp.where(level == 0, jnp.broadcast_to(base, (NZ, 128)), light)

    def turn(x):
        return jnp.swapaxes(x, 0, 1)

    fill(
        2 + 8 * half,
        turn(flow[0, :, :, own_half]), turn(flow[1, :, :, own_half]), turn(temp[:, :, own_half]),
        bot[:, own_half], sun[:, own_half],
    )
    for one in to_partner:
        one.wait_recv()
    fill(10 - 8 * half, turn(pf[0]), turn(pf[1]), turn(pt[...]), pb[...], ps[...])
    start(soon_n, rows_n)
    start(soon_s, rows_s)

    def pack(j, carry):
        i = j + 2
        acc = zero
        for n in range(NT):
            x = c0[i, n]
            acc = jnp.where((lane // 2) == (8 * n + 2) // 2, roll(x, 8 * n + 2), acc)
            acc = jnp.where((lane // 2) == (8 * n + 4) // 2, roll(x, 8 * n + 6), acc)
        for f in range(4):
            x = fm0[i, f]
            acc = jnp.where((lane // 2) == (8 * f + 6) // 2, roll(x, 8 * f + 6), acc)
            acc = jnp.where((lane // 2) == (8 * f + 8) // 2, roll(x, 8 * f + 10), acc)
        xo[j] = acc
        return carry

    lax.fori_loop(0, 16, pack, 0)
    start(has_e, to_east)
    start(has_w, to_west)

    @pl.when(has_w)
    def _():
        to_east.wait_recv()

    @pl.when(has_e)
    def _():
        to_west.wait_recv()

    def spread_field(x, f):
        y = jnp.where(lane < 8, roll(x, -8 * f), 0.0)
        for by in (8, 16, 32, 64):
            y = y + roll(y, by)
        return y

    def unpack_row(j, carry):
        own, w, e = xo[j], xw[j], xe[j]
        p0[j + 2] = jnp.where(group < 2, roll(w, -4), jnp.where(group >= 6, roll(e, 4), own))
        fields = fields_of(j)
        for f in range(4):
            fp0[j + 2, f] = spread_field(fields, f)
        return carry

    def fields_of(j):
        return jnp.where(group < 2, roll(xw[j], -8), jnp.where(group >= 6, xe[j], roll(xo[j], -4)))

    lax.fori_loop(0, 16, unpack_row, 0)
    for side, j in ((0, 0), (1, 15)):
        px_out[side, 0] = p0[j + 2]
        px_out[side, 1] = fields_of(j)
    start(soon_n, edge_n)
    start(soon_s, edge_s)

    @pl.when(late_n)
    def _():
        pl.semaphore_wait(ready.at[0], 1)
        for one in (near_n, rows_n, far_n, edge_n):
            one.start()

    def wet_of(aux):
        return (level_f < jnp.broadcast_to(aux[0:1, :], (NZ, 128))).astype(jnp.float32)

    def light_of(aux):
        return jnp.broadcast_to(aux[1:2, :], (NZ, 128))

    def shear_pressure(u, v, h):
        du = u - roll(u, 7, 0)
        dv = v - roll(v, 7, 0)
        q = jnp.where(level < NZ - 1, du * du + dv * dv, 0.0)
        kappa = kappa_base + kappa_shear * q / (1.0 + q)
        total = h
        for by in (1, 2, 4):
            total = total + jnp.where(level >= by, roll(total, by, 0), 0.0)
        return kappa, -expansion * total

    def prepare_row(i, f, k):
        kappa, pressure = shear_pressure(f[i, 0], f[i, 1], f[i, 2])
        k[i, 0] = kappa
        k[i, 1] = pressure

    def prepare(fm, fp, km, kp, first, last):
        def one(i, carry):
            prepare_row(i, fm, km)
            prepare_row(i, fp, kp)
            return carry

        lax.fori_loop(first, last, one, 0)

    def east_of(m, p, n=0):
        return jnp.where(lane == 127, roll(p, 121 - 8 * n), roll(m, 127))

    def west_of(m, p, n=0):
        return jnp.where(lane == 0, roll(p, 127 - 8 * n), roll(m, 1))

    def apply(a, x, xe_, xw_, xn, xs):
        return (
            a[0] * x + a[1] * xe_ + a[2] * xw_ + a[3] * xn + a[4] * xs
            + a[5] * roll(x, 1, 0) + a[6] * roll(x, 7, 0)
        )

    def flow_row(i, f, k, aux, e_of, w_of, coriolis):
        u, v, h = f[i, 0], f[i, 1], f[i, 2]
        kappa, pressure = k[i, 0], k[i, 1]
        un, us = f[i + 1, 0], f[i - 1, 0]
        vn, vs = f[i + 1, 1], f[i - 1, 1]
        wet = wet_of(aux[i, 3])
        wet_e = w_e = e_of(3)
        wet_w = w_of(3)
        oe = wet * wet_e
        ow = wet * wet_w
        on = wet * wet_of(aux[i + 1, 3])
        os = wet * wet_of(aux[i - 1, 3])
        ue, uw, ve, vw = e_of(0), w_of(0), e_of(1), w_of(1)
        fe = 0.5 * (u + ue) * oe
        fw = 0.5 * (u + uw) * ow
        fn = 0.5 * (v + vn) * on
        fs = 0.5 * (v + vs) * os
        ce = 0.5 * (kappa + e_of(4)) * oe
        cw = 0.5 * (kappa + w_of(4)) * ow
        cn = 0.5 * (kappa + k[i + 1, 0]) * on
        cs = 0.5 * (kappa + k[i - 1, 0]) * os
        lap_u = oe * (ue - u) + ow * (uw - u) + on * (un - u) + os * (us - u)
        lap_v = oe * (ve - v) + ow * (vw - v) + on * (vn - v) + os * (vs - v)
        new_u = wet * (
            u + time_step * (coriolis * v - 0.5 * (e_of(5) - w_of(5)) + viscosity * lap_u)
        )
        new_v = wet * (
            v
            + time_step
            * (-coriolis * u - 0.5 * (k[i + 1, 1] - k[i - 1, 1]) + viscosity * lap_v)
        )
        div = fe - fw + fn - fs
        total = div
        for by in (1, 2, 4):
            total = total + jnp.where(level < NZ - by, roll(total, NZ - by, 0), 0.0)
        w_top = jnp.where(level >= 1, -total, 0.0)
        w_bot = jnp.where(level < NZ - 1, -roll(total, NZ - 1, 0), 0.0)
        a = (
            wet
            * (
                1.0
                - time_step * (ce + cw + cn + cs)
                - 0.5 * time_step * (div + w_top - w_bot)
            ),
            time_step * (ce - 0.5 * fe),
            time_step * (cw + 0.5 * fw),
            time_step * (cn - 0.5 * fn),
            time_step * (cs + 0.5 * fs),
            (-0.5 * time_step) * w_top * wet,
            (0.5 * time_step) * w_bot * wet,
        )
        moved = apply(a, h, e_of(2), w_of(2), f[i + 1, 2], f[i - 1, 2])
        return a, new_u, new_v, moved

    first_lat = 8 * n_row

    def coriolis_of(i):
        latitude = (16 * chip + i - 2).astype(jnp.float32)
        return coriolis_base * (2.0 * (latitude + 0.5) / first_lat - 1.0)

    def main_shift(i, fm, fp, km, kp, of):
        def one(f):
            if f == 3:
                return of(wet_of(fm0[i, 3]), wet_of(fp0[i, 3]))
            if f >= 4:
                return of(km[i, f - 4], kp[i, f - 4])
            return of(fm[i, f], fp[i, f])

        return one

    def packed_shift(i, by):
        def one(f):
            if f == 3:
                return roll(wet_of(fp0[i, 3]), by)
            if f >= 4:
                return roll(kpp[i, f - 4], by)
            return roll(fp0[i, f], by)

        return one

    def keep(i, result, a_new, f_new):
        a, u, v, h = result
        for s in range(7):
            a_new[i, s] = a[s]
        f_new[i, 0] = u
        f_new[i, 1] = v
        f_new[i, 2] = h

    def flow_main(i, fm, fp, km, kp, f_new):
        keep(
            i,
            flow_row(
                i, fm, km, fm0, main_shift(i, fm, fp, km, kp, east_of),
                main_shift(i, fm, fp, km, kp, west_of), coriolis_of(i),
            ),
            am, f_new,
        )

    def flow_packed(i):
        keep(
            i,
            flow_row(i, fp0, kpp, fp0, packed_shift(i, 127), packed_shift(i, 1), coriolis_of(i)),
            ap, fp1,
        )

    def profile_of(pigment):
        squared = pigment * pigment
        depth = water_absorb + pigment_absorb * squared / (1.0 + squared)
        above = zero
        for by in (1, 2, 3):
            above = above + jnp.where(level >= by, roll(depth, by, 0), 0.0)
        return jnp.where(
            level < KL, jnp.exp(-above) * (1.0 - jnp.exp(-depth)), 0.0
        )

    def tracer_row(i, c, p, c_new, i_new, fm_new):
        a = [am[i, s] for s in range(7)]
        wet = wet_of(fm0[i, 3])
        ghost = p[i]
        moved = []
        for n in range(NT):
            x = c[i, n]
            moved.append(
                apply(a, x, east_of(x, ghost, n), west_of(x, ghost, n), c[i + 1, n], c[i - 1, n])
            )
        bent = jnp.concatenate([m * lax.rsqrt(1.0 + m * m) for m in moved], axis=0)
        coupling = jnp.dot(
            wmat[...], bent, precision=lax.Precision.HIGHEST, preferred_element_type=jnp.float32
        )
        scale = react_step * wet
        for n in range(NT):
            value = moved[n] + scale * coupling[8 * n : 8 * n + 8]
            c_new[i_new, n] = value
            if n == 0:
                fm_new[i, 2] = fm_new[i, 2] + heat_gain * light_of(fm0[i, 3]) * wet * profile_of(
                    value
                )

    def step1_flow(i, carry):
        flow_main(i, fm0, fp0, kpm, kpp, fm1)
        flow_packed(i)
        return carry

    def packed_moved(i):
        x = p0[i]
        a = [ap[i, s] for s in range(7)]
        m = apply(a, x, roll(x, 127), roll(x, 1), p0[i + 1], p0[i - 1])
        p1[i] = m
        return m * lax.rsqrt(1.0 + m * m)

    def couple(x):
        return lax.dot_general(
            x, wmat[...], (((1,), (1,)), ((), ())), precision=lax.Precision.HIGHEST,
            preferred_element_type=jnp.float32,
        )

    def packed_react(i, coupling):
        wet = wet_of(fp0[i, 3])
        value = p1[i] + react_step * wet * coupling
        p1[i] = value
        fp1[i, 2] = fp1[i, 2] + heat_gain * light_of(fp0[i, 3]) * wet * profile_of(
            spread_field(value, 0)
        )

    def step1_main(i, carry):
        tracer_row(i, c0, p0, c1, i, fm1)
        return carry

    def step2_main(i, carry):
        flow_main(i, fm1, fp1, kpm1, kpp1, fm2)
        tracer_row(i, c1, p1, c2, i - 2, fm2)
        return carry

    prepare(fm0, fp0, kpm, kpp, 2, 18)
    lax.fori_loop(3, 17, step1_flow, 0)

    def packed_in(i, carry):
        psat[pl.ds(pl.multiple_of(8 * (i - 3), 8), 8), :] = packed_moved(i)
        return carry

    def packed_end(i, carry):
        packed_react(i, psat[pl.ds(pl.multiple_of(8 * (i - 3), 8), 8), :])
        return carry

    lax.fori_loop(3, 17, packed_in, 0)
    psat[...] = couple(psat[...])
    lax.fori_loop(3, 17, packed_end, 0)
    lax.fori_loop(3, 17, step1_main, 0)

    @pl.when(late_s)
    def _():
        pl.semaphore_wait(ready.at[1], 1)
        for one in (near_s, rows_s, far_s, edge_s):
            one.start()

    prepare(fm1, fp1, kpm1, kpp1, 3, 17)
    lax.fori_loop(4, 16, step2_main, 0)

    def finish(out, by, side):
        edge = out + by
        p0[out] = px_in[side, 0]
        for f in range(4):
            fp0[out, f] = spread_field(px_in[side, 1], f)
        prepare_row(out - by, fm0, kpm)
        prepare_row(out, fm0, kpm)
        prepare_row(out, fp0, kpp)
        flow_main(edge, fm0, fp0, kpm, kpp, fm1)
        flow_packed(edge)
        flow_main(out, fm0, fp0, kpm, kpp, fm1)
        packed_react(edge, couple(packed_moved(edge)))
        step1_main(edge, 0)
        step1_main(out, 0)
        prepare_row(edge, fm1, kpm1)
        prepare_row(edge, fp1, kpp1)
        prepare_row(out, fm1, kpm1)
        step2_main(edge + by, 0)
        step2_main(edge, 0)

    @pl.when(has_n)
    def _():
        for one in (near_s, far_s, rows_s, edge_s):
            one.wait_recv()

    finish(18, -1, 1)

    @pl.when(has_s)
    def _():
        for one in (near_n, far_n, rows_n, edge_n):
            one.wait_recv()

    finish(1, 1, 0)

    back = copy(fm2.at[pl.ds(10 - 8 * half, 8)], fr, 14, partner)
    back.start()
    for f in range(3):
        mine_out[:, f] = fm2[pl.ds(2 + 8 * half, 8), f]
    for one in to_partner:
        one.wait_send()
    for here, copies in (
        (has_e, (to_east,)), (has_w, (to_west,)),
        (has_n, (near_n, far_n, rows_n, edge_n)), (has_s, (near_s, far_s, rows_s, edge_s)),
    ):
        @pl.when(here)
        def _(copies=copies):
            for one in copies:
                one.wait_send()

    back.wait()
    theirs_out[...] = fr[...]


def lay_out(c2, mine, theirs, flow_out, temp_out, tr_out):
    half = lax.rem(lax.axis_index("row"), 2)

    def turn_out(n, carry):
        for t in range(2):
            tr_out[0, n, :, 8 * t : 8 * t + 8, :] = jnp.swapaxes(c2[8 * t : 8 * t + 8, n], 0, 1)
        return carry

    lax.fori_loop(0, c2.shape[1], turn_out, 0)

    @pl.when(pl.program_id(0) == 0)
    def _():
        for ref, at in ((mine, half), (theirs, 1 - half)):
            lanes = pl.ds(pl.multiple_of(at * 128, 128), 128)
            for f in range(2):
                flow_out[f, :, :, lanes] = jnp.swapaxes(ref[:, f], 0, 1)
            temp_out[:, :, lanes] = jnp.swapaxes(ref[:, 2], 0, 1)


def on_device(n_row, n_col, *args):
    f32 = jnp.float32
    vmem = pl.BlockSpec(memory_space=pltpu.VMEM)
    tile = (NZ, 128)
    c2, mine, theirs = pl.pallas_call(
        functools.partial(kernel, n_row, n_col),
        out_shape=(
            jax.ShapeDtypeStruct((16, NT) + tile, f32),
            jax.ShapeDtypeStruct((8, 3) + tile, f32),
            jax.ShapeDtypeStruct((8, 3) + tile, f32),
        ),
        in_specs=[vmem] * 6,
        out_specs=(vmem, vmem, vmem),
        scratch_shapes=[
            pltpu.VMEM((20, NT) + tile, f32),
            pltpu.VMEM((20, NT) + tile, f32),
            pltpu.VMEM((20,) + tile, f32),
            pltpu.VMEM((20,) + tile, f32),
            pltpu.VMEM((112, 128), f32),
            pltpu.VMEM((20, 4) + tile, f32),
            pltpu.VMEM((20, 4) + tile, f32),
            pltpu.VMEM((20, 3) + tile, f32),
            pltpu.VMEM((20, 3) + tile, f32),
            pltpu.VMEM((20, 3) + tile, f32),
            pltpu.VMEM((20, 2) + tile, f32),
            pltpu.VMEM((20, 2) + tile, f32),
            pltpu.VMEM((20, 2) + tile, f32),
            pltpu.VMEM((20, 2) + tile, f32),
            pltpu.VMEM((20, 7) + tile, f32),
            pltpu.VMEM((20, 7) + tile, f32),
            pltpu.VMEM((128, 128), f32),
            pltpu.VMEM((16,) + tile, f32),
            pltpu.VMEM((16,) + tile, f32),
            pltpu.VMEM((16,) + tile, f32),
            pltpu.VMEM((2, 2) + tile, f32),
            pltpu.VMEM((2, 2) + tile, f32),
            pltpu.VMEM((2, NZ, 8, 128), f32),
            pltpu.VMEM((NZ, 8, 128), f32),
            pltpu.VMEM((8, 128), jnp.int32),
            pltpu.VMEM((8, 128), f32),
            pltpu.VMEM((8, 3) + tile, f32),
            pltpu.SemaphoreType.DMA((15,)),
            pltpu.SemaphoreType.DMA((15,)),
            pltpu.SemaphoreType.REGULAR((2,)),
        ],
        compiler_params=pltpu.CompilerParams(collective_id=0, has_side_effects=True),
    )(*args)
    small = pl.BlockSpec((8, 3) + tile, lambda g: (0, 0, 0, 0))
    parts = 2
    return tuple(
        pl.pallas_call(
            lay_out,
            grid=(parts,),
            out_shape=(
                jax.ShapeDtypeStruct((2, NZ, 8, 256), f32),
                jax.ShapeDtypeStruct((NZ, 8, 256), f32),
                jax.ShapeDtypeStruct((1, NT, NZ, 16, 128), f32),
            ),
            in_specs=[pl.BlockSpec((16, NT // parts) + tile, lambda g: (0, g, 0, 0)), small, small],
            out_specs=(
                pl.BlockSpec((2, NZ, 8, 256), lambda g: (0, 0, 0, 0)),
                pl.BlockSpec((NZ, 8, 256), lambda g: (0, 0, 0)),
                pl.BlockSpec((1, NT // parts, NZ, 16, 128), lambda g: (0, g, 0, 0, 0)),
            ),
        )(c2, mine, theirs)
    )


def solution(mesh):
    in_specs = (
        P(None, None, "row", "col"),
        P(None, "row", "col"),
        P("row", None, None, None, "col"),
        P("row", "col"),
        P("row", "col"),
        P(),
    )
    out_specs = (
        P(None, None, "row", "col"),
        P(None, "row", "col"),
        P("row", None, None, None, "col"),
    )
    return jax.shard_map(
        functools.partial(on_device, mesh.shape["row"], mesh.shape["col"]),
        mesh=mesh, in_specs=in_specs, out_specs=out_specs, check_vma=False,
    )
```

```python
import functools

import jax
import jax.numpy as jnp
from jax import lax
from jax.experimental import pallas as pl
from jax.experimental.pallas import tpu as pltpu
from jax.sharding import PartitionSpec as P

MESH = pl.DeviceIdType.MESH
NT = 16
NZ = 8
KL = 4
PERIOD = 4

time_step = 0.2
viscosity = 0.2
expansion = 0.05
coriolis_base = 0.5
kappa_base = 0.05
kappa_shear = 0.2
react_step = 0.25
water_absorb = 0.1
pigment_absorb = 0.6
heat_gain = 1.0


def kernel(
    n_row, n_col,
    flow, temp, tr, bot, sun, rates,
    c2, mine_out, theirs_out,
    c0, c1, p0, p1, psat, fm0, fp0, fm1, fp1, fm2, kpm, kpp, kpm1, kpp1, am, ap, wmat, whi, wlo, sbuf,
    xo, xw, xe, px_out, px_in, pf, pt, pb, ps, fr,
    send, recv, ready,
):
    row = lax.axis_index("row")
    col = lax.axis_index("col")
    half = lax.rem(row, 2)
    chip = row // 2
    other = 2 * chip + 1 - half
    west_col = col - 1 + half
    east_col = col + half
    has_w = west_col >= 0
    has_e = east_col < n_col
    has_n = row + 2 < n_row
    has_s = row >= 2
    partner = (other, col)
    west = (other, west_col)
    east = (other, east_col)
    north = (row + 2, col)
    south = (row - 2, col)
    place = lax.rem(chip, PERIOD)
    late_n = has_n & (place != PERIOD - 1)
    late_s = has_s & (place == 0)
    soon_n = has_n & (place == PERIOD - 1)
    soon_s = has_s & (place != 0)

    barrier = pltpu.get_barrier_semaphore()
    for tells, target in ((has_e, east), (has_w, west), (late_n, north), (late_s, south)):
        @pl.when(tells)
        def _(target=target):
            pl.semaphore_signal(barrier, inc=1, device_id=target, device_id_type=MESH)

    count = jnp.int32(0)
    for waits in (has_e, has_w, soon_n, soon_s):
        count = count + waits.astype(jnp.int32)

    lane = lax.broadcasted_iota(jnp.int32, (NZ, 128), 1)
    level = lax.broadcasted_iota(jnp.int32, (NZ, 128), 0)
    level_f = level.astype(jnp.float32)
    group = lax.rem(lane, 8)
    zero = jnp.zeros((NZ, 128), jnp.float32)

    def roll(x, by, axis=1):
        by = by % x.shape[axis]
        return pltpu.roll(x, by, axis) if by else x

    def loop(first, last, by, body):
        def several(k, carry):
            for r in range(by):
                body(first + k * by + r)
            return carry

        assert (last - first) % by == 0
        lax.fori_loop(0, (last - first) // by, several, 0)

    def turn_in(n, carry):
        for t in range(2):
            c0[pl.ds(2 + 8 * t, 8), n] = jnp.swapaxes(tr[0, n, :, 8 * t : 8 * t + 8, :], 0, 1)
        return carry

    lax.fori_loop(0, NT, turn_in, 0)

    def copy(src, dst, k, target):
        return pltpu.make_async_remote_copy(
            src_ref=src, dst_ref=dst, send_sem=send.at[k], recv_sem=recv.at[k],
            device_id=target, device_id_type=MESH,
        )

    own_half = pl.ds(pl.multiple_of(half * 128, 128), 128)
    other_half = pl.ds(pl.multiple_of((1 - half) * 128, 128), 128)
    to_partner = (
        copy(flow.at[:, :, :, other_half], pf, 0, partner),
        copy(temp.at[:, :, other_half], pt, 1, partner),
        copy(bot.at[:, other_half], pb, 2, partner),
        copy(sun.at[:, other_half], ps, 3, partner),
    )
    to_east = copy(xo, xw, 4, east)
    to_west = copy(xo, xe, 5, west)
    near_n = copy(c0.at[17], c0.at[1], 6, north)
    near_s = copy(c0.at[2], c0.at[18], 7, south)
    far_n = copy(c0.at[16], c0.at[0], 8, north)
    far_s = copy(c0.at[3], c0.at[19], 9, south)
    rows_n = copy(fm0.at[pl.ds(16, 2)], fm0.at[pl.ds(0, 2)], 10, north)
    rows_s = copy(fm0.at[pl.ds(2, 2)], fm0.at[pl.ds(18, 2)], 11, south)
    edge_n = copy(px_out.at[1], px_in.at[0], 12, north)
    edge_s = copy(px_out.at[0], px_in.at[1], 13, south)

    def start(here, *copies):
        @pl.when(here)
        def _():
            for one in copies:
                one.start()

    for here, ref, at, length in (
        (has_s, c0, 0, 2), (has_n, c0, 18, 2), (has_s, fm0, 0, 2), (has_n, fm0, 18, 2),
        (has_w, xw, 0, 16), (has_e, xe, 0, 16), (has_s, px_in, 0, 1), (has_n, px_in, 1, 1),
    ):
        @pl.when(jnp.logical_not(here))
        def _(ref=ref, at=at, length=length):
            def clear(r, carry):
                ref[at + r] = jnp.zeros(ref.shape[1:], jnp.float32)
                return carry

            lax.fori_loop(0, length, clear, 0)

    pl.semaphore_wait(barrier, count)
    for one in to_partner:
        one.start()
    for here, target, k in ((soon_s, south, 0), (soon_n, north, 1)):
        @pl.when(here)
        def _(target=target, k=k):
            pl.semaphore_signal(ready.at[k], inc=1, device_id=target, device_id_type=MESH)

    start(soon_n, near_n, far_n)
    start(soon_s, near_s, far_s)

    spread = (
        lax.broadcasted_iota(jnp.int32, (128, NT), 0) // 8
        == lax.broadcasted_iota(jnp.int32, (128, NT), 1)
    ).astype(jnp.float32)
    tall = jnp.dot(
        spread, rates[...], precision=lax.Precision.HIGHEST, preferred_element_type=jnp.float32
    )
    square = lax.dot_general(
        tall, spread, (((1,), (1,)), ((), ())), precision=lax.Precision.HIGHEST,
        preferred_element_type=jnp.float32,
    )
    same = lax.rem(lax.broadcasted_iota(jnp.int32, (128, 128), 0), 8) == lax.rem(
        lax.broadcasted_iota(jnp.int32, (128, 128), 1), 8
    )
    whole = jnp.where(same, square, 0.0)
    wmat[...] = whole
    upper = whole.astype(jnp.bfloat16)
    lower = (whole - upper.astype(jnp.float32)).astype(jnp.bfloat16)
    for at in (0, 128):
        whi[:, at : at + 128] = upper
        wlo[:, at : at + 128] = lower

    def fill(first, field_u, field_v, field_h, field_b, field_s):
        for r in range(8):
            base = field_b[r : r + 1, :].astype(jnp.float32)
            wet = (level_f < jnp.broadcast_to(base, (NZ, 128))).astype(jnp.float32)
            i = first + r
            fm0[i, 0] = field_u[r] * wet
            fm0[i, 1] = field_v[r] * wet
            fm0[i, 2] = field_h[r] * wet
            light = jnp.broadcast_to(field_s[r : r + 1, :], (NZ, 128))
            fm0[i, 3] = jnp.where(level == 0, jnp.broadcast_to(base, (NZ, 128)), light)

    def turn(x):
        return jnp.swapaxes(x, 0, 1)

    fill(
        2 + 8 * half,
        turn(flow[0, :, :, own_half]), turn(flow[1, :, :, own_half]), turn(temp[:, :, own_half]),
        bot[:, own_half], sun[:, own_half],
    )
    for one in to_partner:
        one.wait_recv()
    fill(10 - 8 * half, turn(pf[0]), turn(pf[1]), turn(pt[...]), pb[...], ps[...])
    start(soon_n, rows_n)
    start(soon_s, rows_s)

    def pack(j):
        i = j + 2
        acc = zero
        for n in range(NT):
            x = c0[i, n]
            acc = jnp.where((lane // 2) == (8 * n + 2) // 2, roll(x, 8 * n + 2), acc)
            acc = jnp.where((lane // 2) == (8 * n + 4) // 2, roll(x, 8 * n + 6), acc)
        for f in range(4):
            x = fm0[i, f]
            acc = jnp.where((lane // 2) == (8 * f + 6) // 2, roll(x, 8 * f + 6), acc)
            acc = jnp.where((lane // 2) == (8 * f + 8) // 2, roll(x, 8 * f + 10), acc)
        xo[j] = acc

    loop(0, 16, 2, pack)
    start(has_e, to_east)
    start(has_w, to_west)

    @pl.when(has_w)
    def _():
        to_east.wait_recv()

    @pl.when(has_e)
    def _():
        to_west.wait_recv()

    def spread_field(x, f):
        y = jnp.where(lane < 8, roll(x, -8 * f), 0.0)
        for by in (8, 16, 32, 64):
            y = y + roll(y, by)
        return y

    def unpack_row(j):
        own, w, e = xo[j], xw[j], xe[j]
        p0[j + 2] = jnp.where(group < 2, roll(w, -4), jnp.where(group >= 6, roll(e, 4), own))
        fields = fields_of(j)
        for f in range(4):
            fp0[j + 2, f] = spread_field(fields, f)

    def fields_of(j):
        return jnp.where(group < 2, roll(xw[j], -8), jnp.where(group >= 6, xe[j], roll(xo[j], -4)))

    loop(0, 16, 4, unpack_row)
    for side, j in ((0, 0), (1, 15)):
        px_out[side, 0] = p0[j + 2]
        px_out[side, 1] = fields_of(j)
    start(soon_n, edge_n)
    start(soon_s, edge_s)

    @pl.when(late_n)
    def _():
        pl.semaphore_wait(ready.at[0], 1)
        for one in (near_n, rows_n, far_n, edge_n):
            one.start()

    def wet_of(aux):
        return (level_f < jnp.broadcast_to(aux[0:1, :], (NZ, 128))).astype(jnp.float32)

    def light_of(aux):
        return jnp.broadcast_to(aux[1:2, :], (NZ, 128))

    def shear_pressure(u, v, h):
        du = u - roll(u, 7, 0)
        dv = v - roll(v, 7, 0)
        q = jnp.where(level < NZ - 1, du * du + dv * dv, 0.0)
        kappa = kappa_base + kappa_shear * q / (1.0 + q)
        total = h
        for by in (1, 2, 4):
            total = total + jnp.where(level >= by, roll(total, by, 0), 0.0)
        return kappa, -expansion * total

    def prepare_row(i, f, k):
        kappa, pressure = shear_pressure(f[i, 0], f[i, 1], f[i, 2])
        k[i, 0] = kappa
        k[i, 1] = pressure

    def prepare(fm, fp, km, kp, first, last):
        def one(i):
            prepare_row(i, fm, km)
            prepare_row(i, fp, kp)

        loop(first, last, 2, one)

    def east_of(m, p, n=0):
        return jnp.where(lane == 127, roll(p, 121 - 8 * n), roll(m, 127))

    def west_of(m, p, n=0):
        return jnp.where(lane == 0, roll(p, 127 - 8 * n), roll(m, 1))

    def apply(a, x, xe_, xw_, xn, xs):
        return (
            a[0] * x + a[1] * xe_ + a[2] * xw_ + a[3] * xn + a[4] * xs
            + a[5] * roll(x, 1, 0) + a[6] * roll(x, 7, 0)
        )

    def flow_row(i, f, k, aux, e_of, w_of, coriolis):
        u, v, h = f[i, 0], f[i, 1], f[i, 2]
        kappa, pressure = k[i, 0], k[i, 1]
        un, us = f[i + 1, 0], f[i - 1, 0]
        vn, vs = f[i + 1, 1], f[i - 1, 1]
        wet = wet_of(aux[i, 3])
        wet_e = w_e = e_of(3)
        wet_w = w_of(3)
        oe = wet * wet_e
        ow = wet * wet_w
        on = wet * wet_of(aux[i + 1, 3])
        os = wet * wet_of(aux[i - 1, 3])
        ue, uw, ve, vw = e_of(0), w_of(0), e_of(1), w_of(1)
        fe = 0.5 * (u + ue) * oe
        fw = 0.5 * (u + uw) * ow
        fn = 0.5 * (v + vn) * on
        fs = 0.5 * (v + vs) * os
        ce = 0.5 * (kappa + e_of(4)) * oe
        cw = 0.5 * (kappa + w_of(4)) * ow
        cn = 0.5 * (kappa + k[i + 1, 0]) * on
        cs = 0.5 * (kappa + k[i - 1, 0]) * os
        lap_u = oe * (ue - u) + ow * (uw - u) + on * (un - u) + os * (us - u)
        lap_v = oe * (ve - v) + ow * (vw - v) + on * (vn - v) + os * (vs - v)
        new_u = wet * (
            u + time_step * (coriolis * v - 0.5 * (e_of(5) - w_of(5)) + viscosity * lap_u)
        )
        new_v = wet * (
            v
            + time_step
            * (-coriolis * u - 0.5 * (k[i + 1, 1] - k[i - 1, 1]) + viscosity * lap_v)
        )
        div = fe - fw + fn - fs
        total = div
        for by in (1, 2, 4):
            total = total + jnp.where(level < NZ - by, roll(total, NZ - by, 0), 0.0)
        w_top = jnp.where(level >= 1, -total, 0.0)
        w_bot = jnp.where(level < NZ - 1, -roll(total, NZ - 1, 0), 0.0)
        a = (
            wet
            * (
                1.0
                - time_step * (ce + cw + cn + cs)
                - 0.5 * time_step * (div + w_top - w_bot)
            ),
            time_step * (ce - 0.5 * fe),
            time_step * (cw + 0.5 * fw),
            time_step * (cn - 0.5 * fn),
            time_step * (cs + 0.5 * fs),
            (-0.5 * time_step) * w_top * wet,
            (0.5 * time_step) * w_bot * wet,
        )
        moved = apply(a, h, e_of(2), w_of(2), f[i + 1, 2], f[i - 1, 2])
        return a, new_u, new_v, moved

    first_lat = 8 * n_row

    def coriolis_of(i):
        latitude = (16 * chip + i - 2).astype(jnp.float32)
        return coriolis_base * (2.0 * (latitude + 0.5) / first_lat - 1.0)

    def main_shift(i, fm, fp, km, kp, of):
        def one(f):
            if f == 3:
                return of(wet_of(fm0[i, 3]), wet_of(fp0[i, 3]))
            if f >= 4:
                return of(km[i, f - 4], kp[i, f - 4])
            return of(fm[i, f], fp[i, f])

        return one

    def packed_shift(i, by):
        def one(f):
            if f == 3:
                return roll(wet_of(fp0[i, 3]), by)
            if f >= 4:
                return roll(kpp[i, f - 4], by)
            return roll(fp0[i, f], by)

        return one

    def keep(i, result, a_new, f_new):
        a, u, v, h = result
        for s in range(7):
            a_new[i, s] = a[s]
        f_new[i, 0] = u
        f_new[i, 1] = v
        f_new[i, 2] = h

    def flow_main(i, fm, fp, km, kp, f_new):
        keep(
            i,
            flow_row(
                i, fm, km, fm0, main_shift(i, fm, fp, km, kp, east_of),
                main_shift(i, fm, fp, km, kp, west_of), coriolis_of(i),
            ),
            am, f_new,
        )

    def flow_packed(i):
        keep(
            i,
            flow_row(i, fp0, kpp, fp0, packed_shift(i, 127), packed_shift(i, 1), coriolis_of(i)),
            ap, fp1,
        )

    def profile_of(pigment):
        squared = pigment * pigment
        depth = water_absorb + pigment_absorb * squared / (1.0 + squared)
        above = zero
        for by in (1, 2, 3):
            above = above + jnp.where(level >= by, roll(depth, by, 0), 0.0)
        return jnp.where(
            level < KL, jnp.exp(-above) * (1.0 - jnp.exp(-depth)), 0.0
        )

    def moved_row(i, c, p, c_new, i_new, slot):
        a = [am[i, s] for s in range(7)]
        ghost = jnp.where(lane % 8 == 0, roll(p[i], -6), roll(p[i], -2))
        lanes = pl.ds(pl.multiple_of(slot * 128, 128), 128)
        for pair in range(NT // 2):
            bent = []
            for n in (2 * pair, 2 * pair + 1):
                x = c[i, n]
                g = roll(ghost, -8 * n)
                x_e = roll(jnp.where(lane == 0, g, x), 127)
                x_w = roll(jnp.where(lane == 127, g, x), 1)
                m = apply(a, x, x_e, x_w, c[i + 1, n], c[i - 1, n])
                c_new[i_new, n] = m
                bent.append(m * lax.rsqrt(1.0 + m * m))
            both = jnp.concatenate(bent, axis=0)
            high = both.astype(jnp.bfloat16)
            low = (both - high.astype(jnp.float32)).astype(jnp.bfloat16)
            sbuf[16 * pair : 16 * pair + 16, lanes] = high
            sbuf[128 + 16 * pair : 144 + 16 * pair, lanes] = low

    def react_rows(rows, slot, c_new, shift, f_new):
        part = sbuf[:, 128 * slot : 128 * slot + 256]
        coupling = jnp.dot(whi[...], part, preferred_element_type=jnp.float32) + jnp.dot(
            wlo[...], part, preferred_element_type=jnp.float32
        )
        for r, i in enumerate(rows):
            wet = wet_of(fm0[i, 3])
            scale = react_step * wet
            for n in range(NT):
                value = c_new[i - shift, n] + scale * coupling[
                    8 * n : 8 * n + 8, 128 * r : 128 * r + 128
                ]
                c_new[i - shift, n] = value
                if n == 0:
                    f_new[i, 2] = f_new[i, 2] + heat_gain * light_of(
                        fm0[i, 3]
                    ) * wet * profile_of(value)

    def step1_flow(i):
        flow_main(i, fm0, fp0, kpm, kpp, fm1)
        flow_packed(i)

    def packed_moved(i):
        x = p0[i]
        a = [ap[i, s] for s in range(7)]
        m = apply(a, x, roll(x, 127), roll(x, 1), p0[i + 1], p0[i - 1])
        p1[i] = m
        return m * lax.rsqrt(1.0 + m * m)

    def couple(x):
        return lax.dot_general(
            x, wmat[...], (((1,), (1,)), ((), ())), precision=lax.Precision.HIGHEST,
            preferred_element_type=jnp.float32,
        )

    def packed_react(i, coupling):
        wet = wet_of(fp0[i, 3])
        value = p1[i] + react_step * wet * coupling
        p1[i] = value
        fp1[i, 2] = fp1[i, 2] + heat_gain * light_of(fp0[i, 3]) * wet * profile_of(
            spread_field(value, 0)
        )

    prepare(fm0, fp0, kpm, kpp, 2, 18)
    loop(3, 17, 2, step1_flow)

    def packed_in(i):
        psat[pl.ds(pl.multiple_of(8 * (i - 3), 8), 8), :] = packed_moved(i)

    def packed_end(i):
        packed_react(i, psat[pl.ds(pl.multiple_of(8 * (i - 3), 8), 8), :])

    loop(3, 17, 7, packed_in)
    psat[...] = couple(psat[...])
    loop(3, 17, 7, packed_end)
    loop(3, 17, 1, lambda i: moved_row(i, c0, p0, c1, i, i - 3))
    for i in range(3, 17, 2):
        react_rows((i, i + 1), i - 3, c1, 0, fm1)

    @pl.when(late_s)
    def _():
        pl.semaphore_wait(ready.at[1], 1)
        for one in (near_s, rows_s, far_s, edge_s):
            one.start()

    prepare(fm1, fp1, kpm1, kpp1, 3, 17)
    loop(4, 16, 2, lambda i: flow_main(i, fm1, fp1, kpm1, kpp1, fm2))
    loop(4, 16, 1, lambda i: moved_row(i, c1, p1, c2, i - 2, i - 4))
    for i in range(4, 16, 2):
        react_rows((i, i + 1), i - 4, c2, 2, fm2)

    def finish(out, by, side):
        edge = out + by
        p0[out] = px_in[side, 0]
        for f in range(4):
            fp0[out, f] = spread_field(px_in[side, 1], f)
        prepare_row(out - by, fm0, kpm)
        prepare_row(out, fm0, kpm)
        prepare_row(out, fp0, kpp)
        flow_main(edge, fm0, fp0, kpm, kpp, fm1)
        flow_packed(edge)
        flow_main(out, fm0, fp0, kpm, kpp, fm1)
        packed_react(edge, couple(packed_moved(edge)))
        moved_row(edge, c0, p0, c1, edge, 0)
        moved_row(out, c0, p0, c1, out, 1)
        react_rows((edge, out), 0, c1, 0, fm1)
        prepare_row(edge, fm1, kpm1)
        prepare_row(edge, fp1, kpp1)
        prepare_row(out, fm1, kpm1)
        flow_main(edge + by, fm1, fp1, kpm1, kpp1, fm2)
        flow_main(edge, fm1, fp1, kpm1, kpp1, fm2)
        moved_row(edge + by, c1, p1, c2, edge + by - 2, 0)
        moved_row(edge, c1, p1, c2, edge - 2, 1)
        react_rows((edge + by, edge), 0, c2, 2, fm2)

    @pl.when(has_n)
    def _():
        for one in (near_s, far_s, rows_s, edge_s):
            one.wait_recv()

    finish(18, -1, 1)

    @pl.when(has_s)
    def _():
        for one in (near_n, far_n, rows_n, edge_n):
            one.wait_recv()

    finish(1, 1, 0)

    back = copy(fm2.at[pl.ds(10 - 8 * half, 8)], fr, 14, partner)
    back.start()
    for f in range(3):
        mine_out[:, f] = fm2[pl.ds(2 + 8 * half, 8), f]
    for one in to_partner:
        one.wait_send()
    for here, copies in (
        (has_e, (to_east,)), (has_w, (to_west,)),
        (has_n, (near_n, far_n, rows_n, edge_n)), (has_s, (near_s, far_s, rows_s, edge_s)),
    ):
        @pl.when(here)
        def _(copies=copies):
            for one in copies:
                one.wait_send()

    back.wait()
    theirs_out[...] = fr[...]


def lay_out(c2, mine, theirs, flow_out, temp_out, tr_out):
    half = lax.rem(lax.axis_index("row"), 2)

    def turn_out(n, carry):
        for t in range(2):
            tr_out[0, n, :, 8 * t : 8 * t + 8, :] = jnp.swapaxes(c2[8 * t : 8 * t + 8, n], 0, 1)
        return carry

    lax.fori_loop(0, c2.shape[1], turn_out, 0)

    @pl.when(pl.program_id(0) == 0)
    def _():
        for ref, at in ((mine, half), (theirs, 1 - half)):
            lanes = pl.ds(pl.multiple_of(at * 128, 128), 128)
            for f in range(2):
                flow_out[f, :, :, lanes] = jnp.swapaxes(ref[:, f], 0, 1)
            temp_out[:, :, lanes] = jnp.swapaxes(ref[:, 2], 0, 1)


def on_device(n_row, n_col, *args):
    f32 = jnp.float32
    vmem = pl.BlockSpec(memory_space=pltpu.VMEM)
    tile = (NZ, 128)
    c2, mine, theirs = pl.pallas_call(
        functools.partial(kernel, n_row, n_col),
        out_shape=(
            jax.ShapeDtypeStruct((16, NT) + tile, f32),
            jax.ShapeDtypeStruct((8, 3) + tile, f32),
            jax.ShapeDtypeStruct((8, 3) + tile, f32),
        ),
        in_specs=[vmem] * 6,
        out_specs=(vmem, vmem, vmem),
        scratch_shapes=[
            pltpu.VMEM((20, NT) + tile, f32),
            pltpu.VMEM((20, NT) + tile, f32),
            pltpu.VMEM((20,) + tile, f32),
            pltpu.VMEM((20,) + tile, f32),
            pltpu.VMEM((112, 128), f32),
            pltpu.VMEM((20, 4) + tile, f32),
            pltpu.VMEM((20, 4) + tile, f32),
            pltpu.VMEM((20, 3) + tile, f32),
            pltpu.VMEM((20, 3) + tile, f32),
            pltpu.VMEM((20, 3) + tile, f32),
            pltpu.VMEM((20, 2) + tile, f32),
            pltpu.VMEM((20, 2) + tile, f32),
            pltpu.VMEM((20, 2) + tile, f32),
            pltpu.VMEM((20, 2) + tile, f32),
            pltpu.VMEM((20, 7) + tile, f32),
            pltpu.VMEM((20, 7) + tile, f32),
            pltpu.VMEM((128, 128), f32),
            pltpu.VMEM((128, 256), jnp.bfloat16),
            pltpu.VMEM((128, 256), jnp.bfloat16),
            pltpu.VMEM((256, 14 * 128), jnp.bfloat16),
            pltpu.VMEM((16,) + tile, f32),
            pltpu.VMEM((16,) + tile, f32),
            pltpu.VMEM((16,) + tile, f32),
            pltpu.VMEM((2, 2) + tile, f32),
            pltpu.VMEM((2, 2) + tile, f32),
            pltpu.VMEM((2, NZ, 8, 128), f32),
            pltpu.VMEM((NZ, 8, 128), f32),
            pltpu.VMEM((8, 128), jnp.int32),
            pltpu.VMEM((8, 128), f32),
            pltpu.VMEM((8, 3) + tile, f32),
            pltpu.SemaphoreType.DMA((15,)),
            pltpu.SemaphoreType.DMA((15,)),
            pltpu.SemaphoreType.REGULAR((2,)),
        ],
        compiler_params=pltpu.CompilerParams(collective_id=0, has_side_effects=True),
    )(*args)
    small = pl.BlockSpec((8, 3) + tile, lambda g: (0, 0, 0, 0))
    parts = 2
    return tuple(
        pl.pallas_call(
            lay_out,
            grid=(parts,),
            out_shape=(
                jax.ShapeDtypeStruct((2, NZ, 8, 256), f32),
                jax.ShapeDtypeStruct((NZ, 8, 256), f32),
                jax.ShapeDtypeStruct((1, NT, NZ, 16, 128), f32),
            ),
            in_specs=[pl.BlockSpec((16, NT // parts) + tile, lambda g: (0, g, 0, 0)), small, small],
            out_specs=(
                pl.BlockSpec((2, NZ, 8, 256), lambda g: (0, 0, 0, 0)),
                pl.BlockSpec((NZ, 8, 256), lambda g: (0, 0, 0)),
                pl.BlockSpec((1, NT // parts, NZ, 16, 128), lambda g: (0, g, 0, 0, 0)),
            ),
        )(c2, mine, theirs)
    )


def solution(mesh):
    in_specs = (
        P(None, None, "row", "col"),
        P(None, "row", "col"),
        P("row", None, None, None, "col"),
        P("row", "col"),
        P("row", "col"),
        P(),
    )
    out_specs = (
        P(None, None, "row", "col"),
        P(None, "row", "col"),
        P("row", None, None, None, "col"),
    )
    return jax.shard_map(
        functools.partial(on_device, mesh.shape["row"], mesh.shape["col"]),
        mesh=mesh, in_specs=in_specs, out_specs=out_specs, check_vma=False,
    )
```

```python
import functools

import jax
import jax.numpy as jnp
from jax import lax
from jax.experimental import pallas as pl
from jax.experimental.pallas import tpu as pltpu
from jax.sharding import PartitionSpec as P

MESH = pl.DeviceIdType.MESH
NT = 16
NZ = 8
KL = 4
PERIOD = 4

time_step = 0.2
viscosity = 0.2
expansion = 0.05
coriolis_base = 0.5
kappa_base = 0.05
kappa_shear = 0.2
react_step = 0.25
water_absorb = 0.1
pigment_absorb = 0.6
heat_gain = 1.0


def kernel(
    n_row, n_col,
    flow, temp, tr, bot, sun, rates,
    c2, mine_out, theirs_out,
    c0, c1, p0, p1, psat, fm0, fp0, fm1, fp1, fm2, kpm, kpp, kpm1, kpp1, am, ap, wmat, whi, wlo, sbuf,
    xo, xf, te, tw, xw, xe, px_out, px_in, pf, pt, pb, ps, fr,
    send, recv, ready,
):
    row = lax.axis_index("row")
    col = lax.axis_index("col")
    half = lax.rem(row, 2)
    chip = row // 2
    other = 2 * chip + 1 - half
    west_col = col - 1 + half
    east_col = col + half
    has_w = west_col >= 0
    has_e = east_col < n_col
    has_n = row + 2 < n_row
    has_s = row >= 2
    partner = (other, col)
    west = (other, west_col)
    east = (other, east_col)
    north = (row + 2, col)
    south = (row - 2, col)
    place = lax.rem(chip, PERIOD)
    late_n = has_n & (place != PERIOD - 1)
    late_s = has_s & (place == 0)
    soon_n = has_n & (place == PERIOD - 1)
    soon_s = has_s & (place != 0)

    barrier = pltpu.get_barrier_semaphore()
    for tells, target in ((has_e, east), (has_w, west), (late_n, north), (late_s, south)):
        @pl.when(tells)
        def _(target=target):
            pl.semaphore_signal(barrier, inc=1, device_id=target, device_id_type=MESH)

    count = jnp.int32(0)
    for waits in (has_e, has_w, soon_n, soon_s):
        count = count + waits.astype(jnp.int32)

    lane = lax.broadcasted_iota(jnp.int32, (NZ, 128), 1)
    level = lax.broadcasted_iota(jnp.int32, (NZ, 128), 0)
    level_f = level.astype(jnp.float32)
    group = lax.rem(lane, 8)
    zero = jnp.zeros((NZ, 128), jnp.float32)

    def roll(x, by, axis=1):
        by = by % x.shape[axis]
        return pltpu.roll(x, by, axis) if by else x

    def loop(first, last, by, body):
        def several(k, carry):
            for r in range(by):
                body(first + k * by + r)
            return carry

        assert (last - first) % by == 0
        lax.fori_loop(0, (last - first) // by, several, 0)

    def turn_in(n, carry):
        for t in range(2):
            c0[pl.ds(2 + 8 * t, 8), n] = jnp.swapaxes(tr[0, n, :, 8 * t : 8 * t + 8, :], 0, 1)
        return carry

    lax.fori_loop(0, NT, turn_in, 0)

    def copy(src, dst, k, target):
        return pltpu.make_async_remote_copy(
            src_ref=src, dst_ref=dst, send_sem=send.at[k], recv_sem=recv.at[k],
            device_id=target, device_id_type=MESH,
        )

    own_half = pl.ds(pl.multiple_of(half * 128, 128), 128)
    other_half = pl.ds(pl.multiple_of((1 - half) * 128, 128), 128)
    to_partner = (
        copy(flow.at[:, :, :, other_half], pf, 0, partner),
        copy(temp.at[:, :, other_half], pt, 1, partner),
        copy(bot.at[:, other_half], pb, 2, partner),
        copy(sun.at[:, other_half], ps, 3, partner),
    )
    to_east = copy(te, xw, 4, east)
    to_west = copy(tw, xe, 5, west)
    near_n = copy(c0.at[17], c0.at[1], 6, north)
    near_s = copy(c0.at[2], c0.at[18], 7, south)
    far_n = copy(c0.at[16], c0.at[0], 8, north)
    far_s = copy(c0.at[3], c0.at[19], 9, south)
    rows_n = copy(fm0.at[pl.ds(16, 2)], fm0.at[pl.ds(0, 2)], 10, north)
    rows_s = copy(fm0.at[pl.ds(2, 2)], fm0.at[pl.ds(18, 2)], 11, south)
    edge_n = copy(px_out.at[1], px_in.at[0], 12, north)
    edge_s = copy(px_out.at[0], px_in.at[1], 13, south)

    def start(here, *copies):
        @pl.when(here)
        def _():
            for one in copies:
                one.start()

    for here, ref, at, length in (
        (has_s, c0, 0, 2), (has_n, c0, 18, 2), (has_s, fm0, 0, 2), (has_n, fm0, 18, 2),
        (has_w, xw, 0, 5), (has_e, xe, 0, 5), (has_s, px_in, 0, 1), (has_n, px_in, 1, 1),
    ):
        @pl.when(jnp.logical_not(here))
        def _(ref=ref, at=at, length=length):
            def clear(r, carry):
                ref[at + r] = jnp.zeros(ref.shape[1:], jnp.float32)
                return carry

            lax.fori_loop(0, length, clear, 0)

    pl.semaphore_wait(barrier, count)
    for one in to_partner:
        one.start()
    for here, target, k in ((soon_s, south, 0), (soon_n, north, 1)):
        @pl.when(here)
        def _(target=target, k=k):
            pl.semaphore_signal(ready.at[k], inc=1, device_id=target, device_id_type=MESH)

    start(soon_n, near_n)
    start(soon_s, near_s)

    spread = (
        lax.broadcasted_iota(jnp.int32, (128, NT), 0) // 8
        == lax.broadcasted_iota(jnp.int32, (128, NT), 1)
    ).astype(jnp.float32)
    tall = jnp.dot(
        spread, rates[...], precision=lax.Precision.HIGHEST, preferred_element_type=jnp.float32
    )
    square = lax.dot_general(
        tall, spread, (((1,), (1,)), ((), ())), precision=lax.Precision.HIGHEST,
        preferred_element_type=jnp.float32,
    )
    same = lax.rem(lax.broadcasted_iota(jnp.int32, (128, 128), 0), 8) == lax.rem(
        lax.broadcasted_iota(jnp.int32, (128, 128), 1), 8
    )
    whole = jnp.where(same, square, 0.0)
    wmat[...] = whole
    upper = whole.astype(jnp.bfloat16)
    lower = (whole - upper.astype(jnp.float32)).astype(jnp.bfloat16)
    for at in (0, 128):
        whi[:, at : at + 128] = upper
        wlo[:, at : at + 128] = lower

    def fill(first, field_u, field_v, field_h, field_b, field_s):
        for r in range(8):
            base = field_b[r : r + 1, :].astype(jnp.float32)
            wet = (level_f < jnp.broadcast_to(base, (NZ, 128))).astype(jnp.float32)
            i = first + r
            fm0[i, 0] = field_u[r] * wet
            fm0[i, 1] = field_v[r] * wet
            fm0[i, 2] = field_h[r] * wet
            light = jnp.broadcast_to(field_s[r : r + 1, :], (NZ, 128))
            fm0[i, 3] = jnp.where(level == 0, jnp.broadcast_to(base, (NZ, 128)), light)

    def turn(x):
        return jnp.swapaxes(x, 0, 1)

    fill(
        2 + 8 * half,
        turn(flow[0, :, :, own_half]), turn(flow[1, :, :, own_half]), turn(temp[:, :, own_half]),
        bot[:, own_half], sun[:, own_half],
    )
    for one in to_partner:
        one.wait_recv()
    fill(10 - 8 * half, turn(pf[0]), turn(pf[1]), turn(pt[...]), pb[...], ps[...])

    def pack(j):
        i = j + 2
        acc = zero
        for n in range(NT):
            x = c0[i, n]
            acc = jnp.where((lane // 2) == (8 * n + 2) // 2, roll(x, 8 * n + 2), acc)
            acc = jnp.where((lane // 2) == (8 * n + 4) // 2, roll(x, 8 * n + 6), acc)
        xo[j] = acc
        acc = zero
        for f in range(4):
            x = fm0[i, f]
            acc = jnp.where((lane // 2) == (8 * f + 2) // 2, roll(x, 8 * f + 2), acc)
            acc = jnp.where((lane // 2) == (8 * f + 4) // 2, roll(x, 8 * f + 6), acc)
        xf[j] = acc

    loop(0, 16, 2, pack)

    for tile_of, first in ((te, 4), (tw, 2)):
        fields = zero
        for q in range(4):
            tracers = zero
            for r in range(4):
                here = group // 2 == r
                tracers = jnp.where(here, roll(xo[4 * q + r], 2 * r - first), tracers)
                fields = jnp.where(
                    here & (lane // 32 == q), roll(xf[4 * q + r], 32 * q + 2 * r - first), fields
                )
            tile_of[q] = tracers
        tile_of[4] = fields
    start(has_e, to_east)
    start(has_w, to_west)
    start(soon_n, rows_n)
    start(soon_s, rows_s)

    @pl.when(has_w)
    def _():
        to_east.wait_recv()

    @pl.when(has_e)
    def _():
        to_west.wait_recv()

    def spread_field(x, f):
        y = jnp.where(lane < 8, roll(x, -8 * f), 0.0)
        for by in (8, 16, 32, 64):
            y = y + roll(y, by)
        return y

    def sides(own, w, e, by_w, by_e):
        return jnp.where(group < 2, roll(w, by_w), jnp.where(group >= 6, roll(e, by_e), own))

    def fields_of(j):
        by = 32 * (j // 4) + 2 * (j % 4)
        return sides(xf[j], xw[4], xe[4], -by, 6 - by)

    for j in range(16):
        q, by = j // 4, 2 * (j % 4)
        p0[j + 2] = sides(xo[j], xw[q], xe[q], -by, 6 - by)
        fields = fields_of(j)
        for f in range(4):
            fp0[j + 2, f] = spread_field(fields, f)
    for side, j in ((0, 0), (1, 15)):
        px_out[side, 0] = p0[j + 2]
        px_out[side, 1] = fields_of(j)
    start(soon_n, edge_n, far_n)
    start(soon_s, edge_s, far_s)

    @pl.when(late_n)
    def _():
        pl.semaphore_wait(ready.at[0], 1)
        for one in (near_n, rows_n, edge_n, far_n):
            one.start()

    def wet_of(aux):
        return (level_f < jnp.broadcast_to(aux[0:1, :], (NZ, 128))).astype(jnp.float32)

    def light_of(aux):
        return jnp.broadcast_to(aux[1:2, :], (NZ, 128))

    def shear_pressure(u, v, h):
        du = u - roll(u, 7, 0)
        dv = v - roll(v, 7, 0)
        q = jnp.where(level < NZ - 1, du * du + dv * dv, 0.0)
        kappa = kappa_base + kappa_shear * q / (1.0 + q)
        total = h
        for by in (1, 2, 4):
            total = total + jnp.where(level >= by, roll(total, by, 0), 0.0)
        return kappa, -expansion * total

    def prepare_row(i, f, k):
        kappa, pressure = shear_pressure(f[i, 0], f[i, 1], f[i, 2])
        k[i, 0] = kappa
        k[i, 1] = pressure

    def prepare(fm, fp, km, kp, first, last):
        def one(i):
            prepare_row(i, fm, km)
            prepare_row(i, fp, kp)

        loop(first, last, 2, one)

    def east_of(m, p, n=0):
        return jnp.where(lane == 127, roll(p, 121 - 8 * n), roll(m, 127))

    def west_of(m, p, n=0):
        return jnp.where(lane == 0, roll(p, 127 - 8 * n), roll(m, 1))

    def apply(a, x, xe_, xw_, xn, xs):
        return (
            a[0] * x + a[1] * xe_ + a[2] * xw_ + a[3] * xn + a[4] * xs
            + a[5] * roll(x, 1, 0) + a[6] * roll(x, 7, 0)
        )

    def flow_row(i, f, k, aux, e_of, w_of, coriolis):
        u, v, h = f[i, 0], f[i, 1], f[i, 2]
        kappa, pressure = k[i, 0], k[i, 1]
        un, us = f[i + 1, 0], f[i - 1, 0]
        vn, vs = f[i + 1, 1], f[i - 1, 1]
        wet = wet_of(aux[i, 3])
        wet_e = w_e = e_of(3)
        wet_w = w_of(3)
        oe = wet * wet_e
        ow = wet * wet_w
        on = wet * wet_of(aux[i + 1, 3])
        os = wet * wet_of(aux[i - 1, 3])
        ue, uw, ve, vw = e_of(0), w_of(0), e_of(1), w_of(1)
        fe = 0.5 * (u + ue) * oe
        fw = 0.5 * (u + uw) * ow
        fn = 0.5 * (v + vn) * on
        fs = 0.5 * (v + vs) * os
        ce = 0.5 * (kappa + e_of(4)) * oe
        cw = 0.5 * (kappa + w_of(4)) * ow
        cn = 0.5 * (kappa + k[i + 1, 0]) * on
        cs = 0.5 * (kappa + k[i - 1, 0]) * os
        lap_u = oe * (ue - u) + ow * (uw - u) + on * (un - u) + os * (us - u)
        lap_v = oe * (ve - v) + ow * (vw - v) + on * (vn - v) + os * (vs - v)
        new_u = wet * (
            u + time_step * (coriolis * v - 0.5 * (e_of(5) - w_of(5)) + viscosity * lap_u)
        )
        new_v = wet * (
            v
            + time_step
            * (-coriolis * u - 0.5 * (k[i + 1, 1] - k[i - 1, 1]) + viscosity * lap_v)
        )
        div = fe - fw + fn - fs
        total = div
        for by in (1, 2, 4):
            total = total + jnp.where(level < NZ - by, roll(total, NZ - by, 0), 0.0)
        w_top = jnp.where(level >= 1, -total, 0.0)
        w_bot = jnp.where(level < NZ - 1, -roll(total, NZ - 1, 0), 0.0)
        a = (
            wet
            * (
                1.0
                - time_step * (ce + cw + cn + cs)
                - 0.5 * time_step * (div + w_top - w_bot)
            ),
            time_step * (ce - 0.5 * fe),
            time_step * (cw + 0.5 * fw),
            time_step * (cn - 0.5 * fn),
            time_step * (cs + 0.5 * fs),
            (-0.5 * time_step) * w_top * wet,
            (0.5 * time_step) * w_bot * wet,
        )
        moved = apply(a, h, e_of(2), w_of(2), f[i + 1, 2], f[i - 1, 2])
        return a, new_u, new_v, moved

    first_lat = 8 * n_row

    def coriolis_of(i):
        latitude = (16 * chip + i - 2).astype(jnp.float32)
        return coriolis_base * (2.0 * (latitude + 0.5) / first_lat - 1.0)

    def main_shift(i, fm, fp, km, kp, of):
        def one(f):
            if f == 3:
                return of(wet_of(fm0[i, 3]), wet_of(fp0[i, 3]))
            if f >= 4:
                return of(km[i, f - 4], kp[i, f - 4])
            return of(fm[i, f], fp[i, f])

        return one

    def packed_shift(i, by):
        def one(f):
            if f == 3:
                return roll(wet_of(fp0[i, 3]), by)
            if f >= 4:
                return roll(kpp[i, f - 4], by)
            return roll(fp0[i, f], by)

        return one

    def keep(i, result, a_new, f_new):
        a, u, v, h = result
        for s in range(7):
            a_new[i, s] = a[s]
        f_new[i, 0] = u
        f_new[i, 1] = v
        f_new[i, 2] = h

    def flow_main(i, fm, fp, km, kp, f_new):
        keep(
            i,
            flow_row(
                i, fm, km, fm0, main_shift(i, fm, fp, km, kp, east_of),
                main_shift(i, fm, fp, km, kp, west_of), coriolis_of(i),
            ),
            am, f_new,
        )

    def flow_packed(i):
        keep(
            i,
            flow_row(i, fp0, kpp, fp0, packed_shift(i, 127), packed_shift(i, 1), coriolis_of(i)),
            ap, fp1,
        )

    def profile_of(pigment):
        squared = pigment * pigment
        depth = water_absorb + pigment_absorb * squared / (1.0 + squared)
        above = zero
        for by in (1, 2, 3):
            above = above + jnp.where(level >= by, roll(depth, by, 0), 0.0)
        return jnp.where(
            level < KL, jnp.exp(-above) * (1.0 - jnp.exp(-depth)), 0.0
        )

    def moved_row(i, c, p, c_new, i_new, slot):
        a = [am[i, s] for s in range(7)]
        ghost = jnp.where(lane % 8 == 0, roll(p[i], -6), roll(p[i], -2))
        lanes = pl.ds(pl.multiple_of(slot * 128, 128), 128)
        for pair in range(NT // 2):
            bent = []
            for n in (2 * pair, 2 * pair + 1):
                x = c[i, n]
                g = roll(ghost, -8 * n)
                x_e = roll(jnp.where(lane == 0, g, x), 127)
                x_w = roll(jnp.where(lane == 127, g, x), 1)
                m = apply(a, x, x_e, x_w, c[i + 1, n], c[i - 1, n])
                c_new[i_new, n] = m
                bent.append(m * lax.rsqrt(1.0 + m * m))
            both = jnp.concatenate(bent, axis=0)
            high = both.astype(jnp.bfloat16)
            low = (both - high.astype(jnp.float32)).astype(jnp.bfloat16)
            sbuf[16 * pair : 16 * pair + 16, lanes] = high
            sbuf[128 + 16 * pair : 144 + 16 * pair, lanes] = low

    def react_rows(rows, slot, c_new, shift, f_new):
        part = sbuf[:, 128 * slot : 128 * slot + 256]
        coupling = jnp.dot(whi[...], part, preferred_element_type=jnp.float32) + jnp.dot(
            wlo[...], part, preferred_element_type=jnp.float32
        )
        for r, i in enumerate(rows):
            wet = wet_of(fm0[i, 3])
            scale = react_step * wet
            for n in range(NT):
                value = c_new[i - shift, n] + scale * coupling[
                    8 * n : 8 * n + 8, 128 * r : 128 * r + 128
                ]
                c_new[i - shift, n] = value
                if n == 0:
                    f_new[i, 2] = f_new[i, 2] + heat_gain * light_of(
                        fm0[i, 3]
                    ) * wet * profile_of(value)

    def step1_flow(i):
        flow_main(i, fm0, fp0, kpm, kpp, fm1)
        flow_packed(i)

    def packed_moved(i):
        x = p0[i]
        a = [ap[i, s] for s in range(7)]
        m = apply(a, x, roll(x, 127), roll(x, 1), p0[i + 1], p0[i - 1])
        p1[i] = m
        return m * lax.rsqrt(1.0 + m * m)

    def couple(x):
        return lax.dot_general(
            x, wmat[...], (((1,), (1,)), ((), ())), precision=lax.Precision.HIGHEST,
            preferred_element_type=jnp.float32,
        )

    def packed_react(i, coupling):
        wet = wet_of(fp0[i, 3])
        value = p1[i] + react_step * wet * coupling
        p1[i] = value
        fp1[i, 2] = fp1[i, 2] + heat_gain * light_of(fp0[i, 3]) * wet * profile_of(
            spread_field(value, 0)
        )

    prepare(fm0, fp0, kpm, kpp, 2, 18)
    loop(3, 17, 2, step1_flow)

    def packed_in(i):
        psat[pl.ds(pl.multiple_of(8 * (i - 3), 8), 8), :] = packed_moved(i)

    def packed_end(i):
        packed_react(i, psat[pl.ds(pl.multiple_of(8 * (i - 3), 8), 8), :])

    loop(3, 17, 7, packed_in)
    psat[...] = couple(psat[...])
    loop(3, 17, 7, packed_end)
    loop(3, 17, 1, lambda i: moved_row(i, c0, p0, c1, i, i - 3))
    for i in range(3, 17, 2):
        react_rows((i, i + 1), i - 3, c1, 0, fm1)

    @pl.when(late_s)
    def _():
        pl.semaphore_wait(ready.at[1], 1)
        for one in (near_s, rows_s, edge_s, far_s):
            one.start()

    prepare(fm1, fp1, kpm1, kpp1, 3, 17)
    loop(4, 16, 2, lambda i: flow_main(i, fm1, fp1, kpm1, kpp1, fm2))
    loop(4, 16, 1, lambda i: moved_row(i, c1, p1, c2, i - 2, i - 4))
    for i in range(4, 16, 2):
        react_rows((i, i + 1), i - 4, c2, 2, fm2)

    def finish(out, by, side):
        edge = out + by
        p0[out] = px_in[side, 0]
        for f in range(4):
            fp0[out, f] = spread_field(px_in[side, 1], f)
        prepare_row(out - by, fm0, kpm)
        prepare_row(out, fm0, kpm)
        prepare_row(out, fp0, kpp)
        flow_main(edge, fm0, fp0, kpm, kpp, fm1)
        flow_packed(edge)
        flow_main(out, fm0, fp0, kpm, kpp, fm1)
        packed_react(edge, couple(packed_moved(edge)))
        moved_row(edge, c0, p0, c1, edge, 0)
        moved_row(out, c0, p0, c1, out, 1)
        react_rows((edge, out), 0, c1, 0, fm1)
        prepare_row(edge, fm1, kpm1)
        prepare_row(edge, fp1, kpp1)
        prepare_row(out, fm1, kpm1)
        flow_main(edge + by, fm1, fp1, kpm1, kpp1, fm2)
        flow_main(edge, fm1, fp1, kpm1, kpp1, fm2)
        moved_row(edge + by, c1, p1, c2, edge + by - 2, 0)
        moved_row(edge, c1, p1, c2, edge - 2, 1)
        react_rows((edge + by, edge), 0, c2, 2, fm2)

    @pl.when(has_n)
    def _():
        for one in (near_s, far_s, rows_s, edge_s):
            one.wait_recv()

    finish(18, -1, 1)

    @pl.when(has_s)
    def _():
        for one in (near_n, far_n, rows_n, edge_n):
            one.wait_recv()

    finish(1, 1, 0)

    back = copy(fm2.at[pl.ds(10 - 8 * half, 8)], fr, 14, partner)
    back.start()
    for f in range(3):
        mine_out[:, f] = fm2[pl.ds(2 + 8 * half, 8), f]
    for one in to_partner:
        one.wait_send()
    for here, copies in (
        (has_e, (to_east,)), (has_w, (to_west,)),
        (has_n, (near_n, far_n, rows_n, edge_n)), (has_s, (near_s, far_s, rows_s, edge_s)),
    ):
        @pl.when(here)
        def _(copies=copies):
            for one in copies:
                one.wait_send()

    back.wait()
    theirs_out[...] = fr[...]


def lay_out(c2, mine, theirs, flow_out, temp_out, tr_out):
    half = lax.rem(lax.axis_index("row"), 2)

    def turn_out(n, carry):
        for t in range(2):
            tr_out[0, n, :, 8 * t : 8 * t + 8, :] = jnp.swapaxes(c2[8 * t : 8 * t + 8, n], 0, 1)
        return carry

    lax.fori_loop(0, c2.shape[1], turn_out, 0)

    @pl.when(pl.program_id(0) == 0)
    def _():
        for ref, at in ((mine, half), (theirs, 1 - half)):
            lanes = pl.ds(pl.multiple_of(at * 128, 128), 128)
            for f in range(2):
                flow_out[f, :, :, lanes] = jnp.swapaxes(ref[:, f], 0, 1)
            temp_out[:, :, lanes] = jnp.swapaxes(ref[:, 2], 0, 1)


def on_device(n_row, n_col, *args):
    f32 = jnp.float32
    vmem = pl.BlockSpec(memory_space=pltpu.VMEM)
    tile = (NZ, 128)
    c2, mine, theirs = pl.pallas_call(
        functools.partial(kernel, n_row, n_col),
        out_shape=(
            jax.ShapeDtypeStruct((16, NT) + tile, f32),
            jax.ShapeDtypeStruct((8, 3) + tile, f32),
            jax.ShapeDtypeStruct((8, 3) + tile, f32),
        ),
        in_specs=[vmem] * 6,
        out_specs=(vmem, vmem, vmem),
        scratch_shapes=[
            pltpu.VMEM((20, NT) + tile, f32),
            pltpu.VMEM((20, NT) + tile, f32),
            pltpu.VMEM((20,) + tile, f32),
            pltpu.VMEM((20,) + tile, f32),
            pltpu.VMEM((112, 128), f32),
            pltpu.VMEM((20, 4) + tile, f32),
            pltpu.VMEM((20, 4) + tile, f32),
            pltpu.VMEM((20, 3) + tile, f32),
            pltpu.VMEM((20, 3) + tile, f32),
            pltpu.VMEM((20, 3) + tile, f32),
            pltpu.VMEM((20, 2) + tile, f32),
            pltpu.VMEM((20, 2) + tile, f32),
            pltpu.VMEM((20, 2) + tile, f32),
            pltpu.VMEM((20, 2) + tile, f32),
            pltpu.VMEM((20, 7) + tile, f32),
            pltpu.VMEM((20, 7) + tile, f32),
            pltpu.VMEM((128, 128), f32),
            pltpu.VMEM((128, 256), jnp.bfloat16),
            pltpu.VMEM((128, 256), jnp.bfloat16),
            pltpu.VMEM((256, 14 * 128), jnp.bfloat16),
            pltpu.VMEM((16,) + tile, f32),
            pltpu.VMEM((16,) + tile, f32),
            pltpu.VMEM((5,) + tile, f32),
            pltpu.VMEM((5,) + tile, f32),
            pltpu.VMEM((5,) + tile, f32),
            pltpu.VMEM((5,) + tile, f32),
            pltpu.VMEM((2, 2) + tile, f32),
            pltpu.VMEM((2, 2) + tile, f32),
            pltpu.VMEM((2, NZ, 8, 128), f32),
            pltpu.VMEM((NZ, 8, 128), f32),
            pltpu.VMEM((8, 128), jnp.int32),
            pltpu.VMEM((8, 128), f32),
            pltpu.VMEM((8, 3) + tile, f32),
            pltpu.SemaphoreType.DMA((15,)),
            pltpu.SemaphoreType.DMA((15,)),
            pltpu.SemaphoreType.REGULAR((2,)),
        ],
        compiler_params=pltpu.CompilerParams(collective_id=0, has_side_effects=True),
    )(*args)
    small = pl.BlockSpec((8, 3) + tile, lambda g: (0, 0, 0, 0))
    parts = 2
    return tuple(
        pl.pallas_call(
            lay_out,
            grid=(parts,),
            out_shape=(
                jax.ShapeDtypeStruct((2, NZ, 8, 256), f32),
                jax.ShapeDtypeStruct((NZ, 8, 256), f32),
                jax.ShapeDtypeStruct((1, NT, NZ, 16, 128), f32),
            ),
            in_specs=[pl.BlockSpec((16, NT // parts) + tile, lambda g: (0, g, 0, 0)), small, small],
            out_specs=(
                pl.BlockSpec((2, NZ, 8, 256), lambda g: (0, 0, 0, 0)),
                pl.BlockSpec((NZ, 8, 256), lambda g: (0, 0, 0)),
                pl.BlockSpec((1, NT // parts, NZ, 16, 128), lambda g: (0, g, 0, 0, 0)),
            ),
        )(c2, mine, theirs)
    )


def solution(mesh):
    in_specs = (
        P(None, None, "row", "col"),
        P(None, "row", "col"),
        P("row", None, None, None, "col"),
        P("row", "col"),
        P("row", "col"),
        P(),
    )
    out_specs = (
        P(None, None, "row", "col"),
        P(None, "row", "col"),
        P("row", None, None, None, "col"),
    )
    return jax.shard_map(
        functools.partial(on_device, mesh.shape["row"], mesh.shape["col"]),
        mesh=mesh, in_specs=in_specs, out_specs=out_specs, check_vma=False,
    )
```

```python
import functools

import jax
import jax.numpy as jnp
from jax import lax
from jax.experimental import pallas as pl
from jax.experimental.pallas import tpu as pltpu
from jax.sharding import PartitionSpec as P

MESH = pl.DeviceIdType.MESH
NT = 16
NZ = 8
KL = 4
PERIOD = 4

time_step = 0.2
viscosity = 0.2
expansion = 0.05
coriolis_base = 0.5
kappa_base = 0.05
kappa_shear = 0.2
react_step = 0.25
water_absorb = 0.1
pigment_absorb = 0.6
heat_gain = 1.0


def kernel(
    n_row, n_col,
    flow_h, temp_h, tr_h, bot_h, sun_h, rates_h,
    c2, mine_out, theirs_out,
    c0, c1, p0, p1, psat, fm0, fp0, fm1, fp1, fm2, kpm, kpp, kpm1, kpp1, am, ap, wmat, whi, wlo, sbuf,
    xo, xf, te, tw, xw, xe, px_out, px_in, pf, pt, pb, ps, fr,
    flow, temp, tr, bot, sun, rates,
    send, recv, ready, load,
):
    loads = [
        pltpu.make_async_copy(src, dst, load.at[k])
        for k, (src, dst) in enumerate(
            ((tr_h, tr), (flow_h, flow), (temp_h, temp), (bot_h, bot), (sun_h, sun), (rates_h, rates))
        )
    ]
    for one in loads:
        one.start()

    row = lax.axis_index("row")
    col = lax.axis_index("col")
    half = lax.rem(row, 2)
    chip = row // 2
    other = 2 * chip + 1 - half
    west_col = col - 1 + half
    east_col = col + half
    has_w = west_col >= 0
    has_e = east_col < n_col
    has_n = row + 2 < n_row
    has_s = row >= 2
    partner = (other, col)
    west = (other, west_col)
    east = (other, east_col)
    north = (row + 2, col)
    south = (row - 2, col)
    place = lax.rem(chip, PERIOD)
    late_n = has_n & (place != PERIOD - 1)
    late_s = has_s & (place == 0)
    soon_n = has_n & (place == PERIOD - 1)
    soon_s = has_s & (place != 0)

    barrier = pltpu.get_barrier_semaphore()
    for tells, target in ((has_e, east), (has_w, west), (late_n, north), (late_s, south)):
        @pl.when(tells)
        def _(target=target):
            pl.semaphore_signal(barrier, inc=1, device_id=target, device_id_type=MESH)

    count = jnp.int32(0)
    for waits in (has_e, has_w, soon_n, soon_s):
        count = count + waits.astype(jnp.int32)

    lane = lax.broadcasted_iota(jnp.int32, (NZ, 128), 1)
    level = lax.broadcasted_iota(jnp.int32, (NZ, 128), 0)
    level_f = level.astype(jnp.float32)
    group = lax.rem(lane, 8)
    zero = jnp.zeros((NZ, 128), jnp.float32)

    def roll(x, by, axis=1):
        by = by % x.shape[axis]
        return pltpu.roll(x, by, axis) if by else x

    def loop(first, last, by, body):
        def several(k, carry):
            for r in range(by):
                body(first + k * by + r)
            return carry

        assert (last - first) % by == 0
        lax.fori_loop(0, (last - first) // by, several, 0)

    def turn_in(n, carry):
        for t in range(2):
            c0[pl.ds(2 + 8 * t, 8), n] = jnp.swapaxes(tr[0, n, :, 8 * t : 8 * t + 8, :], 0, 1)
        return carry

    loads[0].wait()
    lax.fori_loop(0, NT, turn_in, 0)
    for one in loads[1:]:
        one.wait()

    def copy(src, dst, k, target):
        return pltpu.make_async_remote_copy(
            src_ref=src, dst_ref=dst, send_sem=send.at[k], recv_sem=recv.at[k],
            device_id=target, device_id_type=MESH,
        )

    own_half = pl.ds(pl.multiple_of(half * 128, 128), 128)
    other_half = pl.ds(pl.multiple_of((1 - half) * 128, 128), 128)
    to_partner = (
        copy(flow.at[:, :, :, other_half], pf, 0, partner),
        copy(temp.at[:, :, other_half], pt, 1, partner),
        copy(bot.at[:, other_half], pb, 2, partner),
        copy(sun.at[:, other_half], ps, 3, partner),
    )
    to_east = copy(te, xw, 4, east)
    to_west = copy(tw, xe, 5, west)
    near_n = copy(c0.at[17], c0.at[1], 6, north)
    near_s = copy(c0.at[2], c0.at[18], 7, south)
    far_n = copy(c0.at[16], c0.at[0], 8, north)
    far_s = copy(c0.at[3], c0.at[19], 9, south)
    rows_n = copy(fm0.at[pl.ds(16, 2)], fm0.at[pl.ds(0, 2)], 10, north)
    rows_s = copy(fm0.at[pl.ds(2, 2)], fm0.at[pl.ds(18, 2)], 11, south)
    edge_n = copy(px_out.at[1], px_in.at[0], 12, north)
    edge_s = copy(px_out.at[0], px_in.at[1], 13, south)

    def start(here, *copies):
        @pl.when(here)
        def _():
            for one in copies:
                one.start()

    for here, ref, at, length in (
        (has_s, c0, 0, 2), (has_n, c0, 18, 2), (has_s, fm0, 0, 2), (has_n, fm0, 18, 2),
        (has_w, xw, 0, 5), (has_e, xe, 0, 5), (has_s, px_in, 0, 1), (has_n, px_in, 1, 1),
    ):
        @pl.when(jnp.logical_not(here))
        def _(ref=ref, at=at, length=length):
            def clear(r, carry):
                ref[at + r] = jnp.zeros(ref.shape[1:], jnp.float32)
                return carry

            lax.fori_loop(0, length, clear, 0)

    pl.semaphore_wait(barrier, count)
    for one in to_partner:
        one.start()
    for here, target, k in ((soon_s, south, 0), (soon_n, north, 1)):
        @pl.when(here)
        def _(target=target, k=k):
            pl.semaphore_signal(ready.at[k], inc=1, device_id=target, device_id_type=MESH)

    start(soon_n, near_n, far_n)
    start(soon_s, near_s)

    spread = (
        lax.broadcasted_iota(jnp.int32, (128, NT), 0) // 8
        == lax.broadcasted_iota(jnp.int32, (128, NT), 1)
    ).astype(jnp.float32)
    tall = jnp.dot(
        spread, rates[...], precision=lax.Precision.HIGHEST, preferred_element_type=jnp.float32
    )
    square = lax.dot_general(
        tall, spread, (((1,), (1,)), ((), ())), precision=lax.Precision.HIGHEST,
        preferred_element_type=jnp.float32,
    )
    same = lax.rem(lax.broadcasted_iota(jnp.int32, (128, 128), 0), 8) == lax.rem(
        lax.broadcasted_iota(jnp.int32, (128, 128), 1), 8
    )
    whole = jnp.where(same, square, 0.0)
    wmat[...] = whole
    upper = whole.astype(jnp.bfloat16)
    lower = (whole - upper.astype(jnp.float32)).astype(jnp.bfloat16)
    for at in (0, 128):
        whi[:, at : at + 128] = upper
        wlo[:, at : at + 128] = lower

    def fill(first, field_u, field_v, field_h, field_b, field_s):
        for r in range(8):
            base = field_b[r : r + 1, :].astype(jnp.float32)
            wet = (level_f < jnp.broadcast_to(base, (NZ, 128))).astype(jnp.float32)
            i = first + r
            fm0[i, 0] = field_u[r] * wet
            fm0[i, 1] = field_v[r] * wet
            fm0[i, 2] = field_h[r] * wet
            light = jnp.broadcast_to(field_s[r : r + 1, :], (NZ, 128))
            fm0[i, 3] = jnp.where(level == 0, jnp.broadcast_to(base, (NZ, 128)), light)

    def turn(x):
        return jnp.swapaxes(x, 0, 1)

    fill(
        2 + 8 * half,
        turn(flow[0, :, :, own_half]), turn(flow[1, :, :, own_half]), turn(temp[:, :, own_half]),
        bot[:, own_half], sun[:, own_half],
    )
    for one in to_partner:
        one.wait_recv()
    fill(10 - 8 * half, turn(pf[0]), turn(pf[1]), turn(pt[...]), pb[...], ps[...])

    def pack(j):
        i = j + 2
        acc = zero
        for n in range(NT):
            x = c0[i, n]
            acc = jnp.where((lane // 2) == (8 * n + 2) // 2, roll(x, 8 * n + 2), acc)
            acc = jnp.where((lane // 2) == (8 * n + 4) // 2, roll(x, 8 * n + 6), acc)
        xo[j] = acc
        acc = zero
        for f in range(4):
            x = fm0[i, f]
            acc = jnp.where((lane // 2) == (8 * f + 2) // 2, roll(x, 8 * f + 2), acc)
            acc = jnp.where((lane // 2) == (8 * f + 4) // 2, roll(x, 8 * f + 6), acc)
        xf[j] = acc

    loop(0, 16, 2, pack)

    for tile_of, first in ((te, 4), (tw, 2)):
        fields = zero
        for q in range(4):
            tracers = zero
            for r in range(4):
                here = group // 2 == r
                tracers = jnp.where(here, roll(xo[4 * q + r], 2 * r - first), tracers)
                fields = jnp.where(
                    here & (lane // 32 == q), roll(xf[4 * q + r], 32 * q + 2 * r - first), fields
                )
            tile_of[q] = tracers
        tile_of[4] = fields
    start(has_e, to_east)
    start(has_w, to_west)
    start(soon_n, rows_n)
    start(soon_s, rows_s)

    @pl.when(has_w)
    def _():
        to_east.wait_recv()

    @pl.when(has_e)
    def _():
        to_west.wait_recv()

    def spread_field(x, f):
        y = jnp.where(lane < 8, roll(x, -8 * f), 0.0)
        for by in (8, 16, 32, 64):
            y = y + roll(y, by)
        return y

    def sides(own, w, e, by_w, by_e):
        return jnp.where(group < 2, roll(w, by_w), jnp.where(group >= 6, roll(e, by_e), own))

    def fields_of(j):
        by = 32 * (j // 4) + 2 * (j % 4)
        return sides(xf[j], xw[4], xe[4], -by, 6 - by)

    for j in range(16):
        q, by = j // 4, 2 * (j % 4)
        p0[j + 2] = sides(xo[j], xw[q], xe[q], -by, 6 - by)
        fields = fields_of(j)
        for f in range(4):
            fp0[j + 2, f] = spread_field(fields, f)
    for side, j in ((0, 0), (1, 15)):
        px_out[side, 0] = p0[j + 2]
        px_out[side, 1] = fields_of(j)
    start(soon_n, edge_n)
    start(soon_s, edge_s, far_s)

    @pl.when(late_n)
    def _():
        pl.semaphore_wait(ready.at[0], 1)
        for one in (near_n, rows_n, edge_n, far_n):
            one.start()

    def wet_of(aux):
        return (level_f < jnp.broadcast_to(aux[0:1, :], (NZ, 128))).astype(jnp.float32)

    def light_of(aux):
        return jnp.broadcast_to(aux[1:2, :], (NZ, 128))

    def shear_pressure(u, v, h):
        du = u - roll(u, 7, 0)
        dv = v - roll(v, 7, 0)
        q = jnp.where(level < NZ - 1, du * du + dv * dv, 0.0)
        kappa = kappa_base + kappa_shear * q / (1.0 + q)
        total = h
        for by in (1, 2, 4):
            total = total + jnp.where(level >= by, roll(total, by, 0), 0.0)
        return kappa, -expansion * total

    def prepare_row(i, f, k):
        kappa, pressure = shear_pressure(f[i, 0], f[i, 1], f[i, 2])
        k[i, 0] = kappa
        k[i, 1] = pressure

    def prepare(fm, fp, km, kp, first, last):
        def one(i):
            prepare_row(i, fm, km)
            prepare_row(i, fp, kp)

        loop(first, last, 2, one)

    def east_of(m, p, n=0):
        return jnp.where(lane == 127, roll(p, 121 - 8 * n), roll(m, 127))

    def west_of(m, p, n=0):
        return jnp.where(lane == 0, roll(p, 127 - 8 * n), roll(m, 1))

    def apply(a, x, xe_, xw_, xn, xs):
        return ((a[0] * x + a[3] * xn) + (a[4] * xs + a[5] * roll(x, 1, 0))) + (
            a[6] * roll(x, 7, 0) + (a[1] * xe_ + a[2] * xw_)
        )

    def flow_row(i, f, k, aux, e_of, w_of, coriolis):
        u, v, h = f[i, 0], f[i, 1], f[i, 2]
        kappa, pressure = k[i, 0], k[i, 1]
        un, us = f[i + 1, 0], f[i - 1, 0]
        vn, vs = f[i + 1, 1], f[i - 1, 1]
        wet = wet_of(aux[i, 3])
        wet_e = w_e = e_of(3)
        wet_w = w_of(3)
        oe = wet * wet_e
        ow = wet * wet_w
        on = wet * wet_of(aux[i + 1, 3])
        os = wet * wet_of(aux[i - 1, 3])
        ue, uw, ve, vw = e_of(0), w_of(0), e_of(1), w_of(1)
        fe = 0.5 * (u + ue) * oe
        fw = 0.5 * (u + uw) * ow
        fn = 0.5 * (v + vn) * on
        fs = 0.5 * (v + vs) * os
        ce = 0.5 * (kappa + e_of(4)) * oe
        cw = 0.5 * (kappa + w_of(4)) * ow
        cn = 0.5 * (kappa + k[i + 1, 0]) * on
        cs = 0.5 * (kappa + k[i - 1, 0]) * os
        lap_u = oe * (ue - u) + ow * (uw - u) + on * (un - u) + os * (us - u)
        lap_v = oe * (ve - v) + ow * (vw - v) + on * (vn - v) + os * (vs - v)
        new_u = wet * (
            u + time_step * (coriolis * v - 0.5 * (e_of(5) - w_of(5)) + viscosity * lap_u)
        )
        new_v = wet * (
            v
            + time_step
            * (-coriolis * u - 0.5 * (k[i + 1, 1] - k[i - 1, 1]) + viscosity * lap_v)
        )
        div = fe - fw + fn - fs
        total = div
        for by in (1, 2, 4):
            total = total + jnp.where(level < NZ - by, roll(total, NZ - by, 0), 0.0)
        w_top = jnp.where(level >= 1, -total, 0.0)
        w_bot = jnp.where(level < NZ - 1, -roll(total, NZ - 1, 0), 0.0)
        a = (
            wet
            * (
                1.0
                - time_step * (ce + cw + cn + cs)
                - 0.5 * time_step * (div + w_top - w_bot)
            ),
            time_step * (ce - 0.5 * fe),
            time_step * (cw + 0.5 * fw),
            time_step * (cn - 0.5 * fn),
            time_step * (cs + 0.5 * fs),
            (-0.5 * time_step) * w_top * wet,
            (0.5 * time_step) * w_bot * wet,
        )
        moved = apply(a, h, e_of(2), w_of(2), f[i + 1, 2], f[i - 1, 2])
        return a, new_u, new_v, moved

    first_lat = 8 * n_row

    def coriolis_of(i):
        latitude = (16 * chip + i - 2).astype(jnp.float32)
        return coriolis_base * (2.0 * (latitude + 0.5) / first_lat - 1.0)

    def main_shift(i, fm, fp, km, kp, of):
        def one(f):
            if f == 3:
                return of(wet_of(fm0[i, 3]), wet_of(fp0[i, 3]))
            if f >= 4:
                return of(km[i, f - 4], kp[i, f - 4])
            return of(fm[i, f], fp[i, f])

        return one

    def packed_shift(i, by):
        def one(f):
            if f == 3:
                return roll(wet_of(fp0[i, 3]), by)
            if f >= 4:
                return roll(kpp[i, f - 4], by)
            return roll(fp0[i, f], by)

        return one

    def keep(i, result, a_new, f_new):
        a, u, v, h = result
        for s in range(7):
            a_new[i, s] = a[s]
        f_new[i, 0] = u
        f_new[i, 1] = v
        f_new[i, 2] = h

    def flow_main(i, fm, fp, km, kp, f_new):
        keep(
            i,
            flow_row(
                i, fm, km, fm0, main_shift(i, fm, fp, km, kp, east_of),
                main_shift(i, fm, fp, km, kp, west_of), coriolis_of(i),
            ),
            am, f_new,
        )

    def flow_packed(i):
        keep(
            i,
            flow_row(i, fp0, kpp, fp0, packed_shift(i, 127), packed_shift(i, 1), coriolis_of(i)),
            ap, fp1,
        )

    def profile_of(pigment):
        squared = pigment * pigment
        depth = water_absorb + pigment_absorb * squared / (1.0 + squared)
        above = zero
        for by in (1, 2, 3):
            above = above + jnp.where(level >= by, roll(depth, by, 0), 0.0)
        return jnp.where(
            level < KL, jnp.exp(-above) * (1.0 - jnp.exp(-depth)), 0.0
        )

    def moved_row(i, c, p, c_new, i_new, slot):
        a = [am[i, s] for s in range(7)]
        ghost = jnp.where(lane % 8 == 0, roll(p[i], -6), roll(p[i], -2))
        lanes = pl.ds(pl.multiple_of(slot * 128, 128), 128)
        for pair in range(NT // 2):
            bent = []
            for n in (2 * pair, 2 * pair + 1):
                x = c[i, n]
                g = roll(ghost, -8 * n)
                x_e = roll(jnp.where(lane == 0, g, x), 127)
                x_w = roll(jnp.where(lane == 127, g, x), 1)
                m = apply(a, x, x_e, x_w, c[i + 1, n], c[i - 1, n])
                c_new[i_new, n] = m
                bent.append(m * lax.rsqrt(1.0 + m * m))
            both = jnp.concatenate(bent, axis=0)
            high = both.astype(jnp.bfloat16)
            low = (both - high.astype(jnp.float32)).astype(jnp.bfloat16)
            sbuf[16 * pair : 16 * pair + 16, lanes] = high
            sbuf[128 + 16 * pair : 144 + 16 * pair, lanes] = low

    def react_rows(rows, slot, c_new, shift, f_new):
        part = sbuf[:, 128 * slot : 128 * slot + 256]
        coupling = jnp.dot(whi[...], part, preferred_element_type=jnp.float32) + jnp.dot(
            wlo[...], part, preferred_element_type=jnp.float32
        )
        for r, i in enumerate(rows):
            wet = wet_of(fm0[i, 3])
            scale = react_step * wet
            for n in range(NT):
                value = c_new[i - shift, n] + scale * coupling[
                    8 * n : 8 * n + 8, 128 * r : 128 * r + 128
                ]
                c_new[i - shift, n] = value
                if n == 0:
                    f_new[i, 2] = f_new[i, 2] + heat_gain * light_of(
                        fm0[i, 3]
                    ) * wet * profile_of(value)

    def step1_flow(i):
        flow_main(i, fm0, fp0, kpm, kpp, fm1)
        flow_packed(i)

    def packed_moved(i):
        x = p0[i]
        a = [ap[i, s] for s in range(7)]
        m = apply(a, x, roll(x, 127), roll(x, 1), p0[i + 1], p0[i - 1])
        p1[i] = m
        return m * lax.rsqrt(1.0 + m * m)

    def couple(x):
        return lax.dot_general(
            x, wmat[...], (((1,), (1,)), ((), ())), precision=lax.Precision.HIGHEST,
            preferred_element_type=jnp.float32,
        )

    def packed_react(i, coupling):
        wet = wet_of(fp0[i, 3])
        value = p1[i] + react_step * wet * coupling
        p1[i] = value
        fp1[i, 2] = fp1[i, 2] + heat_gain * light_of(fp0[i, 3]) * wet * profile_of(
            spread_field(value, 0)
        )

    prepare(fm0, fp0, kpm, kpp, 2, 18)
    loop(3, 17, 2, step1_flow)

    def packed_in(i):
        psat[pl.ds(pl.multiple_of(8 * (i - 3), 8), 8), :] = packed_moved(i)

    def packed_end(i):
        packed_react(i, psat[pl.ds(pl.multiple_of(8 * (i - 3), 8), 8), :])

    loop(3, 17, 7, packed_in)
    psat[...] = couple(psat[...])
    loop(3, 17, 7, packed_end)
    loop(3, 17, 2, lambda i: moved_row(i, c0, p0, c1, i, i - 3))
    for i in range(3, 17, 2):
        react_rows((i, i + 1), i - 3, c1, 0, fm1)

    @pl.when(late_s)
    def _():
        pl.semaphore_wait(ready.at[1], 1)
        for one in (near_s, rows_s, edge_s, far_s):
            one.start()

    prepare(fm1, fp1, kpm1, kpp1, 3, 17)
    loop(4, 16, 2, lambda i: flow_main(i, fm1, fp1, kpm1, kpp1, fm2))
    loop(4, 16, 2, lambda i: moved_row(i, c1, p1, c2, i - 2, i - 4))
    for i in range(4, 16, 2):
        react_rows((i, i + 1), i - 4, c2, 2, fm2)

    def finish(out, by, side):
        edge = out + by
        p0[out] = px_in[side, 0]
        for f in range(4):
            fp0[out, f] = spread_field(px_in[side, 1], f)
        prepare_row(out - by, fm0, kpm)
        prepare_row(out, fm0, kpm)
        prepare_row(out, fp0, kpp)
        flow_main(edge, fm0, fp0, kpm, kpp, fm1)
        flow_packed(edge)
        flow_main(out, fm0, fp0, kpm, kpp, fm1)
        packed_react(edge, couple(packed_moved(edge)))
        moved_row(edge, c0, p0, c1, edge, 0)
        moved_row(out, c0, p0, c1, out, 1)
        react_rows((edge, out), 0, c1, 0, fm1)
        prepare_row(edge, fm1, kpm1)
        prepare_row(edge, fp1, kpp1)
        prepare_row(out, fm1, kpm1)
        flow_main(edge + by, fm1, fp1, kpm1, kpp1, fm2)
        flow_main(edge, fm1, fp1, kpm1, kpp1, fm2)
        moved_row(edge + by, c1, p1, c2, edge + by - 2, 0)
        moved_row(edge, c1, p1, c2, edge - 2, 1)
        react_rows((edge + by, edge), 0, c2, 2, fm2)

    @pl.when(has_n)
    def _():
        for one in (near_s, far_s, rows_s, edge_s):
            one.wait_recv()

    finish(18, -1, 1)

    @pl.when(has_s)
    def _():
        for one in (near_n, far_n, rows_n, edge_n):
            one.wait_recv()

    finish(1, 1, 0)

    back = copy(fm2.at[pl.ds(10 - 8 * half, 8)], fr, 14, partner)
    back.start()
    for f in range(3):
        mine_out[:, f] = fm2[pl.ds(2 + 8 * half, 8), f]
    for one in to_partner:
        one.wait_send()
    for here, copies in (
        (has_e, (to_east,)), (has_w, (to_west,)),
        (has_n, (near_n, far_n, rows_n, edge_n)), (has_s, (near_s, far_s, rows_s, edge_s)),
    ):
        @pl.when(here)
        def _(copies=copies):
            for one in copies:
                one.wait_send()

    back.wait()
    theirs_out[...] = fr[...]


def lay_out(c2, mine, theirs, flow_out, temp_out, tr_out):
    half = lax.rem(lax.axis_index("row"), 2)

    def turn_out(n, carry):
        for t in range(2):
            tr_out[0, n, :, 8 * t : 8 * t + 8, :] = jnp.swapaxes(c2[8 * t : 8 * t + 8, n], 0, 1)
        return carry

    lax.fori_loop(0, c2.shape[1], turn_out, 0)

    @pl.when(pl.program_id(0) == 0)
    def _():
        for ref, at in ((mine, half), (theirs, 1 - half)):
            lanes = pl.ds(pl.multiple_of(at * 128, 128), 128)
            for f in range(2):
                flow_out[f, :, :, lanes] = jnp.swapaxes(ref[:, f], 0, 1)
            temp_out[:, :, lanes] = jnp.swapaxes(ref[:, 2], 0, 1)


def on_device(n_row, n_col, *args):
    f32 = jnp.float32
    vmem = pl.BlockSpec(memory_space=pltpu.VMEM)
    tile = (NZ, 128)
    c2, mine, theirs = pl.pallas_call(
        functools.partial(kernel, n_row, n_col),
        out_shape=(
            jax.ShapeDtypeStruct((16, NT) + tile, f32),
            jax.ShapeDtypeStruct((8, 3) + tile, f32),
            jax.ShapeDtypeStruct((8, 3) + tile, f32),
        ),
        in_specs=[pl.BlockSpec(memory_space=pl.ANY)] * 6,
        out_specs=(vmem, vmem, vmem),
        scratch_shapes=[
            pltpu.VMEM((20, NT) + tile, f32),
            pltpu.VMEM((20, NT) + tile, f32),
            pltpu.VMEM((20,) + tile, f32),
            pltpu.VMEM((20,) + tile, f32),
            pltpu.VMEM((112, 128), f32),
            pltpu.VMEM((20, 4) + tile, f32),
            pltpu.VMEM((20, 4) + tile, f32),
            pltpu.VMEM((20, 3) + tile, f32),
            pltpu.VMEM((20, 3) + tile, f32),
            pltpu.VMEM((20, 3) + tile, f32),
            pltpu.VMEM((20, 2) + tile, f32),
            pltpu.VMEM((20, 2) + tile, f32),
            pltpu.VMEM((20, 2) + tile, f32),
            pltpu.VMEM((20, 2) + tile, f32),
            pltpu.VMEM((20, 7) + tile, f32),
            pltpu.VMEM((20, 7) + tile, f32),
            pltpu.VMEM((128, 128), f32),
            pltpu.VMEM((128, 256), jnp.bfloat16),
            pltpu.VMEM((128, 256), jnp.bfloat16),
            pltpu.VMEM((256, 14 * 128), jnp.bfloat16),
            pltpu.VMEM((16,) + tile, f32),
            pltpu.VMEM((16,) + tile, f32),
            pltpu.VMEM((5,) + tile, f32),
            pltpu.VMEM((5,) + tile, f32),
            pltpu.VMEM((5,) + tile, f32),
            pltpu.VMEM((5,) + tile, f32),
            pltpu.VMEM((2, 2) + tile, f32),
            pltpu.VMEM((2, 2) + tile, f32),
            pltpu.VMEM((2, NZ, 8, 128), f32),
            pltpu.VMEM((NZ, 8, 128), f32),
            pltpu.VMEM((8, 128), jnp.int32),
            pltpu.VMEM((8, 128), f32),
            pltpu.VMEM((8, 3) + tile, f32),
            pltpu.VMEM((2, NZ, 8, 256), f32),
            pltpu.VMEM((NZ, 8, 256), f32),
            pltpu.VMEM((1, NT, NZ, 16, 128), f32),
            pltpu.VMEM((8, 256), jnp.int32),
            pltpu.VMEM((8, 256), f32),
            pltpu.VMEM((NT, NT), f32),
            pltpu.SemaphoreType.DMA((15,)),
            pltpu.SemaphoreType.DMA((15,)),
            pltpu.SemaphoreType.REGULAR((2,)),
            pltpu.SemaphoreType.DMA((6,)),
        ],
        compiler_params=pltpu.CompilerParams(collective_id=0, has_side_effects=True),
    )(*args)
    small = pl.BlockSpec((8, 3) + tile, lambda g: (0, 0, 0, 0))
    parts = 2
    return tuple(
        pl.pallas_call(
            lay_out,
            grid=(parts,),
            out_shape=(
                jax.ShapeDtypeStruct((2, NZ, 8, 256), f32),
                jax.ShapeDtypeStruct((NZ, 8, 256), f32),
                jax.ShapeDtypeStruct((1, NT, NZ, 16, 128), f32),
            ),
            in_specs=[pl.BlockSpec((16, NT // parts) + tile, lambda g: (0, g, 0, 0)), small, small],
            out_specs=(
                pl.BlockSpec((2, NZ, 8, 256), lambda g: (0, 0, 0, 0)),
                pl.BlockSpec((NZ, 8, 256), lambda g: (0, 0, 0)),
                pl.BlockSpec((1, NT // parts, NZ, 16, 128), lambda g: (0, g, 0, 0, 0)),
            ),
        )(c2, mine, theirs)
    )


def solution(mesh):
    in_specs = (
        P(None, None, "row", "col"),
        P(None, "row", "col"),
        P("row", None, None, None, "col"),
        P("row", "col"),
        P("row", "col"),
        P(),
    )
    out_specs = (
        P(None, None, "row", "col"),
        P(None, "row", "col"),
        P("row", None, None, None, "col"),
    )
    return jax.shard_map(
        functools.partial(on_device, mesh.shape["row"], mesh.shape["col"]),
        mesh=mesh, in_specs=in_specs, out_specs=out_specs, check_vma=False,
    )
```

```python
import functools

import jax
import jax.numpy as jnp
from jax import lax
from jax.experimental import pallas as pl
from jax.experimental.pallas import tpu as pltpu
from jax.sharding import PartitionSpec as P

MESH = pl.DeviceIdType.MESH
NT = 16
NZ = 8
KL = 4
PERIOD = 4
RUN = 4

time_step = 0.2
viscosity = 0.2
expansion = 0.05
coriolis_base = 0.5
kappa_base = 0.05
kappa_shear = 0.2
react_step = 0.25
water_absorb = 0.1
pigment_absorb = 0.6
heat_gain = 1.0


def kernel(
    n_row, n_col,
    flow_h, temp_h, tr_h, bot_h, sun_h, rates_h,
    c2, mine_out, theirs_out,
    c0, c1, p0, p1, psat, fm0, fp0, fm1, fp1, fm2, kpm, kpp, kpm1, kpp1, am, ap, wmat, whi, wlo, sbuf,
    xo, xf, te, tw, xw, xe, px_out, px_in, pf, pt, pb, ps, fr,
    flow, temp, tr, bot, sun, rates,
    send, recv, ready, load,
):
    loads = [
        pltpu.make_async_copy(src, dst, load.at[k])
        for k, (src, dst) in enumerate(
            ((tr_h, tr), (flow_h, flow), (temp_h, temp), (bot_h, bot), (sun_h, sun), (rates_h, rates))
        )
    ]
    for one in loads:
        one.start()

    row = lax.axis_index("row")
    col = lax.axis_index("col")
    half = lax.rem(row, 2)
    chip = row // 2
    other = 2 * chip + 1 - half
    west_col = col - 1 + half
    east_col = col + half
    has_w = west_col >= 0
    has_e = east_col < n_col
    has_n = row + 2 < n_row
    has_s = row >= 2
    partner = (other, col)
    west = (other, west_col)
    east = (other, east_col)
    north = (row + 2, col)
    south = (row - 2, col)
    place = lax.rem(chip, PERIOD)
    late_n = has_n & (place != PERIOD - 1)
    late_s = has_s & (place == 0)
    soon_n = has_n & (place == PERIOD - 1)
    soon_s = has_s & (place != 0)
    farthest = lax.rem(col, RUN) == 0

    barrier = pltpu.get_barrier_semaphore()
    for tells, target in ((has_e, east), (has_w, west), (late_n, north), (late_s, south)):
        @pl.when(tells)
        def _(target=target):
            pl.semaphore_signal(barrier, inc=1, device_id=target, device_id_type=MESH)

    count = jnp.int32(0)
    for waits in (has_e, has_w, soon_n, soon_s):
        count = count + waits.astype(jnp.int32)

    lane = lax.broadcasted_iota(jnp.int32, (NZ, 128), 1)
    level = lax.broadcasted_iota(jnp.int32, (NZ, 128), 0)
    level_f = level.astype(jnp.float32)
    group = lax.rem(lane, 8)
    zero = jnp.zeros((NZ, 128), jnp.float32)

    def roll(x, by, axis=1):
        by = by % x.shape[axis]
        return pltpu.roll(x, by, axis) if by else x

    def loop(first, last, by, body):
        def several(k, carry):
            for r in range(by):
                body(first + k * by + r)
            return carry

        assert (last - first) % by == 0
        lax.fori_loop(0, (last - first) // by, several, 0)

    def turn_in(n, carry):
        for t in range(2):
            c0[pl.ds(2 + 8 * t, 8), n] = jnp.swapaxes(tr[0, n, :, 8 * t : 8 * t + 8, :], 0, 1)
        return carry

    loads[0].wait()
    lax.fori_loop(0, NT, turn_in, 0)
    for one in loads[1:]:
        one.wait()

    def copy(src, dst, k, target):
        return pltpu.make_async_remote_copy(
            src_ref=src, dst_ref=dst, send_sem=send.at[k], recv_sem=recv.at[k],
            device_id=target, device_id_type=MESH,
        )

    own_half = pl.ds(pl.multiple_of(half * 128, 128), 128)
    other_half = pl.ds(pl.multiple_of((1 - half) * 128, 128), 128)
    to_partner = (
        copy(flow.at[:, :, :, other_half], pf, 0, partner),
        copy(temp.at[:, :, other_half], pt, 1, partner),
        copy(bot.at[:, other_half], pb, 2, partner),
        copy(sun.at[:, other_half], ps, 3, partner),
    )
    to_east = copy(te, xw, 4, east)
    to_west = copy(tw, xe, 5, west)
    near_n = copy(c0.at[17], c0.at[1], 6, north)
    near_s = copy(c0.at[2], c0.at[18], 7, south)
    far_n = copy(c0.at[16], c0.at[0], 8, north)
    far_s = copy(c0.at[3], c0.at[19], 9, south)
    rows_n = copy(fm0.at[pl.ds(16, 2), pl.ds(0, 3)], fm0.at[pl.ds(0, 2), pl.ds(0, 3)], 10, north)
    rows_s = copy(fm0.at[pl.ds(2, 2), pl.ds(0, 3)], fm0.at[pl.ds(18, 2), pl.ds(0, 3)], 11, south)
    edge_n = copy(px_out.at[1], px_in.at[0], 12, north)
    edge_s = copy(px_out.at[0], px_in.at[1], 13, south)

    def start(here, *copies):
        @pl.when(here)
        def _():
            for one in copies:
                one.start()

    for here, ref, at, length in (
        (has_s, c0, 0, 2), (has_n, c0, 18, 2), (has_s, fm0, 0, 2), (has_n, fm0, 18, 2),
        (has_w, xw, 0, 5), (has_e, xe, 0, 5), (has_s, px_in, 0, 1), (has_n, px_in, 1, 1),
    ):
        @pl.when(jnp.logical_not(here))
        def _(ref=ref, at=at, length=length):
            def clear(r, carry):
                ref[at + r] = jnp.zeros(ref.shape[1:], jnp.float32)
                return carry

            lax.fori_loop(0, length, clear, 0)

    pl.semaphore_wait(barrier, count)
    for one in to_partner:
        one.start()
    for here, target, k in ((soon_s, south, 0), (soon_n, north, 1)):
        @pl.when(here)
        def _(target=target, k=k):
            pl.semaphore_signal(ready.at[k], inc=1, device_id=target, device_id_type=MESH)

    start(soon_n, near_n)
    start(soon_n & farthest, far_n)
    start(soon_s, near_s)

    spread = (
        lax.broadcasted_iota(jnp.int32, (128, NT), 0) // 8
        == lax.broadcasted_iota(jnp.int32, (128, NT), 1)
    ).astype(jnp.float32)
    tall = jnp.dot(
        spread, rates[...], precision=lax.Precision.HIGHEST, preferred_element_type=jnp.float32
    )
    square = lax.dot_general(
        tall, spread, (((1,), (1,)), ((), ())), precision=lax.Precision.HIGHEST,
        preferred_element_type=jnp.float32,
    )
    same = lax.rem(lax.broadcasted_iota(jnp.int32, (128, 128), 0), 8) == lax.rem(
        lax.broadcasted_iota(jnp.int32, (128, 128), 1), 8
    )
    whole = jnp.where(same, square, 0.0)
    wmat[...] = whole
    upper = whole.astype(jnp.bfloat16)
    lower = (whole - upper.astype(jnp.float32)).astype(jnp.bfloat16)
    for at in (0, 128):
        whi[:, at : at + 128] = upper
        wlo[:, at : at + 128] = lower

    def fill(first, field_u, field_v, field_h, field_b, field_s):
        for r in range(8):
            base = field_b[r : r + 1, :].astype(jnp.float32)
            wet = (level_f < jnp.broadcast_to(base, (NZ, 128))).astype(jnp.float32)
            i = first + r
            fm0[i, 0] = field_u[r] * wet
            fm0[i, 1] = field_v[r] * wet
            fm0[i, 2] = field_h[r] * wet
            light = jnp.broadcast_to(field_s[r : r + 1, :], (NZ, 128))
            fm0[i, 3] = jnp.where(level == 0, jnp.broadcast_to(base, (NZ, 128)), light)

    def turn(x):
        return jnp.swapaxes(x, 0, 1)

    fill(
        2 + 8 * half,
        turn(flow[0, :, :, own_half]), turn(flow[1, :, :, own_half]), turn(temp[:, :, own_half]),
        bot[:, own_half], sun[:, own_half],
    )
    for one in to_partner:
        one.wait_recv()
    fill(10 - 8 * half, turn(pf[0]), turn(pf[1]), turn(pt[...]), pb[...], ps[...])

    def pack(j):
        i = j + 2
        acc = zero
        for n in range(NT):
            x = c0[i, n]
            acc = jnp.where((lane // 2) == (8 * n + 2) // 2, roll(x, 8 * n + 2), acc)
            acc = jnp.where((lane // 2) == (8 * n + 4) // 2, roll(x, 8 * n + 6), acc)
        xo[j] = acc
        acc = zero
        for f in range(4):
            x = fm0[i, f]
            acc = jnp.where((lane // 2) == (8 * f + 2) // 2, roll(x, 8 * f + 2), acc)
            acc = jnp.where((lane // 2) == (8 * f + 4) // 2, roll(x, 8 * f + 6), acc)
        xf[j] = acc

    loop(0, 16, 2, pack)

    for tile_of, first in ((te, 4), (tw, 2)):
        fields = zero
        for q in range(4):
            tracers = zero
            for r in range(4):
                here = group // 2 == r
                tracers = jnp.where(here, roll(xo[4 * q + r], 2 * r - first), tracers)
                fields = jnp.where(
                    here & (lane // 32 == q), roll(xf[4 * q + r], 32 * q + 2 * r - first), fields
                )
            tile_of[q] = tracers
        tile_of[4] = fields
    start(has_e, to_east)
    start(has_w, to_west)
    start(soon_n, rows_n)
    start(soon_s, rows_s)

    @pl.when(has_w)
    def _():
        to_east.wait_recv()

    @pl.when(has_e)
    def _():
        to_west.wait_recv()

    def spread_field(x, f):
        y = jnp.where(lane < 8, roll(x, -8 * f), 0.0)
        for by in (8, 16, 32, 64):
            y = y + roll(y, by)
        return y

    def sides(own, w, e, by_w, by_e):
        return jnp.where(group < 2, roll(w, by_w), jnp.where(group >= 6, roll(e, by_e), own))

    def fields_of(j):
        by = 32 * (j // 4) + 2 * (j % 4)
        return sides(xf[j], xw[4], xe[4], -by, 6 - by)

    for j in range(16):
        q, by = j // 4, 2 * (j % 4)
        p0[j + 2] = sides(xo[j], xw[q], xe[q], -by, 6 - by)
        fields = fields_of(j)
        for f in range(4):
            fp0[j + 2, f] = spread_field(fields, f)
    for side, j, two in ((0, 0, (2, 3)), (1, 15, (16, 17))):
        px_out[side, 0] = jnp.where(
            (group == 1) | (group == 6), p0[j + 2], roll(fields_of(j), 1)
        )
        px_out[side, 1] = jnp.where(level < 2, fm0[two[0], 3], roll(fm0[two[1], 3], 2, 0))

    start(soon_n, edge_n)
    start(soon_n & jnp.logical_not(farthest), far_n)
    start(soon_s, edge_s, far_s)

    @pl.when(late_n)
    def _():
        pl.semaphore_wait(ready.at[0], 1)
        for one in (near_n, rows_n, edge_n, far_n):
            one.start()

    def wet_of(aux):
        return (level_f < jnp.broadcast_to(aux[0:1, :], (NZ, 128))).astype(jnp.float32)

    def light_of(aux):
        return jnp.broadcast_to(aux[1:2, :], (NZ, 128))

    def shear_pressure(u, v, h):
        du = u - roll(u, 7, 0)
        dv = v - roll(v, 7, 0)
        q = jnp.where(level < NZ - 1, du * du + dv * dv, 0.0)
        kappa = kappa_base + kappa_shear * q / (1.0 + q)
        total = h
        for by in (1, 2, 4):
            total = total + jnp.where(level >= by, roll(total, by, 0), 0.0)
        return kappa, -expansion * total

    def prepare_row(i, f, k):
        kappa, pressure = shear_pressure(f[i, 0], f[i, 1], f[i, 2])
        k[i, 0] = kappa
        k[i, 1] = pressure

    def prepare(fm, fp, km, kp, first, last):
        def one(i):
            prepare_row(i, fm, km)
            prepare_row(i, fp, kp)

        loop(first, last, 2, one)

    def east_of(m, p, n=0):
        return jnp.where(lane == 127, roll(p, 121 - 8 * n), roll(m, 127))

    def west_of(m, p, n=0):
        return jnp.where(lane == 0, roll(p, 127 - 8 * n), roll(m, 1))

    def apply(a, x, xe_, xw_, xn, xs):
        return ((a[0] * x + a[3] * xn) + (a[4] * xs + a[5] * roll(x, 1, 0))) + (
            a[6] * roll(x, 7, 0) + (a[1] * xe_ + a[2] * xw_)
        )

    def flow_row(i, f, k, aux, e_of, w_of, coriolis):
        u, v, h = f[i, 0], f[i, 1], f[i, 2]
        kappa, pressure = k[i, 0], k[i, 1]
        un, us = f[i + 1, 0], f[i - 1, 0]
        vn, vs = f[i + 1, 1], f[i - 1, 1]
        wet = wet_of(aux[i, 3])
        wet_e = w_e = e_of(3)
        wet_w = w_of(3)
        oe = wet * wet_e
        ow = wet * wet_w
        on = wet * wet_of(aux[i + 1, 3])
        os = wet * wet_of(aux[i - 1, 3])
        ue, uw, ve, vw = e_of(0), w_of(0), e_of(1), w_of(1)
        fe = 0.5 * (u + ue) * oe
        fw = 0.5 * (u + uw) * ow
        fn = 0.5 * (v + vn) * on
        fs = 0.5 * (v + vs) * os
        ce = 0.5 * (kappa + e_of(4)) * oe
        cw = 0.5 * (kappa + w_of(4)) * ow
        cn = 0.5 * (kappa + k[i + 1, 0]) * on
        cs = 0.5 * (kappa + k[i - 1, 0]) * os
        lap_u = oe * (ue - u) + ow * (uw - u) + on * (un - u) + os * (us - u)
        lap_v = oe * (ve - v) + ow * (vw - v) + on * (vn - v) + os * (vs - v)
        new_u = wet * (
            u + time_step * (coriolis * v - 0.5 * (e_of(5) - w_of(5)) + viscosity * lap_u)
        )
        new_v = wet * (
            v
            + time_step
            * (-coriolis * u - 0.5 * (k[i + 1, 1] - k[i - 1, 1]) + viscosity * lap_v)
        )
        div = fe - fw + fn - fs
        total = div
        for by in (1, 2, 4):
            total = total + jnp.where(level < NZ - by, roll(total, NZ - by, 0), 0.0)
        w_top = jnp.where(level >= 1, -total, 0.0)
        w_bot = jnp.where(level < NZ - 1, -roll(total, NZ - 1, 0), 0.0)
        a = (
            wet
            * (
                1.0
                - time_step * (ce + cw + cn + cs)
                - 0.5 * time_step * (div + w_top - w_bot)
            ),
            time_step * (ce - 0.5 * fe),
            time_step * (cw + 0.5 * fw),
            time_step * (cn - 0.5 * fn),
            time_step * (cs + 0.5 * fs),
            (-0.5 * time_step) * w_top * wet,
            (0.5 * time_step) * w_bot * wet,
        )
        moved = apply(a, h, e_of(2), w_of(2), f[i + 1, 2], f[i - 1, 2])
        return a, new_u, new_v, moved

    first_lat = 8 * n_row

    def coriolis_of(i):
        latitude = (16 * chip + i - 2).astype(jnp.float32)
        return coriolis_base * (2.0 * (latitude + 0.5) / first_lat - 1.0)

    def main_shift(i, fm, fp, km, kp, of):
        def one(f):
            if f == 3:
                return of(wet_of(fm0[i, 3]), wet_of(fp0[i, 3]))
            if f >= 4:
                return of(km[i, f - 4], kp[i, f - 4])
            return of(fm[i, f], fp[i, f])

        return one

    def packed_shift(i, by):
        def one(f):
            if f == 3:
                return roll(wet_of(fp0[i, 3]), by)
            if f >= 4:
                return roll(kpp[i, f - 4], by)
            return roll(fp0[i, f], by)

        return one

    def keep(i, result, a_new, f_new):
        a, u, v, h = result
        for s in range(7):
            a_new[i, s] = a[s]
        f_new[i, 0] = u
        f_new[i, 1] = v
        f_new[i, 2] = h

    def flow_main(i, fm, fp, km, kp, f_new):
        keep(
            i,
            flow_row(
                i, fm, km, fm0, main_shift(i, fm, fp, km, kp, east_of),
                main_shift(i, fm, fp, km, kp, west_of), coriolis_of(i),
            ),
            am, f_new,
        )

    def flow_packed(i):
        keep(
            i,
            flow_row(i, fp0, kpp, fp0, packed_shift(i, 127), packed_shift(i, 1), coriolis_of(i)),
            ap, fp1,
        )

    def profile_of(pigment):
        squared = pigment * pigment
        depth = water_absorb + pigment_absorb * squared / (1.0 + squared)
        above = zero
        for by in (1, 2, 3):
            above = above + jnp.where(level >= by, roll(depth, by, 0), 0.0)
        return jnp.where(
            level < KL, jnp.exp(-above) * (1.0 - jnp.exp(-depth)), 0.0
        )

    def moved_row(i, c, p, c_new, i_new, slot):
        a = [am[i, s] for s in range(7)]
        ghost = jnp.where(lane % 8 == 0, roll(p[i], -6), roll(p[i], -2))
        lanes = pl.ds(pl.multiple_of(slot * 128, 128), 128)
        for pair in range(NT // 2):
            bent = []
            for n in (2 * pair, 2 * pair + 1):
                x = c[i, n]
                g = roll(ghost, -8 * n)
                x_e = roll(jnp.where(lane == 0, g, x), 127)
                x_w = roll(jnp.where(lane == 127, g, x), 1)
                m = apply(a, x, x_e, x_w, c[i + 1, n], c[i - 1, n])
                c_new[i_new, n] = m
                bent.append(m * lax.rsqrt(1.0 + m * m))
            both = jnp.concatenate(bent, axis=0)
            high = both.astype(jnp.bfloat16)
            low = (both - high.astype(jnp.float32)).astype(jnp.bfloat16)
            sbuf[16 * pair : 16 * pair + 16, lanes] = high
            sbuf[128 + 16 * pair : 144 + 16 * pair, lanes] = low

    def react_rows(rows, slot, c_new, shift, f_new):
        part = sbuf[:, 128 * slot : 128 * slot + 256]
        coupling = jnp.dot(whi[...], part, preferred_element_type=jnp.float32) + jnp.dot(
            wlo[...], part, preferred_element_type=jnp.float32
        )
        for r, i in enumerate(rows):
            wet = wet_of(fm0[i, 3])
            scale = react_step * wet
            for n in range(NT):
                value = c_new[i - shift, n] + scale * coupling[
                    8 * n : 8 * n + 8, 128 * r : 128 * r + 128
                ]
                c_new[i - shift, n] = value
                if n == 0:
                    f_new[i, 2] = f_new[i, 2] + heat_gain * light_of(
                        fm0[i, 3]
                    ) * wet * profile_of(value)

    def step1_flow(i):
        flow_main(i, fm0, fp0, kpm, kpp, fm1)
        flow_packed(i)

    def packed_moved(i):
        x = p0[i]
        a = [ap[i, s] for s in range(7)]
        m = apply(a, x, roll(x, 127), roll(x, 1), p0[i + 1], p0[i - 1])
        p1[i] = m
        return m * lax.rsqrt(1.0 + m * m)

    def couple(x):
        return lax.dot_general(
            x, wmat[...], (((1,), (1,)), ((), ())), precision=lax.Precision.HIGHEST,
            preferred_element_type=jnp.float32,
        )

    def packed_react(i, coupling):
        wet = wet_of(fp0[i, 3])
        value = p1[i] + react_step * wet * coupling
        p1[i] = value
        fp1[i, 2] = fp1[i, 2] + heat_gain * light_of(fp0[i, 3]) * wet * profile_of(
            spread_field(value, 0)
        )

    prepare(fm0, fp0, kpm, kpp, 2, 18)
    loop(3, 17, 2, step1_flow)

    def packed_in(i):
        psat[pl.ds(pl.multiple_of(8 * (i - 3), 8), 8), :] = packed_moved(i)

    def packed_end(i):
        packed_react(i, psat[pl.ds(pl.multiple_of(8 * (i - 3), 8), 8), :])

    loop(3, 17, 7, packed_in)
    psat[...] = couple(psat[...])
    loop(3, 17, 7, packed_end)
    loop(3, 17, 2, lambda i: moved_row(i, c0, p0, c1, i, i - 3))
    for i in range(3, 17, 2):
        react_rows((i, i + 1), i - 3, c1, 0, fm1)

    @pl.when(late_s)
    def _():
        pl.semaphore_wait(ready.at[1], 1)
        for one in (near_s, rows_s, edge_s, far_s):
            one.start()

    prepare(fm1, fp1, kpm1, kpp1, 3, 17)
    loop(4, 16, 2, lambda i: flow_main(i, fm1, fp1, kpm1, kpp1, fm2))
    loop(4, 16, 2, lambda i: moved_row(i, c1, p1, c2, i - 2, i - 4))
    for i in range(4, 16, 2):
        react_rows((i, i + 1), i - 4, c2, 2, fm2)

    def finish(out, by, side):
        edge = out + by
        p0[out] = px_in[side, 0]
        for f in range(4):
            fp0[out, f] = spread_field(roll(px_in[side, 0], -1), f)
        low = min(out, out - by)
        fm0[low, 3] = px_in[side, 1]
        fm0[low + 1, 3] = roll(px_in[side, 1], -2, 0)
        prepare_row(out - by, fm0, kpm)
        prepare_row(out, fm0, kpm)
        prepare_row(out, fp0, kpp)
        flow_main(edge, fm0, fp0, kpm, kpp, fm1)
        flow_packed(edge)
        flow_main(out, fm0, fp0, kpm, kpp, fm1)
        packed_react(edge, couple(packed_moved(edge)))
        moved_row(edge, c0, p0, c1, edge, 0)
        moved_row(out, c0, p0, c1, out, 1)
        react_rows((edge, out), 0, c1, 0, fm1)
        prepare_row(edge, fm1, kpm1)
        prepare_row(edge, fp1, kpp1)
        prepare_row(out, fm1, kpm1)
        flow_main(edge + by, fm1, fp1, kpm1, kpp1, fm2)
        flow_main(edge, fm1, fp1, kpm1, kpp1, fm2)
        moved_row(edge + by, c1, p1, c2, edge + by - 2, 0)
        moved_row(edge, c1, p1, c2, edge - 2, 1)
        react_rows((edge + by, edge), 0, c2, 2, fm2)

    @pl.when(has_n)
    def _():
        for one in (near_s, far_s, rows_s, edge_s):
            one.wait_recv()

    finish(18, -1, 1)

    @pl.when(has_s)
    def _():
        for one in (near_n, far_n, rows_n, edge_n):
            one.wait_recv()

    finish(1, 1, 0)

    back = copy(fm2.at[pl.ds(10 - 8 * half, 8)], fr, 14, partner)
    back.start()
    for f in range(3):
        mine_out[:, f] = fm2[pl.ds(2 + 8 * half, 8), f]
    for one in to_partner:
        one.wait_send()
    for here, copies in (
        (has_e, (to_east,)), (has_w, (to_west,)),
        (has_n, (near_n, far_n, rows_n, edge_n)), (has_s, (near_s, far_s, rows_s, edge_s)),
    ):
        @pl.when(here)
        def _(copies=copies):
            for one in copies:
                one.wait_send()

    back.wait()
    theirs_out[...] = fr[...]


def lay_out(c2, mine, theirs, flow_out, temp_out, tr_out):
    half = lax.rem(lax.axis_index("row"), 2)

    def turn_out(n, carry):
        for t in range(2):
            tr_out[0, n, :, 8 * t : 8 * t + 8, :] = jnp.swapaxes(c2[8 * t : 8 * t + 8, n], 0, 1)
        return carry

    lax.fori_loop(0, c2.shape[1], turn_out, 0)

    @pl.when(pl.program_id(0) == 0)
    def _():
        for ref, at in ((mine, half), (theirs, 1 - half)):
            lanes = pl.ds(pl.multiple_of(at * 128, 128), 128)
            for f in range(2):
                flow_out[f, :, :, lanes] = jnp.swapaxes(ref[:, f], 0, 1)
            temp_out[:, :, lanes] = jnp.swapaxes(ref[:, 2], 0, 1)


def on_device(n_row, n_col, *args):
    f32 = jnp.float32
    vmem = pl.BlockSpec(memory_space=pltpu.VMEM)
    tile = (NZ, 128)
    c2, mine, theirs = pl.pallas_call(
        functools.partial(kernel, n_row, n_col),
        out_shape=(
            jax.ShapeDtypeStruct((16, NT) + tile, f32),
            jax.ShapeDtypeStruct((8, 3) + tile, f32),
            jax.ShapeDtypeStruct((8, 3) + tile, f32),
        ),
        in_specs=[pl.BlockSpec(memory_space=pl.ANY)] * 6,
        out_specs=(vmem, vmem, vmem),
        scratch_shapes=[
            pltpu.VMEM((20, NT) + tile, f32),
            pltpu.VMEM((20, NT) + tile, f32),
            pltpu.VMEM((20,) + tile, f32),
            pltpu.VMEM((20,) + tile, f32),
            pltpu.VMEM((112, 128), f32),
            pltpu.VMEM((20, 4) + tile, f32),
            pltpu.VMEM((20, 4) + tile, f32),
            pltpu.VMEM((20, 3) + tile, f32),
            pltpu.VMEM((20, 3) + tile, f32),
            pltpu.VMEM((20, 3) + tile, f32),
            pltpu.VMEM((20, 2) + tile, f32),
            pltpu.VMEM((20, 2) + tile, f32),
            pltpu.VMEM((20, 2) + tile, f32),
            pltpu.VMEM((20, 2) + tile, f32),
            pltpu.VMEM((20, 7) + tile, f32),
            pltpu.VMEM((20, 7) + tile, f32),
            pltpu.VMEM((128, 128), f32),
            pltpu.VMEM((128, 256), jnp.bfloat16),
            pltpu.VMEM((128, 256), jnp.bfloat16),
            pltpu.VMEM((256, 14 * 128), jnp.bfloat16),
            pltpu.VMEM((16,) + tile, f32),
            pltpu.VMEM((16,) + tile, f32),
            pltpu.VMEM((5,) + tile, f32),
            pltpu.VMEM((5,) + tile, f32),
            pltpu.VMEM((5,) + tile, f32),
            pltpu.VMEM((5,) + tile, f32),
            pltpu.VMEM((2, 2) + tile, f32),
            pltpu.VMEM((2, 2) + tile, f32),
            pltpu.VMEM((2, NZ, 8, 128), f32),
            pltpu.VMEM((NZ, 8, 128), f32),
            pltpu.VMEM((8, 128), jnp.int32),
            pltpu.VMEM((8, 128), f32),
            pltpu.VMEM((8, 3) + tile, f32),
            pltpu.VMEM((2, NZ, 8, 256), f32),
            pltpu.VMEM((NZ, 8, 256), f32),
            pltpu.VMEM((1, NT, NZ, 16, 128), f32),
            pltpu.VMEM((8, 256), jnp.int32),
            pltpu.VMEM((8, 256), f32),
            pltpu.VMEM((NT, NT), f32),
            pltpu.SemaphoreType.DMA((15,)),
            pltpu.SemaphoreType.DMA((15,)),
            pltpu.SemaphoreType.REGULAR((2,)),
            pltpu.SemaphoreType.DMA((6,)),
        ],
        compiler_params=pltpu.CompilerParams(collective_id=0, has_side_effects=True),
    )(*args)
    small = pl.BlockSpec((8, 3) + tile, lambda g: (0, 0, 0, 0))
    parts = 4
    return tuple(
        pl.pallas_call(
            lay_out,
            grid=(parts,),
            out_shape=(
                jax.ShapeDtypeStruct((2, NZ, 8, 256), f32),
                jax.ShapeDtypeStruct((NZ, 8, 256), f32),
                jax.ShapeDtypeStruct((1, NT, NZ, 16, 128), f32),
            ),
            in_specs=[pl.BlockSpec((16, NT // parts) + tile, lambda g: (0, g, 0, 0)), small, small],
            out_specs=(
                pl.BlockSpec((2, NZ, 8, 256), lambda g: (0, 0, 0, 0)),
                pl.BlockSpec((NZ, 8, 256), lambda g: (0, 0, 0)),
                pl.BlockSpec((1, NT // parts, NZ, 16, 128), lambda g: (0, g, 0, 0, 0)),
            ),
        )(c2, mine, theirs)
    )


def solution(mesh):
    in_specs = (
        P(None, None, "row", "col"),
        P(None, "row", "col"),
        P("row", None, None, None, "col"),
        P("row", "col"),
        P("row", "col"),
        P(),
    )
    out_specs = (
        P(None, None, "row", "col"),
        P(None, "row", "col"),
        P("row", None, None, None, "col"),
    )
    return jax.shard_map(
        functools.partial(on_device, mesh.shape["row"], mesh.shape["col"]),
        mesh=mesh, in_specs=in_specs, out_specs=out_specs, check_vma=False,
    )
```

```python
import functools

import jax
import jax.numpy as jnp
from jax import lax
from jax.experimental import pallas as pl
from jax.experimental.pallas import tpu as pltpu
from jax.sharding import PartitionSpec as P

MESH = pl.DeviceIdType.MESH
NT = 16
NZ = 8
KL = 4
PERIOD = 4

time_step = 0.2
viscosity = 0.2
expansion = 0.05
coriolis_base = 0.5
kappa_base = 0.05
kappa_shear = 0.2
react_step = 0.25
water_absorb = 0.1
pigment_absorb = 0.6
heat_gain = 1.0


def kernel(
    n_row, n_col,
    flow_h, temp_h, tr_h, bot_h, sun_h, rates_h,
    c2, mine_out, theirs_out,
    c0, c1, p0, p1, psat, fm0, fp0, fm1, fp1, fm2, kpm, kpp, kpm1, kpp1, am, ap, wmat, whi, wlo, sbuf,
    xo, xf, te, tw, xw, xe, px_out, px_in, pf, pt, pb, ps, fr,
    flow, temp, tr, bot, sun, rates,
    send, recv, ready, load,
):
    loads = [
        pltpu.make_async_copy(src, dst, load.at[k])
        for k, (src, dst) in enumerate(
            ((tr_h, tr), (flow_h, flow), (temp_h, temp), (bot_h, bot), (sun_h, sun), (rates_h, rates))
        )
    ]
    for one in loads:
        one.start()

    row = lax.axis_index("row")
    col = lax.axis_index("col")
    half = lax.rem(row, 2)
    chip = row // 2
    other = 2 * chip + 1 - half
    west_col = col - 1 + half
    east_col = col + half
    has_w = west_col >= 0
    has_e = east_col < n_col
    has_n = row + 2 < n_row
    has_s = row >= 2
    partner = (other, col)
    west = (other, west_col)
    east = (other, east_col)
    north = (row + 2, col)
    south = (row - 2, col)
    place = lax.rem(chip, PERIOD)
    late_n = has_n & (place != PERIOD - 1)
    late_s = has_s & (place == 0)
    soon_n = has_n & (place == PERIOD - 1)
    soon_s = has_s & (place != 0)

    barrier = pltpu.get_barrier_semaphore()
    for tells, target in ((has_e, east), (has_w, west), (late_n, north), (late_s, south)):
        @pl.when(tells)
        def _(target=target):
            pl.semaphore_signal(barrier, inc=1, device_id=target, device_id_type=MESH)

    count = jnp.int32(0)
    for waits in (has_e, has_w, soon_n, soon_s):
        count = count + waits.astype(jnp.int32)

    lane = lax.broadcasted_iota(jnp.int32, (NZ, 128), 1)
    level = lax.broadcasted_iota(jnp.int32, (NZ, 128), 0)
    level_f = level.astype(jnp.float32)
    group = lax.rem(lane, 8)
    zero = jnp.zeros((NZ, 128), jnp.float32)

    def roll(x, by, axis=1):
        by = by % x.shape[axis]
        return pltpu.roll(x, by, axis) if by else x

    def loop(first, last, by, body):
        def several(k, carry):
            for r in range(by):
                body(first + k * by + r)
            return carry

        assert (last - first) % by == 0
        lax.fori_loop(0, (last - first) // by, several, 0)

    def turn_in(n, carry):
        for t in range(2):
            c0[pl.ds(2 + 8 * t, 8), n] = jnp.swapaxes(tr[0, n, :, 8 * t : 8 * t + 8, :], 0, 1)
        return carry

    loads[0].wait()
    lax.fori_loop(0, NT, turn_in, 0)
    for one in loads[1:]:
        one.wait()

    def copy(src, dst, k, target):
        return pltpu.make_async_remote_copy(
            src_ref=src, dst_ref=dst, send_sem=send.at[k], recv_sem=recv.at[k],
            device_id=target, device_id_type=MESH,
        )

    own_half = pl.ds(pl.multiple_of(half * 128, 128), 128)
    other_half = pl.ds(pl.multiple_of((1 - half) * 128, 128), 128)
    to_partner = (
        copy(flow.at[:, :, :, other_half], pf, 0, partner),
        copy(temp.at[:, :, other_half], pt, 1, partner),
        copy(bot.at[:, other_half], pb, 2, partner),
        copy(sun.at[:, other_half], ps, 3, partner),
    )
    to_east = copy(te, xw, 4, east)
    to_west = copy(tw, xe, 5, west)
    near_n = copy(c0.at[17], c0.at[1], 6, north)
    near_s = copy(c0.at[2], c0.at[18], 7, south)
    far_n = copy(c0.at[16], c0.at[0], 8, north)
    far_s = copy(c0.at[3], c0.at[19], 9, south)
    rows_n = copy(fm0.at[pl.ds(16, 2)], fm0.at[pl.ds(0, 2)], 10, north)
    rows_s = copy(fm0.at[pl.ds(2, 2)], fm0.at[pl.ds(18, 2)], 11, south)
    edge_n = copy(px_out.at[1], px_in.at[0], 12, north)
    edge_s = copy(px_out.at[0], px_in.at[1], 13, south)

    def start(here, *copies):
        @pl.when(here)
        def _():
            for one in copies:
                one.start()

    for here, ref, at, length in (
        (has_s, c0, 0, 2), (has_n, c0, 18, 2), (has_s, fm0, 0, 2), (has_n, fm0, 18, 2),
        (has_w, xw, 0, 5), (has_e, xe, 0, 5), (has_s, px_in, 0, 1), (has_n, px_in, 1, 1),
    ):
        @pl.when(jnp.logical_not(here))
        def _(ref=ref, at=at, length=length):
            def clear(r, carry):
                ref[at + r] = jnp.zeros(ref.shape[1:], jnp.float32)
                return carry

            lax.fori_loop(0, length, clear, 0)

    pl.semaphore_wait(barrier, count)
    for one in to_partner:
        one.start()
    for here, target, k in ((soon_s, south, 0), (soon_n, north, 1)):
        @pl.when(here)
        def _(target=target, k=k):
            pl.semaphore_signal(ready.at[k], inc=1, device_id=target, device_id_type=MESH)

    start(soon_n, near_n)
    start(soon_s, near_s)

    spread = (
        lax.broadcasted_iota(jnp.int32, (128, NT), 0) // 8
        == lax.broadcasted_iota(jnp.int32, (128, NT), 1)
    ).astype(jnp.float32)
    tall = jnp.dot(
        spread, rates[...], precision=lax.Precision.HIGHEST, preferred_element_type=jnp.float32
    )
    square = lax.dot_general(
        tall, spread, (((1,), (1,)), ((), ())), precision=lax.Precision.HIGHEST,
        preferred_element_type=jnp.float32,
    )
    same = lax.rem(lax.broadcasted_iota(jnp.int32, (128, 128), 0), 8) == lax.rem(
        lax.broadcasted_iota(jnp.int32, (128, 128), 1), 8
    )
    whole = jnp.where(same, square, 0.0)
    wmat[...] = whole
    upper = whole.astype(jnp.bfloat16)
    lower = (whole - upper.astype(jnp.float32)).astype(jnp.bfloat16)
    for at in (0, 128):
        whi[:, at : at + 128] = upper
        wlo[:, at : at + 128] = lower

    def fill(first, field_u, field_v, field_h, field_b, field_s):
        for r in range(8):
            base = field_b[r : r + 1, :].astype(jnp.float32)
            wet = (level_f < jnp.broadcast_to(base, (NZ, 128))).astype(jnp.float32)
            i = first + r
            fm0[i, 0] = field_u[r] * wet
            fm0[i, 1] = field_v[r] * wet
            fm0[i, 2] = field_h[r] * wet
            light = jnp.broadcast_to(field_s[r : r + 1, :], (NZ, 128))
            fm0[i, 3] = jnp.where(level == 0, jnp.broadcast_to(base, (NZ, 128)), light)

    def turn(x):
        return jnp.swapaxes(x, 0, 1)

    fill(
        2 + 8 * half,
        turn(flow[0, :, :, own_half]), turn(flow[1, :, :, own_half]), turn(temp[:, :, own_half]),
        bot[:, own_half], sun[:, own_half],
    )
    for one in to_partner:
        one.wait_recv()
    fill(10 - 8 * half, turn(pf[0]), turn(pf[1]), turn(pt[...]), pb[...], ps[...])

    def pack(j):
        i = j + 2
        acc = zero
        for n in range(NT):
            x = c0[i, n]
            acc = jnp.where((lane // 2) == (8 * n + 2) // 2, roll(x, 8 * n + 2), acc)
            acc = jnp.where((lane // 2) == (8 * n + 4) // 2, roll(x, 8 * n + 6), acc)
        xo[j] = acc
        acc = zero
        for f in range(4):
            x = fm0[i, f]
            acc = jnp.where((lane // 2) == (8 * f + 2) // 2, roll(x, 8 * f + 2), acc)
            acc = jnp.where((lane // 2) == (8 * f + 4) // 2, roll(x, 8 * f + 6), acc)
        xf[j] = acc

    loop(0, 16, 2, pack)

    for tile_of, first in ((te, 4), (tw, 2)):
        fields = zero
        for q in range(4):
            tracers = zero
            for r in range(4):
                here = group // 2 == r
                tracers = jnp.where(here, roll(xo[4 * q + r], 2 * r - first), tracers)
                fields = jnp.where(
                    here & (lane // 32 == q), roll(xf[4 * q + r], 32 * q + 2 * r - first), fields
                )
            tile_of[q] = tracers
        tile_of[4] = fields
    start(has_e, to_east)
    start(has_w, to_west)
    start(soon_n, rows_n, far_n)
    start(soon_s, rows_s)

    @pl.when(has_w)
    def _():
        to_east.wait_recv()

    @pl.when(has_e)
    def _():
        to_west.wait_recv()

    def spread_field(x, f):
        y = jnp.where(lane < 8, roll(x, -8 * f), 0.0)
        for by in (8, 16, 32, 64):
            y = y + roll(y, by)
        return y

    def sides(own, w, e, by_w, by_e):
        return jnp.where(group < 2, roll(w, by_w), jnp.where(group >= 6, roll(e, by_e), own))

    def fields_of(j):
        by = 32 * (j // 4) + 2 * (j % 4)
        return sides(xf[j], xw[4], xe[4], -by, 6 - by)

    for j in range(16):
        q, by = j // 4, 2 * (j % 4)
        p0[j + 2] = sides(xo[j], xw[q], xe[q], -by, 6 - by)
        fields = fields_of(j)
        for f in range(4):
            fp0[j + 2, f] = spread_field(fields, f)
    for side, j in ((0, 0), (1, 15)):
        px_out[side, 0] = p0[j + 2]
        px_out[side, 1] = fields_of(j)
    start(soon_n, edge_n)
    start(soon_s, edge_s, far_s)

    @pl.when(late_n)
    def _():
        pl.semaphore_wait(ready.at[0], 1)
        for one in (near_n, rows_n, edge_n, far_n):
            one.start()

    def wet_of(aux):
        return (level_f < jnp.broadcast_to(aux[0:1, :], (NZ, 128))).astype(jnp.float32)

    def light_of(aux):
        return jnp.broadcast_to(aux[1:2, :], (NZ, 128))

    def shear_pressure(u, v, h):
        du = u - roll(u, 7, 0)
        dv = v - roll(v, 7, 0)
        q = jnp.where(level < NZ - 1, du * du + dv * dv, 0.0)
        kappa = kappa_base + kappa_shear * q / (1.0 + q)
        total = h
        for by in (1, 2, 4):
            total = total + jnp.where(level >= by, roll(total, by, 0), 0.0)
        return kappa, -expansion * total

    def prepare_row(i, f, k):
        kappa, pressure = shear_pressure(f[i, 0], f[i, 1], f[i, 2])
        k[i, 0] = kappa
        k[i, 1] = pressure

    def prepare(fm, fp, km, kp, first, last):
        def one(i):
            prepare_row(i, fm, km)
            prepare_row(i, fp, kp)

        loop(first, last, 2, one)

    def east_of(m, p, n=0):
        return jnp.where(lane == 127, roll(p, 121 - 8 * n), roll(m, 127))

    def west_of(m, p, n=0):
        return jnp.where(lane == 0, roll(p, 127 - 8 * n), roll(m, 1))

    def apply(a, x, xe_, xw_, xn, xs):
        return ((a[0] * x + a[3] * xn) + (a[4] * xs + a[5] * roll(x, 1, 0))) + (
            a[6] * roll(x, 7, 0) + (a[1] * xe_ + a[2] * xw_)
        )

    def flow_row(i, f, k, aux, e_of, w_of, coriolis):
        u, v, h = f[i, 0], f[i, 1], f[i, 2]
        kappa, pressure = k[i, 0], k[i, 1]
        un, us = f[i + 1, 0], f[i - 1, 0]
        vn, vs = f[i + 1, 1], f[i - 1, 1]
        wet = wet_of(aux[i, 3])
        wet_e = w_e = e_of(3)
        wet_w = w_of(3)
        oe = wet * wet_e
        ow = wet * wet_w
        on = wet * wet_of(aux[i + 1, 3])
        os = wet * wet_of(aux[i - 1, 3])
        ue, uw, ve, vw = e_of(0), w_of(0), e_of(1), w_of(1)
        fe = 0.5 * (u + ue) * oe
        fw = 0.5 * (u + uw) * ow
        fn = 0.5 * (v + vn) * on
        fs = 0.5 * (v + vs) * os
        ce = 0.5 * (kappa + e_of(4)) * oe
        cw = 0.5 * (kappa + w_of(4)) * ow
        cn = 0.5 * (kappa + k[i + 1, 0]) * on
        cs = 0.5 * (kappa + k[i - 1, 0]) * os
        lap_u = oe * (ue - u) + ow * (uw - u) + on * (un - u) + os * (us - u)
        lap_v = oe * (ve - v) + ow * (vw - v) + on * (vn - v) + os * (vs - v)
        new_u = wet * (
            u + time_step * (coriolis * v - 0.5 * (e_of(5) - w_of(5)) + viscosity * lap_u)
        )
        new_v = wet * (
            v
            + time_step
            * (-coriolis * u - 0.5 * (k[i + 1, 1] - k[i - 1, 1]) + viscosity * lap_v)
        )
        div = fe - fw + fn - fs
        total = div
        for by in (1, 2, 4):
            total = total + jnp.where(level < NZ - by, roll(total, NZ - by, 0), 0.0)
        w_top = jnp.where(level >= 1, -total, 0.0)
        w_bot = jnp.where(level < NZ - 1, -roll(total, NZ - 1, 0), 0.0)
        a = (
            wet
            * (
                1.0
                - time_step * (ce + cw + cn + cs)
                - 0.5 * time_step * (div + w_top - w_bot)
            ),
            time_step * (ce - 0.5 * fe),
            time_step * (cw + 0.5 * fw),
            time_step * (cn - 0.5 * fn),
            time_step * (cs + 0.5 * fs),
            (-0.5 * time_step) * w_top * wet,
            (0.5 * time_step) * w_bot * wet,
        )
        moved = apply(a, h, e_of(2), w_of(2), f[i + 1, 2], f[i - 1, 2])
        return a, new_u, new_v, moved

    first_lat = 8 * n_row

    def coriolis_of(i):
        latitude = (16 * chip + i - 2).astype(jnp.float32)
        return coriolis_base * (2.0 * (latitude + 0.5) / first_lat - 1.0)

    def main_shift(i, fm, fp, km, kp, of):
        def one(f):
            if f == 3:
                return of(wet_of(fm0[i, 3]), wet_of(fp0[i, 3]))
            if f >= 4:
                return of(km[i, f - 4], kp[i, f - 4])
            return of(fm[i, f], fp[i, f])

        return one

    def packed_shift(i, by):
        def one(f):
            if f == 3:
                return roll(wet_of(fp0[i, 3]), by)
            if f >= 4:
                return roll(kpp[i, f - 4], by)
            return roll(fp0[i, f], by)

        return one

    def keep(i, result, a_new, f_new):
        a, u, v, h = result
        for s in range(7):
            a_new[i, s] = a[s]
        f_new[i, 0] = u
        f_new[i, 1] = v
        f_new[i, 2] = h

    def flow_main(i, fm, fp, km, kp, f_new):
        keep(
            i,
            flow_row(
                i, fm, km, fm0, main_shift(i, fm, fp, km, kp, east_of),
                main_shift(i, fm, fp, km, kp, west_of), coriolis_of(i),
            ),
            am, f_new,
        )

    def flow_packed(i):
        keep(
            i,
            flow_row(i, fp0, kpp, fp0, packed_shift(i, 127), packed_shift(i, 1), coriolis_of(i)),
            ap, fp1,
        )

    def profile_of(pigment):
        squared = pigment * pigment
        depth = water_absorb + pigment_absorb * squared / (1.0 + squared)
        above = zero
        for by in (1, 2, 3):
            above = above + jnp.where(level >= by, roll(depth, by, 0), 0.0)
        return jnp.where(
            level < KL, jnp.exp(-above) * (1.0 - jnp.exp(-depth)), 0.0
        )

    def moved_row(i, c, p, c_new, i_new, slot):
        a = [am[i, s] for s in range(7)]
        ghost = jnp.where(lane % 8 == 0, roll(p[i], -6), roll(p[i], -2))
        lanes = pl.ds(pl.multiple_of(slot * 128, 128), 128)
        for pair in range(NT // 2):
            bent = []
            for n in (2 * pair, 2 * pair + 1):
                x = c[i, n]
                g = roll(ghost, -8 * n)
                x_e = roll(jnp.where(lane == 0, g, x), 127)
                x_w = roll(jnp.where(lane == 127, g, x), 1)
                m = apply(a, x, x_e, x_w, c[i + 1, n], c[i - 1, n])
                c_new[i_new, n] = m
                bent.append(m * lax.rsqrt(1.0 + m * m))
            both = jnp.concatenate(bent, axis=0)
            high = both.astype(jnp.bfloat16)
            low = (both - high.astype(jnp.float32)).astype(jnp.bfloat16)
            sbuf[16 * pair : 16 * pair + 16, lanes] = high
            sbuf[128 + 16 * pair : 144 + 16 * pair, lanes] = low

    def react_rows(rows, slot, c_new, shift, f_new):
        part = sbuf[:, 128 * slot : 128 * (slot + len(rows))]
        coupling = jnp.dot(whi[...], part, preferred_element_type=jnp.float32) + jnp.dot(
            wlo[...], part, preferred_element_type=jnp.float32
        )
        for r, i in enumerate(rows):
            wet = wet_of(fm0[i, 3])
            scale = react_step * wet
            for n in range(NT):
                value = c_new[i - shift, n] + scale * coupling[
                    8 * n : 8 * n + 8, 128 * r : 128 * r + 128
                ]
                c_new[i - shift, n] = value
                if n == 0:
                    f_new[i, 2] = f_new[i, 2] + heat_gain * light_of(
                        fm0[i, 3]
                    ) * wet * profile_of(value)

    def step1_flow(i):
        flow_main(i, fm0, fp0, kpm, kpp, fm1)
        flow_packed(i)

    def packed_moved(i):
        x = p0[i]
        a = [ap[i, s] for s in range(7)]
        m = apply(a, x, roll(x, 127), roll(x, 1), p0[i + 1], p0[i - 1])
        p1[i] = m
        return m * lax.rsqrt(1.0 + m * m)

    def couple(x):
        return lax.dot_general(
            x, wmat[...], (((1,), (1,)), ((), ())), precision=lax.Precision.HIGHEST,
            preferred_element_type=jnp.float32,
        )

    def packed_react(i, coupling):
        wet = wet_of(fp0[i, 3])
        value = p1[i] + react_step * wet * coupling
        p1[i] = value
        fp1[i, 2] = fp1[i, 2] + heat_gain * light_of(fp0[i, 3]) * wet * profile_of(
            spread_field(value, 0)
        )

    prepare(fm0, fp0, kpm, kpp, 2, 18)
    loop(3, 17, 2, step1_flow)

    def packed_in(i):
        psat[pl.ds(pl.multiple_of(8 * (i - 3), 8), 8), :] = packed_moved(i)

    def packed_end(i):
        packed_react(i, psat[pl.ds(pl.multiple_of(8 * (i - 3), 8), 8), :])

    loop(3, 17, 7, packed_in)
    psat[...] = couple(psat[...])
    loop(3, 17, 7, packed_end)
    loop(3, 17, 2, lambda i: moved_row(i, c0, p0, c1, i, i - 3))
    for i in range(3, 17, 2):
        react_rows((i, i + 1), i - 3, c1, 0, fm1)

    @pl.when(late_s)
    def _():
        pl.semaphore_wait(ready.at[1], 1)
        for one in (near_s, rows_s, edge_s, far_s):
            one.start()

    prepare(fm1, fp1, kpm1, kpp1, 3, 17)
    loop(4, 16, 2, lambda i: flow_main(i, fm1, fp1, kpm1, kpp1, fm2))
    loop(4, 16, 2, lambda i: moved_row(i, c1, p1, c2, i - 2, i - 4))
    for i in range(4, 16, 2):
        react_rows((i, i + 1), i - 4, c2, 2, fm2)

    def finish_near(out, by):
        edge = out + by
        prepare_row(out, fm0, kpm)
        flow_main(edge, fm0, fp0, kpm, kpp, fm1)
        moved_row(edge, c0, p0, c1, edge, 0)
        react_rows((edge,), 0, c1, 0, fm1)
        prepare_row(edge, fm1, kpm1)
        flow_main(edge + by, fm1, fp1, kpm1, kpp1, fm2)
        moved_row(edge + by, c1, p1, c2, edge + by - 2, 1)
        react_rows((edge + by,), 1, c2, 2, fm2)

    def finish_far(out, by, side):
        edge = out + by
        p0[out] = px_in[side, 0]
        for f in range(4):
            fp0[out, f] = spread_field(px_in[side, 1], f)
        prepare_row(out - by, fm0, kpm)
        prepare_row(out, fp0, kpp)
        flow_packed(edge)
        flow_main(out, fm0, fp0, kpm, kpp, fm1)
        packed_react(edge, couple(packed_moved(edge)))
        moved_row(out, c0, p0, c1, out, 2)
        react_rows((out,), 2, c1, 0, fm1)
        prepare_row(edge, fp1, kpp1)
        prepare_row(out, fm1, kpm1)
        flow_main(edge, fm1, fp1, kpm1, kpp1, fm2)
        moved_row(edge, c1, p1, c2, edge - 2, 3)
        react_rows((edge,), 3, c2, 2, fm2)

    def arrive(here, *copies):
        @pl.when(here)
        def _():
            for one in copies:
                one.wait_recv()

    arrive(has_n, near_s, rows_s)
    finish_near(18, -1)
    arrive(has_n, far_s, edge_s)
    finish_far(18, -1, 1)
    arrive(has_s, near_n, rows_n)
    finish_near(1, 1)
    arrive(has_s, far_n, edge_n)
    finish_far(1, 1, 0)

    back = copy(fm2.at[pl.ds(10 - 8 * half, 8)], fr, 14, partner)
    back.start()
    for f in range(3):
        mine_out[:, f] = fm2[pl.ds(2 + 8 * half, 8), f]
    for one in to_partner:
        one.wait_send()
    for here, copies in (
        (has_e, (to_east,)), (has_w, (to_west,)),
        (has_n, (near_n, far_n, rows_n, edge_n)), (has_s, (near_s, far_s, rows_s, edge_s)),
    ):
        @pl.when(here)
        def _(copies=copies):
            for one in copies:
                one.wait_send()

    back.wait()
    theirs_out[...] = fr[...]


def lay_out(c2, mine, theirs, flow_out, temp_out, tr_out):
    half = lax.rem(lax.axis_index("row"), 2)

    def turn_out(n, carry):
        for t in range(2):
            tr_out[0, n, :, 8 * t : 8 * t + 8, :] = jnp.swapaxes(c2[8 * t : 8 * t + 8, n], 0, 1)
        return carry

    lax.fori_loop(0, c2.shape[1], turn_out, 0)

    @pl.when(pl.program_id(0) == 0)
    def _():
        for ref, at in ((mine, half), (theirs, 1 - half)):
            lanes = pl.ds(pl.multiple_of(at * 128, 128), 128)
            for f in range(2):
                flow_out[f, :, :, lanes] = jnp.swapaxes(ref[:, f], 0, 1)
            temp_out[:, :, lanes] = jnp.swapaxes(ref[:, 2], 0, 1)


def on_device(n_row, n_col, *args):
    f32 = jnp.float32
    vmem = pl.BlockSpec(memory_space=pltpu.VMEM)
    tile = (NZ, 128)
    c2, mine, theirs = pl.pallas_call(
        functools.partial(kernel, n_row, n_col),
        out_shape=(
            jax.ShapeDtypeStruct((16, NT) + tile, f32),
            jax.ShapeDtypeStruct((8, 3) + tile, f32),
            jax.ShapeDtypeStruct((8, 3) + tile, f32),
        ),
        in_specs=[pl.BlockSpec(memory_space=pl.ANY)] * 6,
        out_specs=(vmem, vmem, vmem),
        scratch_shapes=[
            pltpu.VMEM((20, NT) + tile, f32),
            pltpu.VMEM((20, NT) + tile, f32),
            pltpu.VMEM((20,) + tile, f32),
            pltpu.VMEM((20,) + tile, f32),
            pltpu.VMEM((112, 128), f32),
            pltpu.VMEM((20, 4) + tile, f32),
            pltpu.VMEM((20, 4) + tile, f32),
            pltpu.VMEM((20, 3) + tile, f32),
            pltpu.VMEM((20, 3) + tile, f32),
            pltpu.VMEM((20, 3) + tile, f32),
            pltpu.VMEM((20, 2) + tile, f32),
            pltpu.VMEM((20, 2) + tile, f32),
            pltpu.VMEM((20, 2) + tile, f32),
            pltpu.VMEM((20, 2) + tile, f32),
            pltpu.VMEM((20, 7) + tile, f32),
            pltpu.VMEM((20, 7) + tile, f32),
            pltpu.VMEM((128, 128), f32),
            pltpu.VMEM((128, 256), jnp.bfloat16),
            pltpu.VMEM((128, 256), jnp.bfloat16),
            pltpu.VMEM((256, 14 * 128), jnp.bfloat16),
            pltpu.VMEM((16,) + tile, f32),
            pltpu.VMEM((16,) + tile, f32),
            pltpu.VMEM((5,) + tile, f32),
            pltpu.VMEM((5,) + tile, f32),
            pltpu.VMEM((5,) + tile, f32),
            pltpu.VMEM((5,) + tile, f32),
            pltpu.VMEM((2, 2) + tile, f32),
            pltpu.VMEM((2, 2) + tile, f32),
            pltpu.VMEM((2, NZ, 8, 128), f32),
            pltpu.VMEM((NZ, 8, 128), f32),
            pltpu.VMEM((8, 128), jnp.int32),
            pltpu.VMEM((8, 128), f32),
            pltpu.VMEM((8, 3) + tile, f32),
            pltpu.VMEM((2, NZ, 8, 256), f32),
            pltpu.VMEM((NZ, 8, 256), f32),
            pltpu.VMEM((1, NT, NZ, 16, 128), f32),
            pltpu.VMEM((8, 256), jnp.int32),
            pltpu.VMEM((8, 256), f32),
            pltpu.VMEM((NT, NT), f32),
            pltpu.SemaphoreType.DMA((15,)),
            pltpu.SemaphoreType.DMA((15,)),
            pltpu.SemaphoreType.REGULAR((2,)),
            pltpu.SemaphoreType.DMA((6,)),
        ],
        compiler_params=pltpu.CompilerParams(collective_id=0, has_side_effects=True),
    )(*args)
    small = pl.BlockSpec((8, 3) + tile, lambda g: (0, 0, 0, 0))
    parts = 1
    return tuple(
        pl.pallas_call(
            lay_out,
            grid=(parts,),
            out_shape=(
                jax.ShapeDtypeStruct((2, NZ, 8, 256), f32),
                jax.ShapeDtypeStruct((NZ, 8, 256), f32),
                jax.ShapeDtypeStruct((1, NT, NZ, 16, 128), f32),
            ),
            in_specs=[pl.BlockSpec((16, NT // parts) + tile, lambda g: (0, g, 0, 0)), small, small],
            out_specs=(
                pl.BlockSpec((2, NZ, 8, 256), lambda g: (0, 0, 0, 0)),
                pl.BlockSpec((NZ, 8, 256), lambda g: (0, 0, 0)),
                pl.BlockSpec((1, NT // parts, NZ, 16, 128), lambda g: (0, g, 0, 0, 0)),
            ),
        )(c2, mine, theirs)
    )


def solution(mesh):
    in_specs = (
        P(None, None, "row", "col"),
        P(None, "row", "col"),
        P("row", None, None, None, "col"),
        P("row", "col"),
        P("row", "col"),
        P(),
    )
    out_specs = (
        P(None, None, "row", "col"),
        P(None, "row", "col"),
        P("row", None, None, None, "col"),
    )
    return jax.shard_map(
        functools.partial(on_device, mesh.shape["row"], mesh.shape["col"]),
        mesh=mesh, in_specs=in_specs, out_specs=out_specs, check_vma=False,
    )
```

```python
import functools

import jax
import jax.numpy as jnp
from jax import lax
from jax.experimental import pallas as pl
from jax.experimental.pallas import tpu as pltpu
from jax.sharding import PartitionSpec as P

MESH = pl.DeviceIdType.MESH
NT = 16
NZ = 8
KL = 4
PERIOD = 4
RUN = 4

time_step = 0.2
viscosity = 0.2
expansion = 0.05
coriolis_base = 0.5
kappa_base = 0.05
kappa_shear = 0.2
react_step = 0.25
water_absorb = 0.1
pigment_absorb = 0.6
heat_gain = 1.0


def kernel(
    n_row, n_col,
    flow_h, temp_h, tr_h, bot_h, sun_h, rates_h,
    c2, mine_out, theirs_out,
    c0, c1, p0, p1, psat, fm0, fp0, fm1, fp1, fm2, kpm, kpp, kpm1, kpp1, am, ap, wmat, whi, wlo, sbuf,
    xo, xf, te, tw, xw, xe, px_out, px_in, pf, pt, pb, ps, fr,
    flow, temp, tr, bot, sun, rates,
    send, recv, ready, load,
):
    loads = [
        pltpu.make_async_copy(src, dst, load.at[k])
        for k, (src, dst) in enumerate(
            ((tr_h, tr), (flow_h, flow), (temp_h, temp), (bot_h, bot), (sun_h, sun), (rates_h, rates))
        )
    ]
    for one in loads:
        one.start()

    row = lax.axis_index("row")
    col = lax.axis_index("col")
    half = lax.rem(row, 2)
    chip = row // 2
    other = 2 * chip + 1 - half
    west_col = col - 1 + half
    east_col = col + half
    has_w = west_col >= 0
    has_e = east_col < n_col
    has_n = row + 2 < n_row
    has_s = row >= 2
    partner = (other, col)
    west = (other, west_col)
    east = (other, east_col)
    north = (row + 2, col)
    south = (row - 2, col)
    place = lax.rem(chip, PERIOD)
    late_n = has_n & (place != PERIOD - 1)
    late_s = has_s & (place == 0)
    soon_n = has_n & (place == PERIOD - 1)
    soon_s = has_s & (place != 0)
    wrap_w = has_w & (half == 0) & (lax.rem(col, RUN) == 0)
    wrap_e = has_e & (half == 1) & (lax.rem(col, RUN) == RUN - 1)

    barrier = pltpu.get_barrier_semaphore()
    for tells, target in (
        (has_e & jnp.logical_not(wrap_e), east), (has_w, west), (late_n, north), (late_s, south)
    ):
        @pl.when(tells)
        def _(target=target):
            pl.semaphore_signal(barrier, inc=1, device_id=target, device_id_type=MESH)

    count = jnp.int32(0)
    for waits in (has_e, has_w & jnp.logical_not(wrap_w), soon_n, soon_s):
        count = count + waits.astype(jnp.int32)

    lane = lax.broadcasted_iota(jnp.int32, (NZ, 128), 1)
    level = lax.broadcasted_iota(jnp.int32, (NZ, 128), 0)
    level_f = level.astype(jnp.float32)
    group = lax.rem(lane, 8)
    zero = jnp.zeros((NZ, 128), jnp.float32)

    def roll(x, by, axis=1):
        by = by % x.shape[axis]
        return pltpu.roll(x, by, axis) if by else x

    def loop(first, last, by, body):
        def several(k, carry):
            for r in range(by):
                body(first + k * by + r)
            return carry

        assert (last - first) % by == 0
        lax.fori_loop(0, (last - first) // by, several, 0)

    def turn_in(n, carry):
        for t in range(2):
            c0[pl.ds(2 + 8 * t, 8), n] = jnp.swapaxes(tr[0, n, :, 8 * t : 8 * t + 8, :], 0, 1)
        return carry

    loads[0].wait()
    lax.fori_loop(0, NT, turn_in, 0)
    for one in loads[1:]:
        one.wait()

    def copy(src, dst, k, target):
        return pltpu.make_async_remote_copy(
            src_ref=src, dst_ref=dst, send_sem=send.at[k], recv_sem=recv.at[k],
            device_id=target, device_id_type=MESH,
        )

    own_half = pl.ds(pl.multiple_of(half * 128, 128), 128)
    other_half = pl.ds(pl.multiple_of((1 - half) * 128, 128), 128)
    to_partner = (
        copy(flow.at[:, :, :, other_half], pf, 0, partner),
        copy(temp.at[:, :, other_half], pt, 1, partner),
        copy(bot.at[:, other_half], pb, 2, partner),
        copy(sun.at[:, other_half], ps, 3, partner),
    )
    to_east = copy(te, xw, 4, east)
    to_west = copy(tw, xe, 5, west)
    near_n = copy(c0.at[17], c0.at[1], 6, north)
    near_s = copy(c0.at[2], c0.at[18], 7, south)
    far_n = copy(c0.at[16], c0.at[0], 8, north)
    far_s = copy(c0.at[3], c0.at[19], 9, south)
    rows_n = copy(fm0.at[pl.ds(16, 2)], fm0.at[pl.ds(0, 2)], 10, north)
    rows_s = copy(fm0.at[pl.ds(2, 2)], fm0.at[pl.ds(18, 2)], 11, south)
    edge_n = copy(px_out.at[1], px_in.at[0], 12, north)
    edge_s = copy(px_out.at[0], px_in.at[1], 13, south)

    def start(here, *copies):
        @pl.when(here)
        def _():
            for one in copies:
                one.start()

    for here, ref, at, length in (
        (has_s, c0, 0, 2), (has_n, c0, 18, 2), (has_s, fm0, 0, 2), (has_n, fm0, 18, 2),
        (has_w, xw, 0, 5), (has_e, xe, 0, 5), (has_s, px_in, 0, 1), (has_n, px_in, 1, 1),
    ):
        @pl.when(jnp.logical_not(here))
        def _(ref=ref, at=at, length=length):
            def clear(r, carry):
                ref[at + r] = jnp.zeros(ref.shape[1:], jnp.float32)
                return carry

            lax.fori_loop(0, length, clear, 0)

    pl.semaphore_wait(barrier, count)
    for one in to_partner:
        one.start()
    for here, target, k in ((soon_s, south, 0), (soon_n, north, 1), (wrap_e, east, 2)):
        @pl.when(here)
        def _(target=target, k=k):
            pl.semaphore_signal(ready.at[k], inc=1, device_id=target, device_id_type=MESH)

    start(soon_n, near_n, far_n)
    start(soon_s, near_s)

    spread = (
        lax.broadcasted_iota(jnp.int32, (128, NT), 0) // 8
        == lax.broadcasted_iota(jnp.int32, (128, NT), 1)
    ).astype(jnp.float32)
    tall = jnp.dot(
        spread, rates[...], precision=lax.Precision.HIGHEST, preferred_element_type=jnp.float32
    )
    square = lax.dot_general(
        tall, spread, (((1,), (1,)), ((), ())), precision=lax.Precision.HIGHEST,
        preferred_element_type=jnp.float32,
    )
    same = lax.rem(lax.broadcasted_iota(jnp.int32, (128, 128), 0), 8) == lax.rem(
        lax.broadcasted_iota(jnp.int32, (128, 128), 1), 8
    )
    whole = jnp.where(same, square, 0.0)
    wmat[...] = whole
    upper = whole.astype(jnp.bfloat16)
    lower = (whole - upper.astype(jnp.float32)).astype(jnp.bfloat16)
    for at in (0, 128):
        whi[:, at : at + 128] = upper
        wlo[:, at : at + 128] = lower

    def fill(first, field_u, field_v, field_h, field_b, field_s):
        for r in range(8):
            base = field_b[r : r + 1, :].astype(jnp.float32)
            wet = (level_f < jnp.broadcast_to(base, (NZ, 128))).astype(jnp.float32)
            i = first + r
            fm0[i, 0] = field_u[r] * wet
            fm0[i, 1] = field_v[r] * wet
            fm0[i, 2] = field_h[r] * wet
            light = jnp.broadcast_to(field_s[r : r + 1, :], (NZ, 128))
            fm0[i, 3] = jnp.where(level == 0, jnp.broadcast_to(base, (NZ, 128)), light)

    def turn(x):
        return jnp.swapaxes(x, 0, 1)

    fill(
        2 + 8 * half,
        turn(flow[0, :, :, own_half]), turn(flow[1, :, :, own_half]), turn(temp[:, :, own_half]),
        bot[:, own_half], sun[:, own_half],
    )
    for one in to_partner:
        one.wait_recv()
    fill(10 - 8 * half, turn(pf[0]), turn(pf[1]), turn(pt[...]), pb[...], ps[...])

    def pack(j):
        i = j + 2
        acc = zero
        for n in range(NT):
            x = c0[i, n]
            acc = jnp.where((lane // 2) == (8 * n + 2) // 2, roll(x, 8 * n + 2), acc)
            acc = jnp.where((lane // 2) == (8 * n + 4) // 2, roll(x, 8 * n + 6), acc)
        xo[j] = acc
        acc = zero
        for f in range(4):
            x = fm0[i, f]
            acc = jnp.where((lane // 2) == (8 * f + 2) // 2, roll(x, 8 * f + 2), acc)
            acc = jnp.where((lane // 2) == (8 * f + 4) // 2, roll(x, 8 * f + 6), acc)
        xf[j] = acc

    loop(0, 16, 2, pack)

    for tile_of, first in ((te, 4), (tw, 2)):
        fields = zero
        for q in range(4):
            tracers = zero
            for r in range(4):
                here = group // 2 == r
                tracers = jnp.where(here, roll(xo[4 * q + r], 2 * r - first), tracers)
                fields = jnp.where(
                    here & (lane // 32 == q), roll(xf[4 * q + r], 32 * q + 2 * r - first), fields
                )
            tile_of[q] = tracers
        tile_of[4] = fields
    start(has_e, to_east)

    @pl.when(wrap_w)
    def _():
        pl.semaphore_wait(ready.at[2], 1)

    start(has_w, to_west)
    start(soon_n, rows_n)
    start(soon_s, rows_s)

    @pl.when(has_w)
    def _():
        to_east.wait_recv()

    @pl.when(has_e)
    def _():
        to_west.wait_recv()

    def spread_field(x, f):
        y = jnp.where(lane < 8, roll(x, -8 * f), 0.0)
        for by in (8, 16, 32, 64):
            y = y + roll(y, by)
        return y

    def sides(own, w, e, by_w, by_e):
        return jnp.where(group < 2, roll(w, by_w), jnp.where(group >= 6, roll(e, by_e), own))

    def fields_of(j):
        by = 32 * (j // 4) + 2 * (j % 4)
        return sides(xf[j], xw[4], xe[4], -by, 6 - by)

    for j in range(16):
        q, by = j // 4, 2 * (j % 4)
        p0[j + 2] = sides(xo[j], xw[q], xe[q], -by, 6 - by)
        fields = fields_of(j)
        for f in range(4):
            fp0[j + 2, f] = spread_field(fields, f)
    for side, j in ((0, 0), (1, 15)):
        px_out[side, 0] = p0[j + 2]
        px_out[side, 1] = fields_of(j)
    start(soon_n, edge_n)
    start(soon_s, edge_s, far_s)

    @pl.when(late_n)
    def _():
        pl.semaphore_wait(ready.at[0], 1)
        for one in (near_n, rows_n, edge_n, far_n):
            one.start()

    def wet_of(aux):
        return (level_f < jnp.broadcast_to(aux[0:1, :], (NZ, 128))).astype(jnp.float32)

    def light_of(aux):
        return jnp.broadcast_to(aux[1:2, :], (NZ, 128))

    def shear_pressure(u, v, h):
        du = u - roll(u, 7, 0)
        dv = v - roll(v, 7, 0)
        q = jnp.where(level < NZ - 1, du * du + dv * dv, 0.0)
        kappa = kappa_base + kappa_shear * q / (1.0 + q)
        total = h
        for by in (1, 2, 4):
            total = total + jnp.where(level >= by, roll(total, by, 0), 0.0)
        return kappa, -expansion * total

    def prepare_row(i, f, k):
        kappa, pressure = shear_pressure(f[i, 0], f[i, 1], f[i, 2])
        k[i, 0] = kappa
        k[i, 1] = pressure

    def prepare(fm, fp, km, kp, first, last):
        def one(i):
            prepare_row(i, fm, km)
            prepare_row(i, fp, kp)

        loop(first, last, 2, one)

    def east_of(m, p, n=0):
        return jnp.where(lane == 127, roll(p, 121 - 8 * n), roll(m, 127))

    def west_of(m, p, n=0):
        return jnp.where(lane == 0, roll(p, 127 - 8 * n), roll(m, 1))

    def apply(a, x, xe_, xw_, xn, xs):
        return ((a[0] * x + a[3] * xn) + (a[4] * xs + a[5] * roll(x, 1, 0))) + (
            a[6] * roll(x, 7, 0) + (a[1] * xe_ + a[2] * xw_)
        )

    def flow_row(i, f, k, aux, e_of, w_of, coriolis):
        u, v, h = f[i, 0], f[i, 1], f[i, 2]
        kappa, pressure = k[i, 0], k[i, 1]
        un, us = f[i + 1, 0], f[i - 1, 0]
        vn, vs = f[i + 1, 1], f[i - 1, 1]
        wet = wet_of(aux[i, 3])
        wet_e = w_e = e_of(3)
        wet_w = w_of(3)
        oe = wet * wet_e
        ow = wet * wet_w
        on = wet * wet_of(aux[i + 1, 3])
        os = wet * wet_of(aux[i - 1, 3])
        ue, uw, ve, vw = e_of(0), w_of(0), e_of(1), w_of(1)
        fe = 0.5 * (u + ue) * oe
        fw = 0.5 * (u + uw) * ow
        fn = 0.5 * (v + vn) * on
        fs = 0.5 * (v + vs) * os
        ce = 0.5 * (kappa + e_of(4)) * oe
        cw = 0.5 * (kappa + w_of(4)) * ow
        cn = 0.5 * (kappa + k[i + 1, 0]) * on
        cs = 0.5 * (kappa + k[i - 1, 0]) * os
        lap_u = oe * (ue - u) + ow * (uw - u) + on * (un - u) + os * (us - u)
        lap_v = oe * (ve - v) + ow * (vw - v) + on * (vn - v) + os * (vs - v)
        new_u = wet * (
            u + time_step * (coriolis * v - 0.5 * (e_of(5) - w_of(5)) + viscosity * lap_u)
        )
        new_v = wet * (
            v
            + time_step
            * (-coriolis * u - 0.5 * (k[i + 1, 1] - k[i - 1, 1]) + viscosity * lap_v)
        )
        div = fe - fw + fn - fs
        total = div
        for by in (1, 2, 4):
            total = total + jnp.where(level < NZ - by, roll(total, NZ - by, 0), 0.0)
        w_top = jnp.where(level >= 1, -total, 0.0)
        w_bot = jnp.where(level < NZ - 1, -roll(total, NZ - 1, 0), 0.0)
        a = (
            wet
            * (
                1.0
                - time_step * (ce + cw + cn + cs)
                - 0.5 * time_step * (div + w_top - w_bot)
            ),
            time_step * (ce - 0.5 * fe),
            time_step * (cw + 0.5 * fw),
            time_step * (cn - 0.5 * fn),
            time_step * (cs + 0.5 * fs),
            (-0.5 * time_step) * w_top * wet,
            (0.5 * time_step) * w_bot * wet,
        )
        moved = apply(a, h, e_of(2), w_of(2), f[i + 1, 2], f[i - 1, 2])
        return a, new_u, new_v, moved

    first_lat = 8 * n_row

    def coriolis_of(i):
        latitude = (16 * chip + i - 2).astype(jnp.float32)
        return coriolis_base * (2.0 * (latitude + 0.5) / first_lat - 1.0)

    def main_shift(i, fm, fp, km, kp, of):
        def one(f):
            if f == 3:
                return of(wet_of(fm0[i, 3]), wet_of(fp0[i, 3]))
            if f >= 4:
                return of(km[i, f - 4], kp[i, f - 4])
            return of(fm[i, f], fp[i, f])

        return one

    def packed_shift(i, by):
        def one(f):
            if f == 3:
                return roll(wet_of(fp0[i, 3]), by)
            if f >= 4:
                return roll(kpp[i, f - 4], by)
            return roll(fp0[i, f], by)

        return one

    def keep(i, result, a_new, f_new):
        a, u, v, h = result
        for s in range(7):
            a_new[i, s] = a[s]
        f_new[i, 0] = u
        f_new[i, 1] = v
        f_new[i, 2] = h

    def flow_main(i, fm, fp, km, kp, f_new):
        keep(
            i,
            flow_row(
                i, fm, km, fm0, main_shift(i, fm, fp, km, kp, east_of),
                main_shift(i, fm, fp, km, kp, west_of), coriolis_of(i),
            ),
            am, f_new,
        )

    def flow_packed(i):
        keep(
            i,
            flow_row(i, fp0, kpp, fp0, packed_shift(i, 127), packed_shift(i, 1), coriolis_of(i)),
            ap, fp1,
        )

    def profile_of(pigment):
        squared = pigment * pigment
        depth = water_absorb + pigment_absorb * squared / (1.0 + squared)
        above = zero
        for by in (1, 2, 3):
            above = above + jnp.where(level >= by, roll(depth, by, 0), 0.0)
        return jnp.where(
            level < KL, jnp.exp(-above) * (1.0 - jnp.exp(-depth)), 0.0
        )

    def moved_row(i, c, p, c_new, i_new, slot):
        a = [am[i, s] for s in range(7)]
        ghost = jnp.where(lane % 8 == 0, roll(p[i], -6), roll(p[i], -2))
        lanes = pl.ds(pl.multiple_of(slot * 128, 128), 128)
        for pair in range(NT // 2):
            bent = []
            for n in (2 * pair, 2 * pair + 1):
                x = c[i, n]
                g = roll(ghost, -8 * n)
                x_e = roll(jnp.where(lane == 0, g, x), 127)
                x_w = roll(jnp.where(lane == 127, g, x), 1)
                m = apply(a, x, x_e, x_w, c[i + 1, n], c[i - 1, n])
                c_new[i_new, n] = m
                bent.append(m * lax.rsqrt(1.0 + m * m))
            both = jnp.concatenate(bent, axis=0)
            high = both.astype(jnp.bfloat16)
            low = (both - high.astype(jnp.float32)).astype(jnp.bfloat16)
            sbuf[16 * pair : 16 * pair + 16, lanes] = high
            sbuf[128 + 16 * pair : 144 + 16 * pair, lanes] = low

    def react_rows(rows, slot, c_new, shift, f_new):
        part = sbuf[:, 128 * slot : 128 * slot + 256]
        coupling = jnp.dot(whi[...], part, preferred_element_type=jnp.float32) + jnp.dot(
            wlo[...], part, preferred_element_type=jnp.float32
        )
        for r, i in enumerate(rows):
            wet = wet_of(fm0[i, 3])
            scale = react_step * wet
            for n in range(NT):
                value = c_new[i - shift, n] + scale * coupling[
                    8 * n : 8 * n + 8, 128 * r : 128 * r + 128
                ]
                c_new[i - shift, n] = value
                if n == 0:
                    f_new[i, 2] = f_new[i, 2] + heat_gain * light_of(
                        fm0[i, 3]
                    ) * wet * profile_of(value)

    def step1_flow(i):
        flow_main(i, fm0, fp0, kpm, kpp, fm1)
        flow_packed(i)

    def packed_moved(i):
        x = p0[i]
        a = [ap[i, s] for s in range(7)]
        m = apply(a, x, roll(x, 127), roll(x, 1), p0[i + 1], p0[i - 1])
        p1[i] = m
        return m * lax.rsqrt(1.0 + m * m)

    def couple(x):
        return lax.dot_general(
            x, wmat[...], (((1,), (1,)), ((), ())), precision=lax.Precision.HIGHEST,
            preferred_element_type=jnp.float32,
        )

    def packed_react(i, coupling):
        wet = wet_of(fp0[i, 3])
        value = p1[i] + react_step * wet * coupling
        p1[i] = value
        fp1[i, 2] = fp1[i, 2] + heat_gain * light_of(fp0[i, 3]) * wet * profile_of(
            spread_field(value, 0)
        )

    prepare(fm0, fp0, kpm, kpp, 2, 18)
    loop(3, 17, 2, step1_flow)

    def packed_in(i):
        psat[pl.ds(pl.multiple_of(8 * (i - 3), 8), 8), :] = packed_moved(i)

    def packed_end(i):
        packed_react(i, psat[pl.ds(pl.multiple_of(8 * (i - 3), 8), 8), :])

    loop(3, 17, 7, packed_in)
    psat[...] = couple(psat[...])
    loop(3, 17, 7, packed_end)
    loop(3, 17, 2, lambda i: moved_row(i, c0, p0, c1, i, i - 3))
    for i in range(3, 17, 2):
        react_rows((i, i + 1), i - 3, c1, 0, fm1)

    @pl.when(late_s)
    def _():
        pl.semaphore_wait(ready.at[1], 1)
        for one in (near_s, rows_s, edge_s, far_s):
            one.start()

    prepare(fm1, fp1, kpm1, kpp1, 3, 17)
    loop(4, 16, 2, lambda i: flow_main(i, fm1, fp1, kpm1, kpp1, fm2))
    loop(4, 16, 2, lambda i: moved_row(i, c1, p1, c2, i - 2, i - 4))
    for i in range(4, 16, 2):
        react_rows((i, i + 1), i - 4, c2, 2, fm2)

    def finish(out, by, side):
        edge = out + by
        p0[out] = px_in[side, 0]
        for f in range(4):
            fp0[out, f] = spread_field(px_in[side, 1], f)
        prepare_row(out - by, fm0, kpm)
        prepare_row(out, fm0, kpm)
        prepare_row(out, fp0, kpp)
        flow_main(edge, fm0, fp0, kpm, kpp, fm1)
        flow_packed(edge)
        flow_main(out, fm0, fp0, kpm, kpp, fm1)
        packed_react(edge, couple(packed_moved(edge)))
        moved_row(edge, c0, p0, c1, edge, 0)
        moved_row(out, c0, p0, c1, out, 1)
        react_rows((edge, out), 0, c1, 0, fm1)
        prepare_row(edge, fm1, kpm1)
        prepare_row(edge, fp1, kpp1)
        prepare_row(out, fm1, kpm1)
        flow_main(edge + by, fm1, fp1, kpm1, kpp1, fm2)
        flow_main(edge, fm1, fp1, kpm1, kpp1, fm2)
        moved_row(edge + by, c1, p1, c2, edge + by - 2, 0)
        moved_row(edge, c1, p1, c2, edge - 2, 1)
        react_rows((edge + by, edge), 0, c2, 2, fm2)

    @pl.when(has_n)
    def _():
        for one in (near_s, far_s, rows_s, edge_s):
            one.wait_recv()

    finish(18, -1, 1)

    @pl.when(has_s)
    def _():
        for one in (near_n, far_n, rows_n, edge_n):
            one.wait_recv()

    finish(1, 1, 0)

    back = copy(fm2.at[pl.ds(10 - 8 * half, 8)], fr, 14, partner)
    back.start()
    for f in range(3):
        mine_out[:, f] = fm2[pl.ds(2 + 8 * half, 8), f]
    for one in to_partner:
        one.wait_send()
    for here, copies in (
        (has_e, (to_east,)), (has_w, (to_west,)),
        (has_n, (near_n, far_n, rows_n, edge_n)), (has_s, (near_s, far_s, rows_s, edge_s)),
    ):
        @pl.when(here)
        def _(copies=copies):
            for one in copies:
                one.wait_send()

    back.wait()
    theirs_out[...] = fr[...]


def lay_out(c2, mine, theirs, flow_out, temp_out, tr_out):
    half = lax.rem(lax.axis_index("row"), 2)

    def turn_out(n, carry):
        for t in range(2):
            tr_out[0, n, :, 8 * t : 8 * t + 8, :] = jnp.swapaxes(c2[8 * t : 8 * t + 8, n], 0, 1)
        return carry

    lax.fori_loop(0, c2.shape[1], turn_out, 0)

    @pl.when(pl.program_id(0) == 0)
    def _():
        for ref, at in ((mine, half), (theirs, 1 - half)):
            lanes = pl.ds(pl.multiple_of(at * 128, 128), 128)
            for f in range(2):
                flow_out[f, :, :, lanes] = jnp.swapaxes(ref[:, f], 0, 1)
            temp_out[:, :, lanes] = jnp.swapaxes(ref[:, 2], 0, 1)


def on_device(n_row, n_col, *args):
    f32 = jnp.float32
    vmem = pl.BlockSpec(memory_space=pltpu.VMEM)
    tile = (NZ, 128)
    c2, mine, theirs = pl.pallas_call(
        functools.partial(kernel, n_row, n_col),
        out_shape=(
            jax.ShapeDtypeStruct((16, NT) + tile, f32),
            jax.ShapeDtypeStruct((8, 3) + tile, f32),
            jax.ShapeDtypeStruct((8, 3) + tile, f32),
        ),
        in_specs=[pl.BlockSpec(memory_space=pl.ANY)] * 6,
        out_specs=(vmem, vmem, vmem),
        scratch_shapes=[
            pltpu.VMEM((20, NT) + tile, f32),
            pltpu.VMEM((20, NT) + tile, f32),
            pltpu.VMEM((20,) + tile, f32),
            pltpu.VMEM((20,) + tile, f32),
            pltpu.VMEM((112, 128), f32),
            pltpu.VMEM((20, 4) + tile, f32),
            pltpu.VMEM((20, 4) + tile, f32),
            pltpu.VMEM((20, 3) + tile, f32),
            pltpu.VMEM((20, 3) + tile, f32),
            pltpu.VMEM((20, 3) + tile, f32),
            pltpu.VMEM((20, 2) + tile, f32),
            pltpu.VMEM((20, 2) + tile, f32),
            pltpu.VMEM((20, 2) + tile, f32),
            pltpu.VMEM((20, 2) + tile, f32),
            pltpu.VMEM((20, 7) + tile, f32),
            pltpu.VMEM((20, 7) + tile, f32),
            pltpu.VMEM((128, 128), f32),
            pltpu.VMEM((128, 256), jnp.bfloat16),
            pltpu.VMEM((128, 256), jnp.bfloat16),
            pltpu.VMEM((256, 14 * 128), jnp.bfloat16),
            pltpu.VMEM((16,) + tile, f32),
            pltpu.VMEM((16,) + tile, f32),
            pltpu.VMEM((5,) + tile, f32),
            pltpu.VMEM((5,) + tile, f32),
            pltpu.VMEM((5,) + tile, f32),
            pltpu.VMEM((5,) + tile, f32),
            pltpu.VMEM((2, 2) + tile, f32),
            pltpu.VMEM((2, 2) + tile, f32),
            pltpu.VMEM((2, NZ, 8, 128), f32),
            pltpu.VMEM((NZ, 8, 128), f32),
            pltpu.VMEM((8, 128), jnp.int32),
            pltpu.VMEM((8, 128), f32),
            pltpu.VMEM((8, 3) + tile, f32),
            pltpu.VMEM((2, NZ, 8, 256), f32),
            pltpu.VMEM((NZ, 8, 256), f32),
            pltpu.VMEM((1, NT, NZ, 16, 128), f32),
            pltpu.VMEM((8, 256), jnp.int32),
            pltpu.VMEM((8, 256), f32),
            pltpu.VMEM((NT, NT), f32),
            pltpu.SemaphoreType.DMA((15,)),
            pltpu.SemaphoreType.DMA((15,)),
            pltpu.SemaphoreType.REGULAR((3,)),
            pltpu.SemaphoreType.DMA((6,)),
        ],
        compiler_params=pltpu.CompilerParams(collective_id=0, has_side_effects=True),
    )(*args)
    small = pl.BlockSpec((8, 3) + tile, lambda g: (0, 0, 0, 0))
    parts = 2
    return tuple(
        pl.pallas_call(
            lay_out,
            grid=(parts,),
            out_shape=(
                jax.ShapeDtypeStruct((2, NZ, 8, 256), f32),
                jax.ShapeDtypeStruct((NZ, 8, 256), f32),
                jax.ShapeDtypeStruct((1, NT, NZ, 16, 128), f32),
            ),
            in_specs=[pl.BlockSpec((16, NT // parts) + tile, lambda g: (0, g, 0, 0)), small, small],
            out_specs=(
                pl.BlockSpec((2, NZ, 8, 256), lambda g: (0, 0, 0, 0)),
                pl.BlockSpec((NZ, 8, 256), lambda g: (0, 0, 0)),
                pl.BlockSpec((1, NT // parts, NZ, 16, 128), lambda g: (0, g, 0, 0, 0)),
            ),
        )(c2, mine, theirs)
    )


def solution(mesh):
    in_specs = (
        P(None, None, "row", "col"),
        P(None, "row", "col"),
        P("row", None, None, None, "col"),
        P("row", "col"),
        P("row", "col"),
        P(),
    )
    out_specs = (
        P(None, None, "row", "col"),
        P(None, "row", "col"),
        P("row", None, None, None, "col"),
    )
    return jax.shard_map(
        functools.partial(on_device, mesh.shape["row"], mesh.shape["col"]),
        mesh=mesh, in_specs=in_specs, out_specs=out_specs, check_vma=False,
    )
```
